256 devices in a mesh: req: 64 (over z, y, core), head: 4 (over x).
Axes of the slice: x: 4, y: 4, z: 8, core: 2. Of those that a mesh axis runs over, the one named last changes fastest.
Arguments:
- residual: bfloat16 [1024, 2048], P('req'), may hold values from -5.2 to 5.2
- queries: bfloat16 [1024, 1024], P('req', 'head'), may hold values from -5.5 to 5.5
- new_kv: bfloat16 [1024, 2, 1024], P('req', None, 'head'), may hold values from -4.5 to 4.5
- kv_cache: bfloat16 [8192, 2, 32, 1024], P('req', None, None, 'head'), may hold values from -131 to 131
- lengths: int32 [1024], replicated, may hold values from 2 to 16384, as said below
- slot_request: int32 [8192], P('req'), may hold values from 0 to 1023, as said below
- slot_page: int32 [8192], P('req'), may hold values from 0 to 511, as said below
- slot_used: int32 [8192], P('req'), may hold values from 0 to 1
- out_weight: bfloat16 [1024, 2048], P('head'), may hold values from -0.1875 to 0.1875
- norm_gain: float32 [2048], replicated, may hold values from 0.25 to 1.75
- routes: int32 [1024, 8], P('req'), may hold values from 0 to 63, all different within a row; in each aligned block of 16 rows (0 to 15, 16 to 31, ...) at most 4 rows name the same one
- route_weights: float32 [1024, 8], P('req'), may hold values from 0.05 to 0.5
- w_gate: bfloat16 [64, 2048, 1024], P('req', None, 'head'), may hold values from -0.125 to 0.125
- w_up: bfloat16 [64, 2048, 1024], P('req', None, 'head'), may hold values from -0.125 to 0.125
- w_down: bfloat16 [64, 1024, 2048], P('req', 'head'), may hold values from -0.1875 to 0.1875
- next_gain: float32 [2048], replicated, may hold values from 0.25 to 1.75
- next_weight: bfloat16 [2048, 3, 1024], P(None, None, 'head'), may hold values from -0.125 to 0.125
Outputs:
- stream: bfloat16 [1024, 2048], P('req', 'head')
- next_qkv: bfloat16 [1024, 3, 1024], P('req', None, 'head')
The draws below stay inside these ranges and needn't reach their ends.
Inputs may be any that keep to these rules, and one draw needn't show every extreme that they name: Request r has cached positions 0 to lengths[r] - 1, held in pages 0 to ceil(lengths[r] / 32) - 1; some request is 16384 long. `slot_request`: each page of every request lies in exactly one slot with slot_used 1; unused slots hold request 0. `slot_page`: unused slots hold page 0. `routes`: within the rows of one index of req at most 4 rows name the same expert.
All inputs are finite; a program needn't handle non-finite values.
Results may differ from the reference program's by a relative error of at most 0.025.
Values may be sent and summed in bfloat16 or wider, within the bound.
No kernel may reach another device: no remote copies, remote signals or barrier semaphores. Data moves between devices by JAX's collectives and lax.ppermute only.
A program may use at most 64 MiB of HBM per device.

```python
import math
import jax
import jax.numpy as jnp
import numpy as np
from jax import lax

D = 2048
HD = 128
EFF = 1024
TOPK = 8
HEADS = 8
PAGE = 32
PAGES_DEV = 128
MAX_LEN = 16384
REQ_DEV = 16
REQUESTS = 1024
SLOTS = 8192
EXPERTS = 64
CAP = 4
SHORT_PAGES = 7


def page_layout(key):
    base_key = jax.random.fold_in(key, 11)
    key_big, key_pages, key_tail, key_perm = jax.random.split(base_key, 4)
    req_ids = jnp.arange(REQUESTS, dtype=jnp.int32)
    longest = jax.random.randint(key_big, (), 0, REQUESTS)
    page_counts = jnp.where(req_ids == longest, MAX_LEN // PAGE, jax.random.randint(key_pages, (REQUESTS,), 1, SHORT_PAGES + 1))
    tail_len = jax.random.randint(key_tail, (REQUESTS,), 2, PAGE + 1)
    lengths = jnp.where(req_ids == longest, MAX_LEN, (page_counts - 1) * PAGE + tail_len).astype(jnp.int32)
    page_ends = jnp.cumsum(page_counts)
    starts = page_ends - page_counts
    slot_ids = jnp.arange(SLOTS, dtype=jnp.int32)
    filled = slot_ids < page_ends[REQUESTS - 1]
    owner_req = jnp.minimum(jnp.sum((slot_ids[:, None] >= page_ends[None, :]).astype(jnp.int32), axis=1), REQUESTS - 1)
    page_no = jnp.where(filled, slot_ids - starts[owner_req], 0)
    owner_req = jnp.where(filled, owner_req, 0)
    shuffle = jax.random.permutation(key_perm, SLOTS)
    slot_request = jnp.zeros((SLOTS,), jnp.int32).at[shuffle].set(owner_req.astype(jnp.int32))
    slot_page = jnp.zeros((SLOTS,), jnp.int32).at[shuffle].set(page_no.astype(jnp.int32))
    slot_used = jnp.zeros((SLOTS,), jnp.int32).at[shuffle].set(filled.astype(jnp.int32))
    return (lengths, slot_request, slot_page, slot_used)


def query_parts(key):
    key_own, key_key, key_value = jax.random.split(jax.random.fold_in(key, 23), 3)
    full_shape = (REQUESTS, HEADS * HD)
    own_part = jnp.clip(jax.random.normal(key_own, full_shape), -4.5, 4.5)
    fresh_key = jnp.clip(jax.random.normal(key_key, full_shape), -4.5, 4.5)
    fresh_value = jnp.clip(jax.random.normal(key_value, full_shape), -4.5, 4.5)
    return (0.8 * own_part + 0.4 * fresh_key, fresh_key, fresh_value)


def draw_lengths(key, part):
    return page_layout(key)[0]


def draw_slot_request(key, part):
    return page_layout(key)[1]


def draw_slot_page(key, part):
    return page_layout(key)[2]


def draw_slot_used(key, part):
    return page_layout(key)[3]


def draw_queries(key, part):
    return query_parts(key)[0].astype(jnp.bfloat16)


def draw_new_kv(key, part):
    query_rows, fresh_key, fresh_value = query_parts(key)
    return jnp.stack([fresh_key, fresh_value], axis=1).astype(jnp.bfloat16)


def draw_kv_cache(key, part):
    base_draw = jnp.clip(jax.random.normal(jax.random.fold_in(key, 37), (SLOTS, 2, PAGE, HEADS * HD)), -4.5, 4.5)
    return base_draw.astype(jnp.bfloat16)


def draw_residual(key, part):
    key_noise, key_row, key_col = jax.random.split(jax.random.fold_in(key, 53), 3)
    noise_draw = jnp.clip(jax.random.normal(key_noise, (REQUESTS, D)), -4.5, 4.5)
    row_scale = jnp.exp(jax.random.uniform(key_row, (REQUESTS, 1), maxval=math.log(10.0)))
    col_scale = jnp.exp(jax.random.uniform(key_col, (1, D), maxval=math.log(10.0)))
    return (0.01 * noise_draw * row_scale * col_scale).astype(jnp.bfloat16)


def levels(rng, shape, shards, low, largest):
    def one(dim, parts):
        heights = jax.random.uniform(jax.random.fold_in(jax.random.fold_in(rng, 6), dim), (parts,), jnp.float32, low / len(shards), largest / len(shards))
        return jnp.repeat(jnp.exp(heights), shape[dim] // parts).reshape((-1,) + (1,) * (len(shape) - dim - 1))

    factor_of = one(*shards[0])
    for cut in shards[1:]:
        factor_of = factor_of * one(*cut)
    return factor_of


def shared_out(rng, own, number, rows, amount, top, limit, slope):
    sequence = jax.random.permutation(rng, amount)
    heavy_load, common = portions_of(amount, rows * top, limit, slope, True), portions_of(amount, rows * top, limit, slope, False)
    places = jnp.arange(amount)

    def named(tallies, turn):
        used = int((tallies > 0).sum())
        fixed = max(1, used // 4)
        moved = fixed + (places - fixed + turn * (used - fixed)) % max(1, amount - fixed)
        return jnp.zeros((amount,), jnp.int32).at[sequence[jnp.where(places < fixed, places, moved)]].set(jnp.asarray(tallies, jnp.int32))

    tallies = jnp.where(number % 4 == 0, named(heavy_load, number // 4), named(common, number - number // 4 - 1))
    mixed = jax.random.permutation(jax.random.fold_in(own, 3), amount)
    giver, sink = mixed[0:amount // 2 * 2:2], mixed[1:amount // 2 * 2:2]
    slack = jnp.minimum(tallies[giver] - 1, limit - tallies[sink]) // 2
    slack = jnp.where((giver == sequence[0]) | (sink == sequence[0]) | (tallies[sink] == 0), 0, jnp.maximum(slack, 0))
    moved = jax.random.randint(jax.random.fold_in(own, 4), (amount // 2,), 0, 1 << 20) % (slack + 1)
    tallies = tallies.at[giver].add(-moved).at[sink].add(moved)
    items = jnp.searchsorted(jnp.cumsum(tallies), jnp.arange(rows * top), side="right").astype(jnp.int32)
    grid = items.reshape(top, rows).T
    grid = grid[jax.random.permutation(jax.random.fold_in(own, 1), rows)]
    turn = jax.random.randint(jax.random.fold_in(own, 2), (rows, 1), 0, top)
    return jnp.take_along_axis(grid, (jnp.arange(top)[None, :] + turn) % top, axis=1)


def portions_of(count, total, bound, skew, full):
    weights = [(1 << 20) // math.isqrt(rank ** skew) + 1 for rank in range(1, count + 1)]
    largest = bound if full else min(bound, max(-(-total // count), total * weights[0] // sum(weights)))
    least = 1 if total - largest >= count - 1 else 0
    given, spare = [largest] + [least] * (count - 1), total - largest - least * (count - 1)
    while spare > 0:
        candidates = [i for i in range(1, count) if given[i] < largest] or [i for i in range(1, count) if given[i] < bound]
        whole, budget = sum([weights[i] for i in candidates]), spare
        for i in candidates:
            extra = min(bound - given[i], max(1, budget * weights[i] // whole), spare)
            given[i] = given[i] + extra
            spare = spare - extra
    return np.array(given)


def gaussian(own_key, dims, deviation, most, shards=(), kind=jnp.bfloat16):
    values = deviation * jax.random.normal(own_key, dims, jnp.float32)
    if shards:
        values = values * levels(own_key, dims, shards, -0.22, 0.18)
    return jnp.clip(values, -most, most).astype(kind)


def setup_inputs(seed: int = 0) -> dict:
    key_of = jax.random.split(jax.random.key(seed), 18)
    residual = draw_residual(jax.random.fold_in(key_of[17], 71), 0)
    queries = draw_queries(jax.random.fold_in(key_of[17], 71), 0)
    new_kv = draw_new_kv(jax.random.fold_in(key_of[17], 71), 0)
    kv_cache = draw_kv_cache(jax.random.fold_in(key_of[17], 71), 0)
    lengths = draw_lengths(jax.random.fold_in(key_of[17], 71), 0)
    slot_request = draw_slot_request(jax.random.fold_in(key_of[17], 71), 0)
    slot_page = draw_slot_page(jax.random.fold_in(key_of[17], 71), 0)
    slot_used = draw_slot_used(jax.random.fold_in(key_of[17], 71), 0)
    out_weight = gaussian(key_of[8], (HEADS * HD, D), (HEADS * HD) ** -0.5, 0.1875, ((0, 4),))
    norm_gain = jnp.clip(1.0 + 0.15 * jax.random.normal(key_of[9], (D,), jnp.float32), 0.25, 1.75)
    routes_keys = jax.random.split(jax.random.fold_in(key_of[10], 1), REQUESTS // REQ_DEV)
    routes_turns = jax.random.permutation(jax.random.fold_in(key_of[10], 3), REQUESTS // REQ_DEV)
    routes = jax.vmap(lambda own, number: shared_out(jax.random.fold_in(key_of[10], 2), own, number, REQ_DEV, EXPERTS, TOPK, CAP, 2))(routes_keys, routes_turns).reshape((REQUESTS, TOPK))
    route_weights = jnp.clip(jnp.exp(math.log(0.5) - 2.3025851 * jax.random.uniform(key_of[11], (REQUESTS, TOPK), jnp.float32) ** levels(key_of[11], (REQUESTS, TOPK), ((0, 64),), -0.2, 0.2)), 0.05, 0.5)
    w_gate = gaussian(key_of[12], (EXPERTS, D, EFF), D ** -0.5, 0.125, ((0, 64), (2, 4)))
    w_up = gaussian(key_of[13], (EXPERTS, D, EFF), D ** -0.5, 0.125, ((0, 64), (2, 4)))
    w_down = gaussian(key_of[14], (EXPERTS, EFF, D), EFF ** -0.5, 0.1875, ((0, 64), (1, 4)))
    next_gain = jnp.clip(1.0 + 0.15 * jax.random.normal(key_of[15], (D,), jnp.float32), 0.25, 1.75)
    next_weight = gaussian(key_of[16], (D, 3, HEADS * HD), D ** -0.5, 0.125, ((2, 4),))
    return dict(residual=residual, queries=queries, new_kv=new_kv, kv_cache=kv_cache, lengths=lengths, slot_request=slot_request, slot_page=slot_page, slot_used=slot_used, out_weight=out_weight, norm_gain=norm_gain, routes=routes, route_weights=route_weights, w_gate=w_gate, w_up=w_up, w_down=w_down, next_gain=next_gain, next_weight=next_weight)


norm_eps = 1e-06
floor_value = -1e+30

def norm_rows(rows_in, gain):
    wide_rows = rows_in.astype(jnp.float32)
    mean_square = lax.optimization_barrier(jnp.mean(wide_rows * wide_rows, axis=1, keepdims=True))
    return (wide_rows * lax.rsqrt(mean_square + norm_eps) * gain).astype(jnp.bfloat16)

def reference(residual, queries, new_kv, kv_cache, lengths, slot_request, slot_page, slot_used, out_weight, norm_gain, routes, route_weights, w_gate, w_up, w_down, next_gain, next_weight):
    score_scale = 1.0 / HD ** 0.5
    slot_total = kv_cache.shape[0]
    blocks = slot_total // PAGES_DEV
    query_rows = queries.astype(jnp.float32).reshape(REQUESTS, HEADS, HD)
    position = slot_page[:, None] * PAGE + jnp.arange(PAGE, dtype=jnp.int32)[None, :]
    valid = (slot_used[:, None] == 1) & (position < lengths[slot_request][:, None])

    def block_scores(block_index):
        block_start = block_index * PAGES_DEV
        key_rows = lax.dynamic_slice_in_dim(kv_cache, block_start, PAGES_DEV, 0)[:, 0].astype(jnp.float32)
        key_rows = key_rows.reshape(PAGES_DEV, PAGE, HEADS, HD)
        owners = lax.dynamic_slice_in_dim(slot_request, block_start, PAGES_DEV, 0)
        return jnp.einsum('sphd,shd->sph', key_rows, query_rows[owners]) * score_scale
    scores = lax.map(block_scores, jnp.arange(blocks, dtype=jnp.int32)).reshape(slot_total, PAGE, HEADS)
    masked = jnp.where(valid[:, :, None], scores, floor_value)
    slot_peak = lax.optimization_barrier(jnp.max(masked, axis=1))
    member = slot_request[None, :] == jnp.arange(REQUESTS, dtype=jnp.int32)[:, None]
    cache_peak = lax.optimization_barrier(jnp.max(jnp.where(member[:, :, None], slot_peak[None], floor_value), axis=1))
    fresh_key = new_kv[:, 0].astype(jnp.float32).reshape(REQUESTS, HEADS, HD)
    fresh_value = new_kv[:, 1].astype(jnp.float32).reshape(REQUESTS, HEADS, HD)
    own_score = lax.optimization_barrier(jnp.sum(query_rows * fresh_key, axis=2)) * score_scale
    peak_score = jnp.maximum(cache_peak, own_score)
    weights = jnp.where(valid[:, :, None], jnp.exp(masked - peak_score[slot_request][:, None, :]), 0.0).astype(jnp.bfloat16)

    def block_values(block_index):
        block_start = block_index * PAGES_DEV
        value_rows = lax.dynamic_slice_in_dim(kv_cache, block_start, PAGES_DEV, 0)[:, 1].astype(jnp.float32)
        value_rows = value_rows.reshape(PAGES_DEV, PAGE, HEADS, HD)
        block_weights = lax.dynamic_slice_in_dim(weights, block_start, PAGES_DEV, 0).astype(jnp.float32)
        return jnp.einsum('sph,sphd->shd', block_weights, value_rows)
    slot_numer = lax.map(block_values, jnp.arange(blocks, dtype=jnp.int32)).reshape(slot_total, HEADS, HD)
    numerator = jax.ops.segment_sum(slot_numer, slot_request, num_segments=REQUESTS)
    denominator = jax.ops.segment_sum(lax.optimization_barrier(jnp.sum(weights.astype(jnp.float32), axis=1)), slot_request, num_segments=REQUESTS)
    new_lift = jnp.exp(own_score - peak_score)
    attended = (numerator + new_lift[:, :, None] * fresh_value) / (denominator + new_lift)[:, :, None]
    attended = attended.reshape(REQUESTS, HEADS * HD).astype(jnp.bfloat16)
    attn_out = jnp.dot(attended, out_weight, preferred_element_type=jnp.float32)
    hidden_state = (residual.astype(jnp.float32) + attn_out).astype(jnp.bfloat16)
    normed = norm_rows(hidden_state, norm_gain)

    def expert_step(moe_total, expert_index):
        gate_out = jnp.dot(normed, w_gate[expert_index], preferred_element_type=jnp.float32)
        upward = jnp.dot(normed, w_up[expert_index], preferred_element_type=jnp.float32)
        inner_act = (jax.nn.silu(gate_out) * upward).astype(jnp.bfloat16)
        output = jnp.dot(inner_act, w_down[expert_index], preferred_element_type=jnp.float32).astype(jnp.bfloat16)
        route_share = lax.optimization_barrier(jnp.sum(jnp.where(routes == expert_index, route_weights, 0.0), axis=1))
        return (moe_total + route_share[:, None] * output.astype(jnp.float32), None)
    moe_sum, _ = lax.scan(expert_step, jnp.zeros((REQUESTS, D), jnp.float32), jnp.arange(EXPERTS, dtype=jnp.int32))
    stream = (hidden_state.astype(jnp.float32) + moe_sum).astype(jnp.bfloat16)
    final_normed = norm_rows(stream, next_gain)
    next_qkv = jnp.einsum('td,dcf->tcf', final_normed.astype(jnp.float32), next_weight.astype(jnp.float32)).astype(jnp.bfloat16)
    return (stream, next_qkv)
```

```python
import functools
import math

import jax
import jax.numpy as jnp
from jax import lax
from jax.experimental import pallas as pl
from jax.experimental.pallas import tpu as pltpu
from jax.sharding import Mesh, PartitionSpec as P

HD = 128
EPS = 1e-06
FLOOR = -(2.0**99)
SCALE = 1.0 / math.sqrt(HD)
F32 = jnp.float32
BF16 = jnp.bfloat16
REQ = ("z", "y", "c")
VLIM = pltpu.CompilerParams(vmem_limit_bytes=40 * 1024 * 1024)


def iota(shape, dim):
    return lax.broadcasted_iota(jnp.int32, shape, dim)


def core_id():
    return lax.axis_index("c")


def head_id():
    return lax.axis_index("head")


def dot(a, b):
    return jnp.dot(a, b, preferred_element_type=F32)


def hi_lo(x):
    hi = x.astype(BF16)
    return hi, (x - hi.astype(F32)).astype(BF16)


def attn_kernel(sr_ref, sp_ref, su_ref, len_ref, qa_ref, qb_ref, kv_ref, out_ref, kv_buf, n_scr, m_scr, l_scr, sems):
    slots = kv_ref.shape[0]
    page = kv_ref.shape[2]
    total = len_ref.shape[1]
    half = total // 2
    chunks = sems.shape[0]
    per = slots // chunks
    copies = [
        pltpu.make_async_copy(kv_ref.at[pl.ds(i * per, per)], kv_buf.at[pl.ds(i * per, per)], sems.at[i])
        for i in range(chunks)
    ]
    for copy in copies:
        copy.start()
    core = core_id()
    req = sr_ref[...]
    place = jnp.where((req // 16) % 2 == core, 0, half) + (req // 32) * 16 + req % 16
    eye = iota((slots, slots), 0) == iota((slots, slots), 1)

    def to_col(row):
        return jnp.sum(jnp.where(eye, row.astype(F32), 0.0), axis=1, keepdims=True)

    def to_row(wide):
        return jnp.sum(jnp.where(eye, wide, 0.0), axis=0, keepdims=True)

    req_row = req.astype(F32)
    req_col = to_col(req)
    place_row = place.astype(F32)
    place_col = to_col(place)
    lane_total = iota((slots, total), 1).astype(F32)
    len_col = jnp.sum(jnp.where(req_col == lane_total, len_ref[...].astype(F32), 0.0), axis=1, keepdims=True)
    count = jnp.clip(len_col - to_col(sp_ref[...]) * page, 0.0, float(page))
    count = jnp.where(to_col(su_ref[...]) == 1.0, count, 0.0)
    pick = jnp.where(place_col == lane_total, 1.0, 0.0).astype(BF16)
    chosen = dot(pick[:, :half], qa_ref[...]) + dot(pick[:, half:], qb_ref[...])

    low_lanes = iota((8, 2 * HD), 1) < HD
    rel = iota((16, 8 * page), 1) - (iota((16, 8 * page), 0) % 8) * page
    rel = rel.astype(F32)
    for b in range(slots // 8):
        if (b * 8) % per == 0:
            copies[b * 8 // per].wait()
        q8 = chosen[b * 8 : b * 8 + 8]
        q16 = jnp.concatenate([jnp.where(low_lanes, q8, 0.0), jnp.where(low_lanes, 0.0, q8)], axis=0).astype(BF16)
        keys = kv_buf[b * 8 : b * 8 + 8, 0].reshape(8 * page, 2 * HD)
        vals = kv_buf[b * 8 : b * 8 + 8, 1].reshape(8 * page, 2 * HD)
        s = lax.dot_general(q16, keys, (((1,), (1,)), ((), ())), preferred_element_type=F32) * SCALE
        c8 = count[b * 8 : b * 8 + 8]
        ok = (rel >= 0.0) & (rel < jnp.concatenate([c8, c8], axis=0))
        s = jnp.where(ok, s, FLOOR)
        m = jnp.max(s, axis=1, keepdims=True)
        w = jnp.where(ok, jnp.exp(s - m), 0.0).astype(BF16)
        l = jnp.sum(w.astype(F32), axis=1, keepdims=True)
        n = dot(w, vals)
        for h in range(2):
            n_scr[h, b * 8 : b * 8 + 8, :] = n[8 * h : 8 * h + 8, HD * h : HD * h + HD]
            m_scr[h, b * 8 : b * 8 + 8, :] = jnp.broadcast_to(m[8 * h : 8 * h + 8], (8, slots))
            l_scr[h, b * 8 : b * 8 + 8, :] = jnp.broadcast_to(l[8 * h : 8 * h + 8], (8, slots))

    same = req_col == req_row
    slot_row = iota((slots, slots), 1).astype(F32)
    first = jnp.min(jnp.where(same, slot_row, 9999.0), axis=1, keepdims=True)
    leader = first == iota((slots, 1), 0).astype(F32)
    spread = jnp.where(iota((total, slots), 0).astype(F32) == place_row, 1.0, 0.0).astype(BF16)
    stat = []
    for h in range(2):
        m_wide = m_scr[h]
        m_ref = jnp.max(jnp.where(same, to_row(m_wide), FLOOR), axis=1, keepdims=True)
        m_ref = m_ref.astype(BF16).astype(F32)
        lift = jnp.exp(m_wide - m_ref)
        n_hi, n_lo = hi_lo(n_scr[h] * lift)
        l_sum = jnp.sum(jnp.where(same, to_row(l_scr[h] * lift), 0.0), axis=1, keepdims=True)
        out = (dot(spread, n_hi) + dot(spread, n_lo)).astype(BF16)
        out_ref[:, :, 16 * h : 16 * h + 16, :] = out.reshape(2, half // 16, 16, HD)
        l_hi = l_sum.astype(BF16).astype(F32)
        stat.append((m_ref, l_hi, l_sum - l_hi))
    lane = iota((slots, HD), 1)
    group = lane // 16
    board = jnp.zeros((slots, HD), F32)
    for h in range(2):
        for i in range(3):
            board = jnp.where(group == 2 * i + h, stat[h][i], board)
    mine = (lane % 16).astype(F32) == to_col(req % 16)
    board = jnp.where(mine & leader, board, 0.0).astype(BF16)
    spread16 = jnp.where(iota((total, slots), 0) // 16 == place // 16, 1.0, 0.0).astype(BF16)
    out_ref[:, :, 32:48, :] = dot(spread16, board).astype(BF16).reshape(2, half // 16, 16, HD)


def attend_pages(slot_request, slot_page, slot_used, lengths, qa, qb, kv_cache):
    slots = kv_cache.shape[0]
    total = lengths.shape[0]
    vm = pl.BlockSpec(memory_space=pltpu.VMEM)
    return pl.pallas_call(
        attn_kernel,
        name="attend_pages",
        out_shape=jax.ShapeDtypeStruct((2, total // 32, 48, HD), BF16),
        in_specs=[vm] * 6 + [pl.BlockSpec(memory_space=pl.ANY)],
        out_specs=vm,
        scratch_shapes=[
            pltpu.VMEM(kv_cache.shape, BF16),
            pltpu.VMEM((2, slots, HD), F32),
            pltpu.VMEM((2, slots, slots), F32),
            pltpu.VMEM((2, slots, slots), F32),
            pltpu.SemaphoreType.DMA((8,)),
        ],
        compiler_params=VLIM,
    )(
        slot_request.reshape(1, slots),
        slot_page.reshape(1, slots),
        slot_used.reshape(1, slots),
        lengths.reshape(1, total),
        qa.reshape(total // 2, 2 * HD),
        qb.reshape(total // 2, 2 * HD),
        kv_cache,
    )


def read_stats(board, h):
    lane, row = iota(board.shape, 2), iota(board.shape, 1) + 16 * h
    m = jnp.sum(jnp.where(lane == row, board, 0.0), axis=2, keepdims=True)
    l = jnp.sum(jnp.where((lane == row + 32) | (lane == row + 64), board, 0.0), axis=2, keepdims=True)
    return jnp.where(l > 0.0, m, FLOOR), l


def owner_kernel(part_ref, q_ref, nkv_ref, w_ref, *outs):
    board = part_ref[:, 32:48, :].astype(F32)
    q = q_ref[...].astype(F32)
    nkv = nkv_ref[...].astype(F32)
    att = []
    for h in range(2):
        m, l = read_stats(board, h)
        own = jnp.sum(q[:, HD * h : HD * h + HD] * nkv[:, HD * h : HD * h + HD], axis=1, keepdims=True) * SCALE
        top = jnp.maximum(jnp.max(m, axis=0), own)
        lift = jnp.exp(m - top[None])
        n = jnp.sum(part_ref[:, 16 * h : 16 * h + 16, :].astype(F32) * lift, axis=0)
        den = jnp.sum(l * lift, axis=0)
        new = jnp.exp(own - top)
        v = nkv[:, 2 * HD + HD * h : 2 * HD + HD * h + HD]
        att.append((n + new * v) / (den + new))
    attended = jnp.concatenate(att, axis=1).astype(BF16)
    head = head_id()
    width = outs[0].shape[1]
    for k in range(4):
        first = pl.multiple_of(((head + k) % 4) * width, width)
        outs[k][...] = dot(attended, w_ref[:, pl.ds(first, width)]).astype(BF16)


def owner_part(parts, queries, nkv, out_weight):
    rows = queries.shape[0]
    width = out_weight.shape[1] // 4
    vm = pl.BlockSpec(memory_space=pltpu.VMEM)
    return pl.pallas_call(
        owner_kernel,
        name="owner_part",
        out_shape=[jax.ShapeDtypeStruct((rows, width), BF16)] * 4,
        in_specs=[vm] * 4,
        out_specs=[vm] * 4,
        compiler_params=VLIM,
    )(parts, queries, nkv, out_weight)


def rank_of(hit):
    rows = hit.shape[0]
    before = jnp.where(iota((rows, rows), 0) > iota((rows, rows), 1), 1.0, 0.0).astype(BF16)
    return dot(before, hit.astype(BF16))


def dispatch_kernel(p0, p1, p2, p3, res_ref, routes_ref, hid_ref, disp_ref):
    width = hid_ref.shape[1]
    first = pl.multiple_of(head_id() * width, width)
    acc = p0[...].astype(F32) + p1[...].astype(F32) + p2[...].astype(F32) + p3[...].astype(F32)
    hid = (res_ref[:, pl.ds(first, width)].astype(F32) + acc).astype(BF16)
    hid_ref[...] = hid
    rows, picks = routes_ref.shape
    routes = routes_ref[...]
    cells = disp_ref.shape[0] * 8
    lane = iota((rows, cells), 1)
    hit = jnp.zeros((rows, cells), F32)
    for k in range(picks):
        hit = hit + jnp.where(routes[:, k : k + 1] == lane // 8, 1.0, 0.0)
    hit = jnp.where(rank_of(hit) == (lane % 4).astype(F32), hit, 0.0)
    left = lane % 8 < 4
    pick = jnp.concatenate([jnp.where(left, hit, 0.0), jnp.where(left, 0.0, hit)], axis=0).astype(BF16)
    both = jnp.concatenate([hid[:, : width // 2], hid[:, width // 2 :]], axis=0)
    out = lax.dot_general(pick, both, (((0,), (0,)), ((), ())), preferred_element_type=F32)
    disp_ref[...] = out.astype(BF16).reshape(disp_ref.shape)


def dispatch(parts, residual, routes, experts):
    rows, width = parts[0].shape
    vm = pl.BlockSpec(memory_space=pltpu.VMEM)
    return pl.pallas_call(
        dispatch_kernel,
        name="dispatch",
        out_shape=[
            jax.ShapeDtypeStruct((rows, width), BF16),
            jax.ShapeDtypeStruct((experts, 8, width // 2), BF16),
        ],
        in_specs=[vm] * 6,
        out_specs=[vm] * 2,
        compiler_params=VLIM,
    )(*parts, residual, routes)


def unfold(x):
    n, _, w = x.shape
    x = x.reshape(n // 2, 2, 8, w)
    a, b = x[:, 0], x[:, 1]
    top = iota(a.shape, 1) < 4
    left = jnp.where(top, a, pltpu.roll(b, 4, 1))
    right = jnp.where(top, pltpu.roll(a, 4, 1), b)
    return left.reshape(n * 4, w), right.reshape(n * 4, w)


def fold(left, right):
    rows, w = left.shape
    left, right = left.reshape(rows // 8, 8, w), right.reshape(rows // 8, 8, w)
    top = iota(left.shape, 1) < 4
    a = jnp.where(top, left, pltpu.roll(right, 4, 1))
    b = jnp.where(top, pltpu.roll(left, 4, 1), right)
    return a, b


def gate_kernel(x0, x1, x2, x3, gain_ref, wg_ref, wu_ref, inner_ref, xs):
    head = head_id()
    w = x0.shape[2]
    total = jnp.zeros((inner_ref.shape[0], 1), F32)
    for k, x in enumerate((x0, x1, x2, x3)):
        for f, part in enumerate(unfold(x[...].astype(F32))):
            xs[2 * k + f] = part
            total = total + jnp.sum(part * part, axis=1, keepdims=True)
    scale = lax.rsqrt(total / (8 * w) + EPS)
    gate = jnp.zeros(inner_ref.shape, F32)
    up = jnp.zeros(inner_ref.shape, F32)
    for k in range(4):
        for f in range(2):
            first = pl.multiple_of(((head + 4 - k) % 4) * 2 * w + f * w, w)
            normed = (xs[2 * k + f] * scale * gain_ref[:, pl.ds(first, w)]).astype(BF16)
            gate = gate + dot(normed, wg_ref[pl.ds(first, w), :])
            up = up + dot(normed, wu_ref[pl.ds(first, w), :])
    inner_ref[...] = (gate / (1.0 + jnp.exp(-gate)) * up).astype(BF16)


def gate_up(xs, gain, w_gate, w_up):
    n, _, w = xs[0].shape
    eff = w_gate.shape[1]
    vm = pl.BlockSpec(memory_space=pltpu.VMEM)
    return pl.pallas_call(
        gate_kernel,
        name="gate_up",
        out_shape=jax.ShapeDtypeStruct((n * 4, eff), BF16),
        in_specs=[vm] * 7,
        out_specs=vm,
        scratch_shapes=[pltpu.VMEM((8, n * 4, w), F32)],
        compiler_params=VLIM,
    )(*xs, gain.reshape(1, -1), w_gate, w_up)


def down_kernel(i0, i1, i2, i3, w_ref, out_ref, w_buf, sem):
    head = head_id()
    eff = i0.shape[1]
    width = w_buf.shape[1]
    cols = pl.ds(pl.multiple_of(head * width, width), width)
    copy = pltpu.make_async_copy(w_ref.at[:, cols], w_buf, sem)
    copy.start()
    copy.wait()
    acc = jnp.zeros((i0.shape[0], width), F32)
    for k, x in enumerate((i0, i1, i2, i3)):
        first = pl.multiple_of(((head + 4 - k) % 4) * eff, eff)
        acc = acc + dot(x[...], w_buf[pl.ds(first, eff), :])
    a, b = fold(acc[:, : width // 2], acc[:, width // 2 :])
    out_ref[:, 0] = a.astype(BF16)
    out_ref[:, 1] = b.astype(BF16)


def down(inners, w_down):
    rows, eff = inners[0].shape
    width = w_down.shape[1] // 4
    vm = pl.BlockSpec(memory_space=pltpu.VMEM)
    out = pl.pallas_call(
        down_kernel,
        name="down",
        out_shape=jax.ShapeDtypeStruct((rows // 8, 2, 8, width // 2), BF16),
        in_specs=[vm] * 4 + [pl.BlockSpec(memory_space=pl.ANY)],
        out_specs=vm,
        scratch_shapes=[pltpu.VMEM((w_down.shape[0], width), BF16), pltpu.SemaphoreType.DMA],
        compiler_params=VLIM,
    )(*inners, w_down)
    return out.reshape(rows // 4, 8, width // 2)


def blend_kernel(y_ref, hid_ref, routes_ref, rw_ref, out_ref):
    rows, picks = routes_ref.shape
    routes, share = routes_ref[...], rw_ref[...]
    cells = y_ref.shape[0] * 4
    lane = iota((rows, cells), 1)
    hit = jnp.zeros((rows, cells), F32)
    mix = jnp.zeros((rows, cells), F32)
    for k in range(picks):
        on = routes[:, k : k + 1] == lane // 4
        hit = hit + jnp.where(on, 1.0, 0.0)
        mix = mix + jnp.where(on, share[:, k : k + 1], 0.0)
    mix = jnp.where(rank_of(hit) == (lane % 4).astype(F32), mix, 0.0)
    m_hi, m_lo = hi_lo(mix)
    w = y_ref.shape[2]
    for f, part in enumerate(unfold(y_ref[...].astype(F32))):
        part = part.astype(BF16)
        hid = hid_ref[:, f * w : f * w + w].astype(F32)
        out_ref[:, f * w : f * w + w] = (hid + (dot(m_hi, part) + dot(m_lo, part))).astype(BF16)


def blend(returned, hidden, routes, route_weights):
    vm = pl.BlockSpec(memory_space=pltpu.VMEM)
    return pl.pallas_call(
        blend_kernel,
        name="blend",
        out_shape=jax.ShapeDtypeStruct(hidden.shape, BF16),
        in_specs=[vm] * 4,
        out_specs=vm,
        compiler_params=VLIM,
    )(returned, hidden, routes, route_weights)


def norm_kernel(s0, s1, s2, s3, gain_ref, out_ref):
    head = head_id()
    w = s0.shape[1]
    parts = [s[...].astype(F32) for s in (s0, s1, s2, s3)]
    total = sum(jnp.sum(p * p, axis=1, keepdims=True) for p in parts)
    scale = lax.rsqrt(total / (4 * w) + EPS)
    for k, p in enumerate(parts):
        cols = pl.ds(pl.multiple_of(((head + 4 - k) % 4) * w, w), w)
        out_ref[:, cols] = (p * scale * gain_ref[:, cols]).astype(BF16)


def norm_parts(parts, gain):
    rows, w = parts[0].shape
    vm = pl.BlockSpec(memory_space=pltpu.VMEM)
    return pl.pallas_call(
        norm_kernel,
        name="norm_parts",
        out_shape=jax.ShapeDtypeStruct((rows, 4 * w), BF16),
        in_specs=[vm] * 5,
        out_specs=vm,
        compiler_params=VLIM,
    )(*parts, gain.reshape(1, -1))


def from_heads(x):
    n = lax.axis_size("head")
    return [x] + [lax.ppermute(x, "head", [(i, (i + k) % n) for i in range(n)]) for k in range(1, n)]


def to_heads(xs):
    n = lax.axis_size("head")
    return [xs[0]] + [lax.ppermute(xs[k], "head", [(i, (i + k) % n) for i in range(n)]) for k in range(1, n)]


def swap_core(x):
    return lax.ppermute(x, "c", [(0, 1), (1, 0)])


def local(
    residual, queries, new_kv, kv_cache, lengths, slot_request, slot_page, slot_used, out_weight,
    norm_gain, routes, route_weights, w_gate, w_up, w_down, next_gain, next_weight,
):
    rows = queries.shape[0]
    experts = lax.axis_size(REQ)
    chips = experts // 2
    w_down_all = lax.all_gather(w_down.reshape(w_down.shape[1:]), "head", axis=0, tiled=True)
    nkv = new_kv.reshape(rows, -1)
    qa = lax.all_to_all(jnp.broadcast_to(queries[None], (chips,) + queries.shape), ("z", "y"), 0, 0, tiled=True)
    qb = swap_core(qa)
    parts = attend_pages(slot_request, slot_page, slot_used, lengths, qa, qb, kv_cache)
    core = lax.axis_index("c")
    both = jnp.where(core == 0, jnp.stack([parts[0], parts[1]], 1), jnp.stack([parts[1], parts[0]], 1))
    both = both.reshape((experts,) + parts.shape[2:])
    arrived = lax.all_to_all(both, REQ, 0, 0, tiled=True)
    shares = to_heads(owner_part(arrived, queries, nkv, out_weight))
    hidden, disp = dispatch(shares, residual, routes, experts)
    tokens = lax.all_to_all(disp, REQ, 0, 0, tiled=True)
    inner = gate_up(from_heads(tokens), norm_gain, w_gate[0], w_up[0])
    expert_out = down(from_heads(inner), w_down_all)
    returned = lax.all_to_all(expert_out, REQ, 0, 0, tiled=True)
    stream = blend(returned, hidden, routes, route_weights)
    normed = norm_parts(from_heads(stream), next_gain)
    next_qkv = jnp.einsum("td,dcf->tcf", normed, next_weight, preferred_element_type=F32).astype(BF16)
    return stream, next_qkv


def solution(mesh):
    split = Mesh(mesh.devices.reshape(8, 4, 2, 4), ("z", "y", "c", "head"))
    placed = (
        P(REQ, None),
        P(REQ, "head"),
        P(REQ, None, "head"),
        P(REQ, None, None, "head"),
        P(),
        P(REQ),
        P(REQ),
        P(REQ),
        P("head", None),
        P(),
        P(REQ, None),
        P(REQ, None),
        P(REQ, None, "head"),
        P(REQ, None, "head"),
        P(REQ, "head", None),
        P(),
        P(None, None, "head"),
    )
    return jax.shard_map(
        local,
        mesh=split,
        in_specs=placed,
        out_specs=(P(REQ, "head"), P(REQ, None, "head")),
        check_vma=False,
    )
```

```python
import functools
import math

import jax
import jax.numpy as jnp
from jax import lax
from jax.experimental import pallas as pl
from jax.experimental.pallas import tpu as pltpu
from jax.sharding import Mesh, PartitionSpec as P

HD = 128
EPS = 1e-06
FLOOR = -(2.0**99)
SCALE = 1.0 / math.sqrt(HD)
F32 = jnp.float32
BF16 = jnp.bfloat16
REQ = ("z", "y", "c")
VLIM = pltpu.CompilerParams(vmem_limit_bytes=24 * 1024 * 1024)
VM = pl.BlockSpec(memory_space=pltpu.VMEM)


class Pending:
    def __init__(self, buf, copy):
        self.buf, self.copy, self.done = buf, copy, False

    def get(self):
        if not self.done:
            self.copy.wait()
            self.done = True
        return self.buf


def run(body, name, outs, near, far, scratch=(), after=(), moves=()):
    nn, nf, na, nm = len(near), len(far), len(after), len(moves)
    parts = 4

    def kernel(*refs):
        ins, refs = refs[: nn + nf + na + nm], refs[nn + nf + na + nm :]
        outputs, moved, rest = refs[: len(outs)], refs[len(outs) : len(outs) + nm], refs[len(outs) + nm :]
        bufs, sems, move_sems, own = rest[:nf], rest[nf], rest[nf + 1], rest[nf + 2 :]
        copies = [pltpu.make_async_copy(ins[nn + i], bufs[i], sems.at[i]) for i in range(nf)]
        for copy in copies:
            copy.start()
        pending = [Pending(b, c) for b, c in zip(bufs, copies)]
        moving = []
        for i in range(nm):
            rows = moved[i].shape[0] // parts
            for j in range(parts):
                src, dst = ins[nn + nf + na + i].at[pl.ds(j * rows, rows)], moved[i].at[pl.ds(j * rows, rows)]
                moving.append(pltpu.make_async_copy(src, dst, move_sems.at[parts * i + j]))
        for copy in moving:
            copy.start()
        body(ins[:nn], pending, outputs, own)
        for p in pending:
            p.get()
        for copy in moving:
            copy.wait()

    def pin(xs):
        return [pltpu.with_memory_space_constraint(x, pltpu.HBM) for x in xs]

    hbm, any_space = pl.BlockSpec(memory_space=pltpu.HBM), pl.BlockSpec(memory_space=pl.ANY)
    return pl.pallas_call(
        kernel,
        name=name,
        out_shape=list(outs) + [sds(x.shape, x.dtype) for x in moves],
        in_specs=[VM] * nn + [hbm] * nf + [any_space] * na + [hbm] * nm,
        out_specs=[VM] * (len(outs) + nm),
        scratch_shapes=[pltpu.VMEM(x.shape, x.dtype) for x in far]
        + [pltpu.SemaphoreType.DMA((max(nf, 1),)), pltpu.SemaphoreType.DMA((max(nm * parts, 1),))]
        + list(scratch),
        compiler_params=VLIM,
    )(*near, *pin(far), *after, *pin(moves))


def sds(shape, dtype):
    return jax.ShapeDtypeStruct(shape, dtype)


def iota(shape, dim):
    return lax.broadcasted_iota(jnp.int32, shape, dim)


def core_id():
    return lax.axis_index("c")


def head_id():
    return lax.axis_index("head")


def dot(a, b):
    return jnp.dot(a, b, preferred_element_type=F32)


def hi_lo(x):
    hi = x.astype(BF16)
    return hi, (x - hi.astype(F32)).astype(BF16)


def tables_body(near, far, outs, own, page):
    pick_ref, count_ref, same_ref, mine_ref, spread_ref, spread16_ref = outs
    req = far[0].get()[...]
    slots, total = pick_ref.shape
    half = total // 2
    place = jnp.where((req // 16) % 2 == core_id(), 0, half) + (req // 32) * 16 + req % 16
    spread_ref[...] = jnp.where(iota((total, slots), 0) == place, 1.0, 0.0).astype(BF16)
    spread16_ref[...] = jnp.where(iota((total, slots), 0) // 16 == place // 16, 1.0, 0.0).astype(BF16)
    eye = iota((slots, slots), 0) == iota((slots, slots), 1)

    def to_col(row):
        return jnp.sum(jnp.where(eye, row.astype(F32), 0.0), axis=1, keepdims=True)

    req_col = to_col(req)
    same = req_col == req.astype(F32)
    same_ref[...] = jnp.where(same, 1.0, 0.0)
    slot_row = iota((slots, slots), 1).astype(F32)
    first = jnp.min(jnp.where(same, slot_row, 9999.0), axis=1, keepdims=True)
    leader = first == iota((slots, 1), 0).astype(F32)
    mine = (iota((slots, HD), 1) % 16).astype(F32) == to_col(req % 16)
    mine_ref[...] = jnp.where(mine & leader, 1.0, 0.0)
    lane_total = iota((slots, total), 1).astype(F32)
    pick_ref[...] = jnp.where(to_col(place) == lane_total, 1.0, 0.0).astype(BF16)
    lengths = far[3].get()[...].astype(F32)
    len_col = jnp.sum(jnp.where(req_col == lane_total, lengths, 0.0), axis=1, keepdims=True)
    count = jnp.clip(len_col - to_col(far[1].get()[...]) * page, 0.0, float(page))
    count = jnp.where(to_col(far[2].get()[...]) == 1.0, count, 0.0)
    count_ref[...] = jnp.broadcast_to(count, (slots, HD))


def slot_tables(slot_request, slot_page, slot_used, lengths, kv_cache, after):
    slots = kv_cache.shape[0]
    total = lengths.shape[0]
    return run(
        functools.partial(tables_body, page=kv_cache.shape[2]),
        "slot_tables",
        [
            sds((slots, total), BF16),
            sds((slots, HD), F32),
            sds((slots, slots), F32),
            sds((slots, HD), F32),
            sds((total, slots), BF16),
            sds((total, slots), BF16),
        ],
        [],
        [slot_request.reshape(1, slots), slot_page.reshape(1, slots), slot_used.reshape(1, slots), lengths.reshape(1, total)],
        after=[after],
        moves=[kv_cache],
    )


def attn_kernel(pick_ref, count_ref, same_ref, mine_ref, spread_ref, spread16_ref, kv_ref, qa_ref, qb_ref, keep_ref, send_ref, n_scr, m_scr, l_scr):
    slots = kv_ref.shape[0]
    page = kv_ref.shape[2]
    half = qa_ref.shape[0]
    chosen = dot(pick_ref[:, :half], qa_ref[...]) + dot(pick_ref[:, half:], qb_ref[...])
    low_lanes = iota((8, 2 * HD), 1) < HD
    rel = iota((16, 8 * page), 1) - (iota((16, 8 * page), 0) % 8) * page
    rel = rel.astype(F32)
    for b in range(slots // 8):
        q8 = chosen[b * 8 : b * 8 + 8]
        q16 = jnp.concatenate([jnp.where(low_lanes, q8, 0.0), jnp.where(low_lanes, 0.0, q8)], axis=0).astype(BF16)
        keys = kv_ref[b * 8 : b * 8 + 8, 0].reshape(8 * page, 2 * HD)
        vals = kv_ref[b * 8 : b * 8 + 8, 1].reshape(8 * page, 2 * HD)
        s = lax.dot_general(q16, keys, (((1,), (1,)), ((), ())), preferred_element_type=F32) * SCALE
        c8 = count_ref[b * 8 : b * 8 + 8, :1]
        ok = (rel >= 0.0) & (rel < jnp.concatenate([c8, c8], axis=0))
        s = jnp.where(ok, s, FLOOR)
        m = jnp.max(s, axis=1, keepdims=True)
        w = jnp.where(ok, jnp.exp(s - m), 0.0).astype(BF16)
        l = jnp.sum(w.astype(F32), axis=1, keepdims=True)
        n = dot(w, vals)
        for h in range(2):
            n_scr[h, b * 8 : b * 8 + 8, :] = n[8 * h : 8 * h + 8, HD * h : HD * h + HD]
            m_scr[h, b * 8 : b * 8 + 8, :] = jnp.broadcast_to(m[8 * h : 8 * h + 8], (8, slots))
            l_scr[h, b * 8 : b * 8 + 8, :] = jnp.broadcast_to(l[8 * h : 8 * h + 8], (8, slots))

    eye = iota((slots, slots), 0) == iota((slots, slots), 1)
    same = same_ref[...] > 0.0

    def to_row(wide):
        return jnp.sum(jnp.where(eye, wide, 0.0), axis=0, keepdims=True)

    group = iota((slots, HD), 1) // 16
    board = jnp.zeros((slots, HD), F32)
    for h in range(2):
        m_wide = m_scr[h]
        m_ref = jnp.max(jnp.where(same, to_row(m_wide), FLOOR), axis=1, keepdims=True)
        m_ref = m_ref.astype(BF16).astype(F32)
        lift = jnp.exp(m_wide - m_ref)
        n_hi, n_lo = hi_lo(n_scr[h] * lift)
        l_sum = jnp.sum(jnp.where(same, to_row(l_scr[h] * lift), 0.0), axis=1, keepdims=True)
        out = (dot(spread_ref[...], n_hi) + dot(spread_ref[...], n_lo)).astype(BF16)
        keep_ref[:, 16 * h : 16 * h + 16, :] = out[:half].reshape(half // 16, 16, HD)
        send_ref[:, 16 * h : 16 * h + 16, :] = out[half:].reshape(half // 16, 16, HD)
        l_hi = l_sum.astype(BF16).astype(F32)
        for i, stat in enumerate((m_ref, l_hi, l_sum - l_hi)):
            board = jnp.where(group == 2 * i + h, stat, board)
    board = jnp.where(mine_ref[...] > 0.0, board, 0.0).astype(BF16)
    out = dot(spread16_ref[...], board).astype(BF16)
    keep_ref[:, 32:48, :] = out[:half].reshape(half // 16, 16, HD)
    send_ref[:, 32:48, :] = out[half:].reshape(half // 16, 16, HD)


def attend_pages(tables, qa, qb):
    slots, total = tables[0].shape
    return pl.pallas_call(
        attn_kernel,
        name="attend_pages",
        out_shape=[jax.ShapeDtypeStruct((total // 32, 48, HD), BF16)] * 2,
        in_specs=[VM] * 9,
        out_specs=[VM] * 2,
        scratch_shapes=[
            pltpu.VMEM((2, slots, HD), F32),
            pltpu.VMEM((2, slots, slots), F32),
            pltpu.VMEM((2, slots, slots), F32),
        ],
        compiler_params=VLIM,
    )(*tables, qa.reshape(total // 2, 2 * HD), qb.reshape(total // 2, 2 * HD))


def merge_body(near, far, outs, own):
    (a_ref, b_ref), out_ref = near, outs[0]
    a, b = a_ref[:, 32:48, :].astype(F32), b_ref[:, 32:48, :].astype(F32)
    lane, row = iota(a.shape, 2), iota(a.shape, 1)
    board = jnp.zeros(a.shape, F32)
    for h in range(2):
        (ma, la), (mb, lb) = read_stats(a, h), read_stats(b, h)
        m = jnp.maximum(ma, mb)
        fa, fb = jnp.exp(ma - m), jnp.exp(mb - m)
        rows = slice(16 * h, 16 * h + 16)
        out_ref[:, rows, :] = (a_ref[:, rows, :].astype(F32) * fa + b_ref[:, rows, :].astype(F32) * fb).astype(BF16)
        l = la * fa + lb * fb
        l_hi = l.astype(BF16).astype(F32)
        for i, stat in enumerate((m, l_hi, l - l_hi)):
            board = jnp.where(lane == row + 32 * i + 16 * h, stat, board)
    out_ref[:, 32:48, :] = board.astype(BF16)


def merge(a, b, after):
    return run(merge_body, "merge", [sds(a.shape, BF16)], [a, b], [], after=[after])[0]


def fetch(after, *arrays):
    return run(lambda *_: None, "fetch", [], [], [], after=[after], moves=arrays)


def column_kernel(w_ref, after_ref, out_ref, sem):
    width = out_ref.shape[1]
    cols = pl.ds(pl.multiple_of(head_id() * width, width), width)
    copy = pltpu.make_async_copy(w_ref.at[:, cols], out_ref, sem)
    copy.start()
    copy.wait()


def fetch_columns(after, w):
    return pl.pallas_call(
        column_kernel,
        name="fetch_columns",
        out_shape=sds((w.shape[0], w.shape[1] // 4), w.dtype),
        in_specs=[pl.BlockSpec(memory_space=pltpu.HBM), pl.BlockSpec(memory_space=pl.ANY)],
        out_specs=VM,
        scratch_shapes=[pltpu.SemaphoreType.DMA],
        compiler_params=VLIM,
    )(pltpu.with_memory_space_constraint(w, pltpu.HBM), after)


def read_stats(board, h):
    lane, row = iota(board.shape, 2), iota(board.shape, 1) + 16 * h
    m = jnp.sum(jnp.where(lane == row, board, 0.0), axis=2, keepdims=True)
    l = jnp.sum(jnp.where((lane == row + 32) | (lane == row + 64), board, 0.0), axis=2, keepdims=True)
    return jnp.where(l > 0.0, m, FLOOR), l


def owner_body(near, far, outs, own_scratch):
    part_ref, w_ref = near
    board = part_ref[:, 32:48, :].astype(F32)
    q = far[0].get()[...].astype(F32)
    nkv = far[1].get()[...].astype(F32)
    nkv = jnp.concatenate([nkv[:, 0, :], nkv[:, 1, :]], axis=1)
    att = []
    for h in range(2):
        m, l = read_stats(board, h)
        own = jnp.sum(q[:, HD * h : HD * h + HD] * nkv[:, HD * h : HD * h + HD], axis=1, keepdims=True) * SCALE
        top = jnp.maximum(jnp.max(m, axis=0), own)
        lift = jnp.exp(m - top[None])
        n = jnp.sum(part_ref[:, 16 * h : 16 * h + 16, :].astype(F32) * lift, axis=0)
        den = jnp.sum(l * lift, axis=0)
        new = jnp.exp(own - top)
        v = nkv[:, 2 * HD + HD * h : 2 * HD + HD * h + HD]
        att.append((n + new * v) / (den + new))
    attended = jnp.concatenate(att, axis=1).astype(BF16)
    head = head_id()
    width = outs[0].shape[1]
    for k in range(4):
        first = pl.multiple_of(((head + k) % 4) * width, width)
        outs[k][...] = dot(attended, w_ref[:, pl.ds(first, width)]).astype(BF16)


def owner_part(parts, queries, new_kv, out_weight):
    rows = queries.shape[0]
    width = out_weight.shape[1] // 4
    return run(owner_body, "owner_part", [sds((rows, width), BF16)] * 4, [parts, out_weight], [queries, new_kv])


def flip(x, terms):
    n = x.shape[1]
    eye = jnp.where(iota((n, n), 0) == iota((n, n), 1), 1.0, 0.0).astype(BF16)
    x = x.astype(F32)
    out = jnp.zeros((n, x.shape[0]), F32)
    for _ in range(terms):
        part = x.astype(BF16)
        out = out + lax.dot_general(eye, part, (((1,), (1,)), ((), ())), preferred_element_type=F32)
        x = x - part.astype(F32)
    return out


def rank_of(hit):
    rows = hit.shape[0]
    before = jnp.where(iota((rows, rows), 0) > iota((rows, rows), 1), 1.0, 0.0).astype(BF16)
    return dot(before, hit.astype(BF16))


def dispatch_body(near, far, outs, own):
    hid_ref, disp_ref = outs
    rows, width = hid_ref.shape
    first = pl.multiple_of(head_id() * width, width)
    acc = sum(p[...].astype(F32) for p in near)
    routes = flip(far[1].get()[...], 1)
    cells = disp_ref.shape[0] * 8
    lane = iota((rows, cells), 1)
    expert = (lane // 8).astype(F32)
    hit = jnp.zeros((rows, cells), F32)
    for k in range(routes.shape[1]):
        hit = hit + jnp.where(routes[:, k : k + 1] == expert, 1.0, 0.0)
    hit = jnp.where(rank_of(hit) == (lane % 4).astype(F32), hit, 0.0)
    left = lane % 8 < 4
    pick = jnp.concatenate([jnp.where(left, hit, 0.0), jnp.where(left, 0.0, hit)], axis=0).astype(BF16)
    hid = (far[0].get()[:, pl.ds(first, width)].astype(F32) + acc).astype(BF16)
    hid_ref[...] = hid
    both = jnp.concatenate([hid[:, : width // 2], hid[:, width // 2 :]], axis=0)
    out = lax.dot_general(pick, both, (((0,), (0,)), ((), ())), preferred_element_type=F32)
    disp_ref[...] = out.astype(BF16).reshape(disp_ref.shape)


def dispatch(parts, residual, routes, experts):
    rows, width = parts[0].shape
    outs = [sds((rows, width), BF16), sds((experts, 8, width // 2), BF16)]
    return run(dispatch_body, "dispatch", outs, parts, [residual, routes.T])


def unfold(x):
    n, _, w = x.shape
    x = x.reshape(n // 2, 2, 8, w)
    a, b = x[:, 0], x[:, 1]
    top = iota(a.shape, 1) < 4
    left = jnp.where(top, a, pltpu.roll(b, 4, 1))
    right = jnp.where(top, pltpu.roll(a, 4, 1), b)
    return left.reshape(n * 4, w), right.reshape(n * 4, w)


def fold(left, right):
    rows, w = left.shape
    left, right = left.reshape(rows // 8, 8, w), right.reshape(rows // 8, 8, w)
    top = iota(left.shape, 1) < 4
    a = jnp.where(top, left, pltpu.roll(right, 4, 1))
    b = jnp.where(top, pltpu.roll(left, 4, 1), right)
    return a, b


def gate_body(near, far, outs, own):
    inner_ref, xs = outs[0], own[0]
    wg_ref, wu_ref = near[4:]
    head = head_id()
    w = near[0].shape[2]
    total = jnp.zeros((inner_ref.shape[0], 1), F32)
    for k in range(4):
        for f, part in enumerate(unfold(near[k][...].astype(F32))):
            xs[2 * k + f] = part
            total = total + jnp.sum(part * part, axis=1, keepdims=True)
    scale = lax.rsqrt(total / (8 * w) + EPS)
    gain_ref = far[0].get()
    gate = jnp.zeros(inner_ref.shape, F32)
    up = jnp.zeros(inner_ref.shape, F32)
    for k in range(4):
        for f in range(2):
            first = pl.multiple_of(((head + 4 - k) % 4) * 2 * w + f * w, w)
            normed = (xs[2 * k + f] * scale * gain_ref[:, pl.ds(first, w)]).astype(BF16)
            gate = gate + dot(normed, wg_ref[pl.ds(first, w), :])
            up = up + dot(normed, wu_ref[pl.ds(first, w), :])
    inner_ref[...] = (gate / (1.0 + jnp.exp(-gate)) * up).astype(BF16)


def gate_up(xs, gain, w_gate, w_up):
    n, _, w = xs[0].shape
    out = sds((n * 4, w_gate.shape[1]), BF16)
    scratch = [pltpu.VMEM((8, n * 4, w), F32)]
    return run(gate_body, "gate_up", [out], [*xs, w_gate, w_up], [gain.reshape(1, -1)], scratch)[0]


def down_body(near, far, outs, own):
    w_ref, out_ref = near[4], outs[0]
    head = head_id()
    rows, eff = near[0].shape
    width = w_ref.shape[1]
    acc = jnp.zeros((rows, width), F32)
    for k in range(4):
        first = pl.multiple_of(((head + 4 - k) % 4) * eff, eff)
        acc = acc + dot(near[k][...], w_ref[pl.ds(first, eff), :])
    a, b = fold(acc[:, : width // 2], acc[:, width // 2 :])
    out_ref[:, 0] = a.astype(BF16)
    out_ref[:, 1] = b.astype(BF16)


def down(inners, w_cols):
    rows = inners[0].shape[0]
    width = w_cols.shape[1]
    out = run(down_body, "down", [sds((rows // 8, 2, 8, width // 2), BF16)], [*inners, w_cols], [])[0]
    return out.reshape(rows // 4, 8, width // 2)


def blend_body(near, far, outs, own):
    y_ref, out_ref = near[0], outs[0]
    rows = out_ref.shape[0]
    routes, share = flip(far[1].get()[...], 1), flip(far[2].get()[...], 3)
    cells = y_ref.shape[0] * 4
    lane = iota((rows, cells), 1)
    expert = (lane // 4).astype(F32)
    hit = jnp.zeros((rows, cells), F32)
    mix = jnp.zeros((rows, cells), F32)
    for k in range(routes.shape[1]):
        on = routes[:, k : k + 1] == expert
        hit = hit + jnp.where(on, 1.0, 0.0)
        mix = mix + jnp.where(on, share[:, k : k + 1], 0.0)
    mix = jnp.where(rank_of(hit) == (lane % 4).astype(F32), mix, 0.0)
    m_hi, m_lo = hi_lo(mix)
    w = y_ref.shape[2]
    hid_ref = far[0].get()
    for f, part in enumerate(unfold(y_ref[...].astype(F32))):
        part = part.astype(BF16)
        hid = hid_ref[:, f * w : f * w + w].astype(F32)
        out_ref[:, f * w : f * w + w] = (hid + (dot(m_hi, part) + dot(m_lo, part))).astype(BF16)


def blend(returned, hidden, routes, route_weights):
    out = sds(hidden.shape, BF16)
    return run(blend_body, "blend", [out], [returned], [hidden, routes.T, route_weights.T])[0]


def norm_body(near, far, outs, own):
    head = head_id()
    w = near[0].shape[1]
    parts = [s[...].astype(F32) for s in (far[1].get(), *near)]
    total = sum(jnp.sum(p * p, axis=1, keepdims=True) for p in parts)
    scale = lax.rsqrt(total / (4 * w) + EPS)
    gain_ref = far[0].get()
    for k, p in enumerate(parts):
        cols = pl.ds(pl.multiple_of(((head + 4 - k) % 4) * w, w), w)
        outs[0][:, cols] = (p * scale * gain_ref[:, cols]).astype(BF16)


def norm_parts(parts, gain):
    rows, w = parts[0].shape
    return run(norm_body, "norm_parts", [sds((rows, 4 * w), BF16)], parts[1:], [gain.reshape(1, -1), parts[0]])[0]


def from_heads(x):
    n = lax.axis_size("head")
    return [x] + [lax.ppermute(x, "head", [(i, (i + k) % n) for i in range(n)]) for k in range(1, n)]


def to_heads(xs):
    n = lax.axis_size("head")
    return [xs[0]] + [lax.ppermute(xs[k], "head", [(i, (i + k) % n) for i in range(n)]) for k in range(1, n)]


def swap_core(x):
    return lax.ppermute(x, "c", [(0, 1), (1, 0)])


def local(
    residual, queries, new_kv, kv_cache, lengths, slot_request, slot_page, slot_used, out_weight,
    norm_gain, routes, route_weights, w_gate, w_up, w_down, next_gain, next_weight,
):
    rows = queries.shape[0]
    experts = lax.axis_size(REQ)
    chips = experts // 2
    w_down_all = lax.all_gather(w_down.reshape(w_down.shape[1:]), "head", axis=0, tiled=True)
    spread = jnp.broadcast_to(queries[None], (chips,) + queries.shape)
    qa = lax.all_to_all(spread, ("z", "y"), 0, 0, tiled=True)
    tables = slot_tables(slot_request, slot_page, slot_used, lengths, kv_cache, qa)
    keep, send = attend_pages(tables, qa, swap_core(qa))
    out_weight = fetch(send, out_weight)[0]
    arrived = lax.all_to_all(merge(keep, swap_core(send), out_weight), ("z", "y"), 0, 0, tiled=True)
    shares = to_heads(owner_part(arrived, queries, new_kv, out_weight))
    hidden, disp = dispatch(shares, residual, routes, experts)
    tokens = lax.all_to_all(disp, REQ, 0, 0, tiled=True)
    w_gate, w_up = fetch(tokens, w_gate[0], w_up[0])
    inner = gate_up(from_heads(tokens), norm_gain, w_gate, w_up)
    w_cols = fetch_columns(inner, w_down_all)
    expert_out = down(from_heads(inner), w_cols)
    returned = lax.all_to_all(expert_out, REQ, 0, 0, tiled=True)
    stream = blend(returned, hidden, routes, route_weights)
    normed = norm_parts(from_heads(stream), next_gain)
    next_qkv = jnp.einsum("td,dcf->tcf", normed, next_weight, preferred_element_type=F32).astype(BF16)
    return stream, next_qkv


def solution(mesh):
    split = Mesh(mesh.devices.reshape(8, 4, 2, 4), ("z", "y", "c", "head"))
    placed = (
        P(REQ, None),
        P(REQ, "head"),
        P(REQ, None, "head"),
        P(REQ, None, None, "head"),
        P(),
        P(REQ),
        P(REQ),
        P(REQ),
        P("head", None),
        P(),
        P(REQ, None),
        P(REQ, None),
        P(REQ, None, "head"),
        P(REQ, None, "head"),
        P(REQ, "head", None),
        P(),
        P(None, None, "head"),
    )
    return jax.shard_map(
        local,
        mesh=split,
        in_specs=placed,
        out_specs=(P(REQ, "head"), P(REQ, None, "head")),
        check_vma=False,
    )
```

```python
import functools
import math

import jax
import jax.numpy as jnp
from jax import lax
from jax.experimental import pallas as pl
from jax.experimental.pallas import tpu as pltpu
from jax.sharding import Mesh, PartitionSpec as P

HD = 128
EPS = 1e-06
FLOOR = -(2.0**99)
SCALE = 1.0 / math.sqrt(HD)
F32 = jnp.float32
BF16 = jnp.bfloat16
REQ = ("z", "y", "c")
VLIM = pltpu.CompilerParams(vmem_limit_bytes=24 * 1024 * 1024)
VM = pl.BlockSpec(memory_space=pltpu.VMEM)


class Pending:
    def __init__(self, buf, copy):
        self.buf, self.copy, self.done = buf, copy, False

    def get(self):
        if not self.done:
            self.copy.wait()
            self.done = True
        return self.buf


def run(body, name, outs, near, far, scratch=(), after=(), moves=()):
    nn, nf, na, nm = len(near), len(far), len(after), len(moves)
    parts = 4

    def kernel(*refs):
        ins, refs = refs[: nn + nf + na + nm], refs[nn + nf + na + nm :]
        outputs, moved, rest = refs[: len(outs)], refs[len(outs) : len(outs) + nm], refs[len(outs) + nm :]
        bufs, sems, move_sems, own = rest[:nf], rest[nf], rest[nf + 1], rest[nf + 2 :]
        copies = [pltpu.make_async_copy(ins[nn + i], bufs[i], sems.at[i]) for i in range(nf)]
        for copy in copies:
            copy.start()
        pending = [Pending(b, c) for b, c in zip(bufs, copies)]
        moving = []
        for i in range(nm):
            rows = moved[i].shape[0] // parts
            for j in range(parts):
                src, dst = ins[nn + nf + na + i].at[pl.ds(j * rows, rows)], moved[i].at[pl.ds(j * rows, rows)]
                moving.append(pltpu.make_async_copy(src, dst, move_sems.at[parts * i + j]))
        for copy in moving:
            copy.start()
        body(ins[:nn], pending, outputs, own)
        for p in pending:
            p.get()
        for copy in moving:
            copy.wait()

    def pin(xs):
        return [pltpu.with_memory_space_constraint(x, pltpu.HBM) for x in xs]

    hbm, any_space = pl.BlockSpec(memory_space=pltpu.HBM), pl.BlockSpec(memory_space=pl.ANY)
    return pl.pallas_call(
        kernel,
        name=name,
        out_shape=list(outs) + [sds(x.shape, x.dtype) for x in moves],
        in_specs=[VM] * nn + [hbm] * nf + [any_space] * na + [hbm] * nm,
        out_specs=[VM] * (len(outs) + nm),
        scratch_shapes=[pltpu.VMEM(x.shape, x.dtype) for x in far]
        + [pltpu.SemaphoreType.DMA((max(nf, 1),)), pltpu.SemaphoreType.DMA((max(nm * parts, 1),))]
        + list(scratch),
        compiler_params=VLIM,
    )(*near, *pin(far), *after, *pin(moves))


def sds(shape, dtype):
    return jax.ShapeDtypeStruct(shape, dtype)


def iota(shape, dim):
    return lax.broadcasted_iota(jnp.int32, shape, dim)


def core_id():
    return lax.axis_index("c")


def head_id():
    return lax.axis_index("head")


def dot(a, b):
    return jnp.dot(a, b, preferred_element_type=F32)


def hi_lo(x):
    hi = x.astype(BF16)
    return hi, (x - hi.astype(F32)).astype(BF16)


def hits(routes, expert):
    hit = jnp.zeros(expert.shape, F32)
    for k in range(routes.shape[1]):
        hit = hit + jnp.where(routes[:, k : k + 1] == expert, 1.0, 0.0)
    return hit


def cell_map(routes, expert, lane):
    hit = hits(routes, expert)
    hit = jnp.where(rank_of(hit) == (lane % 4).astype(F32), hit, 0.0)
    left = lane % 8 < 4
    return jnp.concatenate([jnp.where(left, hit, 0.0), jnp.where(left, 0.0, hit)], axis=0).astype(BF16)


def outset_body(near, far, outs, own):
    chips, _, width = outs[0].shape
    rows = far[0].buf.shape[0]
    routes = flip(far[2].get()[...], 1)
    lane = iota((rows, chips * 16), 1)
    expert = (lane // 16) * 2 + (core_id() + (lane // 8) % 2) % 2
    pick = cell_map(routes, expert.astype(F32), lane)
    first = pl.multiple_of(head_id() * 2 * width, 2 * width)
    res = far[1].get()
    both = jnp.concatenate([res[:, pl.ds(first, width)], res[:, pl.ds(first + width, width)]], axis=0)
    out = lax.dot_general(pick, both, (((0,), (0,)), ((), ())), preferred_element_type=F32)
    outs[0][:, 16:32, :] = out.astype(BF16).reshape(chips, 16, width)
    q = far[0].get()[...]
    outs[0][:, 0:16, :] = jnp.broadcast_to(q[None], (chips,) + q.shape)


def outset(queries, residual, routes, chips):
    out = sds((chips, 32, queries.shape[1]), BF16)
    return run(outset_body, "outset", [out], [], [queries, residual, routes.T])[0]


def tables_body(near, far, outs, own, page):
    pick_ref, count_ref, same_ref, mine_ref, spread_ref, spread16_ref = outs
    req = far[0].get()[...]
    slots, total = pick_ref.shape
    half = total // 2
    place = jnp.where((req // 16) % 2 == core_id(), 0, half) + (req // 32) * 16 + req % 16
    spread_ref[...] = jnp.where(iota((total, slots), 0) == place, 1.0, 0.0).astype(BF16)
    spread16_ref[...] = jnp.where(iota((total, slots), 0) // 16 == place // 16, 1.0, 0.0).astype(BF16)
    eye = iota((slots, slots), 0) == iota((slots, slots), 1)

    def to_col(row):
        return jnp.sum(jnp.where(eye, row.astype(F32), 0.0), axis=1, keepdims=True)

    req_col = to_col(req)
    same = req_col == req.astype(F32)
    same_ref[...] = jnp.where(same, 1.0, 0.0)
    slot_row = iota((slots, slots), 1).astype(F32)
    first = jnp.min(jnp.where(same, slot_row, 9999.0), axis=1, keepdims=True)
    leader = first == iota((slots, 1), 0).astype(F32)
    mine = (iota((slots, HD), 1) % 16).astype(F32) == to_col(req % 16)
    mine_ref[...] = jnp.where(mine & leader, 1.0, 0.0)
    lane_total = iota((slots, total), 1).astype(F32)
    pick_ref[...] = jnp.where(to_col(place) == lane_total, 1.0, 0.0).astype(BF16)
    lengths = far[3].get()[...].astype(F32)
    len_col = jnp.sum(jnp.where(req_col == lane_total, lengths, 0.0), axis=1, keepdims=True)
    count = jnp.clip(len_col - to_col(far[1].get()[...]) * page, 0.0, float(page))
    count = jnp.where(to_col(far[2].get()[...]) == 1.0, count, 0.0)
    count_ref[...] = jnp.broadcast_to(count, (slots, HD))


def slot_tables(slot_request, slot_page, slot_used, lengths, kv_cache, after):
    slots = kv_cache.shape[0]
    total = lengths.shape[0]
    return run(
        functools.partial(tables_body, page=kv_cache.shape[2]),
        "slot_tables",
        [
            sds((slots, total), BF16),
            sds((slots, HD), F32),
            sds((slots, slots), F32),
            sds((slots, HD), F32),
            sds((total, slots), BF16),
            sds((total, slots), BF16),
        ],
        [],
        [slot_request.reshape(1, slots), slot_page.reshape(1, slots), slot_used.reshape(1, slots), lengths.reshape(1, total)],
        after=after,
        moves=[kv_cache],
    )


def attn_kernel(pick_ref, count_ref, same_ref, mine_ref, spread_ref, spread16_ref, kv_ref, qa_ref, qb_ref, keep_ref, send_ref, res_ref, n_scr, m_scr, l_scr):
    slots = kv_ref.shape[0]
    page = kv_ref.shape[2]
    half = qa_ref.shape[0] * 16
    qa, qb = (r[:, 0:16, :].reshape(half, 2 * HD) for r in (qa_ref, qb_ref))
    chosen = dot(pick_ref[:, :half], qa) + dot(pick_ref[:, half:], qb)
    core = core_id()
    res_ref[:, core] = qa_ref[:, 16:24, :]
    res_ref[:, 1 - core] = qb_ref[:, 24:32, :]
    low_lanes = iota((8, 2 * HD), 1) < HD
    rel = iota((16, 8 * page), 1) - (iota((16, 8 * page), 0) % 8) * page
    rel = rel.astype(F32)
    for b in range(slots // 8):
        q8 = chosen[b * 8 : b * 8 + 8]
        q16 = jnp.concatenate([jnp.where(low_lanes, q8, 0.0), jnp.where(low_lanes, 0.0, q8)], axis=0).astype(BF16)
        keys = kv_ref[b * 8 : b * 8 + 8, 0].reshape(8 * page, 2 * HD)
        vals = kv_ref[b * 8 : b * 8 + 8, 1].reshape(8 * page, 2 * HD)
        s = lax.dot_general(q16, keys, (((1,), (1,)), ((), ())), preferred_element_type=F32) * SCALE
        c8 = count_ref[b * 8 : b * 8 + 8, :1]
        ok = (rel >= 0.0) & (rel < jnp.concatenate([c8, c8], axis=0))
        s = jnp.where(ok, s, FLOOR)
        m = jnp.max(s, axis=1, keepdims=True)
        w = jnp.where(ok, jnp.exp(s - m), 0.0).astype(BF16)
        l = jnp.sum(w.astype(F32), axis=1, keepdims=True)
        n = dot(w, vals)
        for h in range(2):
            n_scr[h, b * 8 : b * 8 + 8, :] = n[8 * h : 8 * h + 8, HD * h : HD * h + HD]
            m_scr[h, b * 8 : b * 8 + 8, :] = jnp.broadcast_to(m[8 * h : 8 * h + 8], (8, slots))
            l_scr[h, b * 8 : b * 8 + 8, :] = jnp.broadcast_to(l[8 * h : 8 * h + 8], (8, slots))

    eye = iota((slots, slots), 0) == iota((slots, slots), 1)
    same = same_ref[...] > 0.0

    def to_row(wide):
        return jnp.sum(jnp.where(eye, wide, 0.0), axis=0, keepdims=True)

    group = iota((slots, HD), 1) // 16
    board = jnp.zeros((slots, HD), F32)
    for h in range(2):
        m_wide = m_scr[h]
        m_ref = jnp.max(jnp.where(same, to_row(m_wide), FLOOR), axis=1, keepdims=True)
        m_ref = m_ref.astype(BF16).astype(F32)
        lift = jnp.exp(m_wide - m_ref)
        n_hi, n_lo = hi_lo(n_scr[h] * lift)
        l_sum = jnp.sum(jnp.where(same, to_row(l_scr[h] * lift), 0.0), axis=1, keepdims=True)
        out = (dot(spread_ref[...], n_hi) + dot(spread_ref[...], n_lo)).astype(BF16)
        keep_ref[:, 16 * h : 16 * h + 16, :] = out[:half].reshape(half // 16, 16, HD)
        send_ref[:, 16 * h : 16 * h + 16, :] = out[half:].reshape(half // 16, 16, HD)
        l_hi = l_sum.astype(BF16).astype(F32)
        for i, stat in enumerate((m_ref, l_hi, l_sum - l_hi)):
            board = jnp.where(group == 2 * i + h, stat, board)
    board = jnp.where(mine_ref[...] > 0.0, board, 0.0).astype(BF16)
    out = dot(spread16_ref[...], board).astype(BF16)
    keep_ref[:, 32:48, :] = out[:half].reshape(half // 16, 16, HD)
    send_ref[:, 32:48, :] = out[half:].reshape(half // 16, 16, HD)


def attend_pages(tables, qa, qb):
    slots, total = tables[0].shape
    return pl.pallas_call(
        attn_kernel,
        name="attend_pages",
        out_shape=[sds((total // 32, 48, HD), BF16)] * 2 + [sds((total // 32, 2, 8, 2 * HD), BF16)],
        in_specs=[VM] * 9,
        out_specs=[VM] * 3,
        scratch_shapes=[
            pltpu.VMEM((2, slots, HD), F32),
            pltpu.VMEM((2, slots, slots), F32),
            pltpu.VMEM((2, slots, slots), F32),
        ],
        compiler_params=VLIM,
    )(*tables, qa, qb)


def merge_body(near, far, outs, own):
    (a_ref, b_ref), out_ref = near, outs[0]
    a, b = a_ref[:, 32:48, :].astype(F32), b_ref[:, 32:48, :].astype(F32)
    lane, row = iota(a.shape, 2), iota(a.shape, 1)
    board = jnp.zeros(a.shape, F32)
    for h in range(2):
        (ma, la), (mb, lb) = read_stats(a, h), read_stats(b, h)
        m = jnp.maximum(ma, mb)
        fa, fb = jnp.exp(ma - m), jnp.exp(mb - m)
        rows = slice(16 * h, 16 * h + 16)
        out_ref[:, rows, :] = (a_ref[:, rows, :].astype(F32) * fa + b_ref[:, rows, :].astype(F32) * fb).astype(BF16)
        l = la * fa + lb * fb
        l_hi = l.astype(BF16).astype(F32)
        for i, stat in enumerate((m, l_hi, l - l_hi)):
            board = jnp.where(lane == row + 32 * i + 16 * h, stat, board)
    out_ref[:, 32:48, :] = board.astype(BF16)


def merge(a, b):
    return run(merge_body, "merge", [sds(a.shape, BF16)], [a, b], [])[0]


def fetch(after, *arrays):
    return run(lambda *_: None, "fetch", [], [], [], after=[after], moves=arrays)


def split_kernel(w_ref, *refs):
    outs, sems = refs[:4], refs[4]
    width = outs[0].shape[1]
    copies = []
    for k in range(4):
        cols = pl.ds(pl.multiple_of(((head_id() + k) % 4) * width, width), width)
        copies.append(pltpu.make_async_copy(w_ref.at[:, cols], outs[k], sems.at[k]))
    for copy in copies:
        copy.start()
    for copy in copies:
        copy.wait()


def split_columns(w):
    return pl.pallas_call(
        split_kernel,
        name="split_columns",
        out_shape=[sds((w.shape[0], w.shape[1] // 4), w.dtype)] * 4,
        in_specs=[pl.BlockSpec(memory_space=pltpu.HBM)],
        out_specs=[VM] * 4,
        scratch_shapes=[pltpu.SemaphoreType.DMA((4,))],
        compiler_params=VLIM,
    )(pltpu.with_memory_space_constraint(w, pltpu.HBM))


def read_stats(board, h):
    lane, row = iota(board.shape, 2), iota(board.shape, 1) + 16 * h
    m = jnp.sum(jnp.where(lane == row, board, 0.0), axis=2, keepdims=True)
    l = jnp.sum(jnp.where((lane == row + 32) | (lane == row + 64), board, 0.0), axis=2, keepdims=True)
    return jnp.where(l > 0.0, m, FLOOR), l


def owner_body(near, far, outs, own_scratch):
    part_ref = near[0]
    board = part_ref[:, 32:48, :].astype(F32)
    q = far[0].get()[...].astype(F32)
    nkv = far[1].get()[...].astype(F32)
    nkv = jnp.concatenate([nkv[:, 0, :], nkv[:, 1, :]], axis=1)
    att = []
    for h in range(2):
        m, l = read_stats(board, h)
        own = jnp.sum(q[:, HD * h : HD * h + HD] * nkv[:, HD * h : HD * h + HD], axis=1, keepdims=True) * SCALE
        top = jnp.maximum(jnp.max(m, axis=0), own)
        lift = jnp.exp(m - top[None])
        n = jnp.sum(part_ref[:, 16 * h : 16 * h + 16, :].astype(F32) * lift, axis=0)
        den = jnp.sum(l * lift, axis=0)
        new = jnp.exp(own - top)
        v = nkv[:, 2 * HD + HD * h : 2 * HD + HD * h + HD]
        att.append((n + new * v) / (den + new))
    att_ref, disp_ref = outs
    att_ref[...] = jnp.concatenate(att, axis=1).astype(BF16)
    rows = att_ref.shape[0]
    lane = iota((rows, disp_ref.shape[0] * 8), 1)
    pick = cell_map(flip(far[2].get()[...], 1), (lane // 8).astype(F32), lane)
    both = jnp.concatenate(att, axis=0).astype(BF16)
    out = lax.dot_general(pick, both, (((0,), (0,)), ((), ())), preferred_element_type=F32)
    disp_ref[...] = out.astype(BF16).reshape(disp_ref.shape)


def owner_part(parts, queries, new_kv, routes, experts):
    outs = [sds(queries.shape, BF16), sds((experts, 8, HD), BF16)]
    return run(owner_body, "owner_part", outs, [parts], [queries, new_kv, routes.T])


def flip(x, terms):
    n = x.shape[1]
    eye = jnp.where(iota((n, n), 0) == iota((n, n), 1), 1.0, 0.0).astype(BF16)
    x = x.astype(F32)
    out = jnp.zeros((n, x.shape[0]), F32)
    for _ in range(terms):
        part = x.astype(BF16)
        out = out + lax.dot_general(eye, part, (((1,), (1,)), ((), ())), preferred_element_type=F32)
        x = x - part.astype(F32)
    return out


def rank_of(hit):
    rows = hit.shape[0]
    before = jnp.where(iota((rows, rows), 0) > iota((rows, rows), 1), 1.0, 0.0).astype(BF16)
    return dot(before, hit.astype(BF16))


def unfold(x):
    n, _, w = x.shape
    x = x.reshape(n // 2, 2, 8, w)
    a, b = x[:, 0], x[:, 1]
    top = iota(a.shape, 1) < 4
    left = jnp.where(top, a, pltpu.roll(b, 4, 1))
    right = jnp.where(top, pltpu.roll(a, 4, 1), b)
    return left.reshape(n * 4, w), right.reshape(n * 4, w)


def fold(left, right):
    rows, w = left.shape
    left, right = left.reshape(rows // 8, 8, w), right.reshape(rows // 8, 8, w)
    top = iota(left.shape, 1) < 4
    a = jnp.where(top, left, pltpu.roll(right, 4, 1))
    b = jnp.where(top, pltpu.roll(left, 4, 1), right)
    return a, b


def expert_body(near, far, outs, own):
    inner_ref, hid_ref = outs
    xs = own[0]
    att, (wo_ref, wg_ref, wu_ref) = near[:4], near[4:]
    gain, mine, res, own_res = far[0], far[1:5], far[5:9], far[9]
    head = head_id()
    n = inner_ref.shape[0]
    eff = 2 * HD
    w = xs.shape[2]
    att = [jnp.concatenate(unfold(a[...].astype(F32)), axis=1).astype(BF16) for a in att]
    block = [pl.multiple_of(((head + 4 - k) % 4) * eff, eff) for k in range(4)]
    total = jnp.zeros((n, 1), F32)
    for k in range(4):
        pair = unfold(res[k].get()[...].astype(F32))
        for f in range(2):
            first = pl.multiple_of(((head + 4 - k) % 4) * 2 * w + f * w, w)
            acc = dot(att[0], wo_ref[pl.ds(block[0], eff), pl.ds(first, w)])
            for i in range(1, 4):
                acc = acc + dot(att[i], wo_ref[pl.ds(block[i], eff), pl.ds(first, w)])
            part = (pair[f] + acc).astype(BF16).astype(F32)
            xs[2 * k + f] = part
            total = total + jnp.sum(part * part, axis=1, keepdims=True)
    scale = lax.rsqrt(total / (8 * w) + EPS)
    gain_ref = gain.get()
    gate = jnp.zeros((n, wg_ref.shape[1]), F32)
    up = jnp.zeros((n, wg_ref.shape[1]), F32)
    for k in range(4):
        for f in range(2):
            first = pl.multiple_of(((head + 4 - k) % 4) * 2 * w + f * w, w)
            normed = (xs[2 * k + f] * scale * gain_ref[:, pl.ds(first, w)]).astype(BF16)
            gate = gate + dot(normed, wg_ref[pl.ds(first, w), :])
            up = up + dot(normed, wu_ref[pl.ds(first, w), :])
    inner_ref[...] = (gate / (1.0 + jnp.exp(-gate)) * up).astype(BF16)
    cols = pl.ds(pl.multiple_of(head * 2 * w, 2 * w), 2 * w)
    acc = own_res.get()[:, cols].astype(F32)
    acc = acc + sum(dot(mine[i].get()[...], wo_ref[pl.ds(block[i], eff), cols]) for i in range(4))
    hid_ref[...] = acc.astype(BF16)


def expert_rows(tokens, out_weight, w_gate, w_up, gain, mine, res, residual):
    n, _, half = tokens[0].shape
    w = res[0].shape[2]
    outs = [sds((n * 4, w_gate.shape[1]), BF16), sds((residual.shape[0], 2 * w), BF16)]
    scratch = [pltpu.VMEM((8, n * 4, w), F32)]
    near = [*tokens, out_weight, w_gate, w_up]
    return run(expert_body, "expert_rows", outs, near, [gain.reshape(1, -1), *mine, *res, residual], scratch)


def down_body(near, far, outs, own):
    out_ref = outs[0]
    acc = sum(dot(near[k][...], near[4 + k][...]) for k in range(4))
    width = acc.shape[1]
    a, b = fold(acc[:, : width // 2], acc[:, width // 2 :])
    out_ref[:, 0] = a.astype(BF16)
    out_ref[:, 1] = b.astype(BF16)


def down(inners, w_cols):
    rows = inners[0].shape[0]
    width = w_cols[0].shape[1]
    out = run(down_body, "down", [sds((rows // 8, 2, 8, width // 2), BF16)], [*inners, *w_cols], [])[0]
    return out.reshape(rows // 4, 8, width // 2)


def blend_body(near, far, outs, own):
    y_ref, out_ref = near[0], outs[0]
    rows = out_ref.shape[0]
    routes, share = flip(far[1].get()[...], 1), flip(far[2].get()[...], 3)
    cells = y_ref.shape[0] * 4
    lane = iota((rows, cells), 1)
    expert = (lane // 4).astype(F32)
    mix = jnp.zeros((rows, cells), F32)
    for k in range(routes.shape[1]):
        mix = mix + jnp.where(routes[:, k : k + 1] == expert, share[:, k : k + 1], 0.0)
    mix = jnp.where(rank_of(hits(routes, expert)) == (lane % 4).astype(F32), mix, 0.0)
    m_hi, m_lo = hi_lo(mix)
    w = y_ref.shape[2]
    hid_ref = far[0].get()
    for f, part in enumerate(unfold(y_ref[...].astype(F32))):
        part = part.astype(BF16)
        hid = hid_ref[:, f * w : f * w + w].astype(F32)
        out_ref[:, f * w : f * w + w] = (hid + (dot(m_hi, part) + dot(m_lo, part))).astype(BF16)


def blend(returned, hidden, routes, route_weights):
    out = sds(hidden.shape, BF16)
    return run(blend_body, "blend", [out], [returned], [hidden, routes.T, route_weights.T])[0]


def norm_body(near, far, outs, own):
    head = head_id()
    w = near[0].shape[1]
    parts = [s[...].astype(F32) for s in (far[1].get(), *near)]
    total = sum(jnp.sum(p * p, axis=1, keepdims=True) for p in parts)
    scale = lax.rsqrt(total / (4 * w) + EPS)
    gain_ref = far[0].get()
    for k, p in enumerate(parts):
        cols = pl.ds(pl.multiple_of(((head + 4 - k) % 4) * w, w), w)
        outs[0][:, cols] = (p * scale * gain_ref[:, cols]).astype(BF16)


def norm_parts(parts, gain):
    rows, w = parts[0].shape
    return run(norm_body, "norm_parts", [sds((rows, 4 * w), BF16)], parts[1:], [gain.reshape(1, -1), parts[0]])[0]


def from_heads(x):
    n = lax.axis_size("head")
    return [x] + [lax.ppermute(x, "head", [(i, (i + k) % n) for i in range(n)]) for k in range(1, n)]


def to_heads(xs):
    n = lax.axis_size("head")
    return [xs[0]] + [lax.ppermute(xs[k], "head", [(i, (i + k) % n) for i in range(n)]) for k in range(1, n)]


def swap_core(x):
    return lax.ppermute(x, "c", [(0, 1), (1, 0)])


def local(
    residual, queries, new_kv, kv_cache, lengths, slot_request, slot_page, slot_used, out_weight,
    norm_gain, routes, route_weights, w_gate, w_up, w_down, next_gain, next_weight,
):
    rows = queries.shape[0]
    experts = lax.axis_size(REQ)
    chips = experts // 2
    out_weight = lax.all_gather(out_weight, "head", axis=0, tiled=True)
    qa = lax.all_to_all(outset(queries, residual, routes, chips), ("z", "y"), 0, 0, tiled=True)
    w_cols = to_heads(split_columns(w_down[0]))
    tables = slot_tables(slot_request, slot_page, slot_used, lengths, kv_cache, [qa])
    keep, send, res = attend_pages(tables, qa, swap_core(qa))
    res = from_heads(res.reshape(experts, 8, -1))
    arrived = lax.all_to_all(merge(keep, swap_core(send)), ("z", "y"), 0, 0, tiled=True)
    attended, disp = owner_part(arrived, queries, new_kv, routes, experts)
    tokens = lax.all_to_all(disp, REQ, 0, 0, tiled=True)
    mine = from_heads(attended)
    tokens, res, mine, w_cols = lax.optimization_barrier((tokens, res, mine, w_cols))
    out_weight, w_gate, w_up = fetch(tokens, out_weight, w_gate[0], w_up[0])
    inner, hidden = expert_rows(from_heads(tokens), out_weight, w_gate, w_up, norm_gain, mine, res, residual)
    expert_out = down(from_heads(inner), fetch(inner, *w_cols))
    returned = lax.all_to_all(expert_out, REQ, 0, 0, tiled=True)
    stream = blend(returned, hidden, routes, route_weights)
    normed = norm_parts(from_heads(stream), next_gain)
    next_qkv = jnp.einsum("td,dcf->tcf", normed, next_weight, preferred_element_type=F32).astype(BF16)
    return stream, next_qkv


def solution(mesh):
    split = Mesh(mesh.devices.reshape(8, 4, 2, 4), ("z", "y", "c", "head"))
    placed = (
        P(REQ, None),
        P(REQ, "head"),
        P(REQ, None, "head"),
        P(REQ, None, None, "head"),
        P(),
        P(REQ),
        P(REQ),
        P(REQ),
        P("head", None),
        P(),
        P(REQ, None),
        P(REQ, None),
        P(REQ, None, "head"),
        P(REQ, None, "head"),
        P(REQ, "head", None),
        P(),
        P(None, None, "head"),
    )
    return jax.shard_map(
        local,
        mesh=split,
        in_specs=placed,
        out_specs=(P(REQ, "head"), P(REQ, None, "head")),
        check_vma=False,
    )
```

```python
import functools
import math

import jax
import jax.numpy as jnp
from jax import lax
from jax.experimental import pallas as pl
from jax.experimental.pallas import tpu as pltpu
from jax.sharding import Mesh, PartitionSpec as P

HD = 128
EPS = 1e-06
FLOOR = -(2.0**99)
SCALE = 1.0 / math.sqrt(HD)
F32 = jnp.float32
BF16 = jnp.bfloat16
REQ = ("z", "y", "c")
VLIM = pltpu.CompilerParams(vmem_limit_bytes=24 * 1024 * 1024)
VM = pl.BlockSpec(memory_space=pltpu.VMEM)


class Pending:
    def __init__(self, buf, copy):
        self.buf, self.copy, self.done = buf, copy, False

    def get(self):
        if not self.done:
            self.copy.wait()
            self.done = True
        return self.buf


class Leaving:
    def __init__(self, buf, copy):
        self.buf, self.copy, self.sent = buf, copy, False

    def send(self):
        self.copy.start()
        self.sent = True


def run(body, name, outs, near, far, scratch=(), after=(), moves=(), leaving=()):
    nn, nf, na, nm, no, nl = len(near), len(far), len(after), len(moves), len(outs), len(leaving)
    parts = 4

    def kernel(*refs):
        ins, refs = refs[: nn + nf + na + nm], refs[nn + nf + na + nm :]
        outputs, out_hbm, moved = refs[:no], refs[no : no + nl], refs[no + nl : no + nl + nm]
        rest = refs[no + nl + nm :]
        bufs, out_bufs, rest = rest[:nf], rest[nf : nf + nl], rest[nf + nl :]
        sems, move_sems, out_sems, own = rest[0], rest[1], rest[2], rest[3:]
        copies = [pltpu.make_async_copy(ins[nn + i], bufs[i], sems.at[i]) for i in range(nf)]
        for copy in copies:
            copy.start()
        pending = [Pending(b, c) for b, c in zip(bufs, copies)]
        moving = []
        for i in range(nm):
            rows = moved[i].shape[0] // parts
            for j in range(parts):
                src, dst = ins[nn + nf + na + i].at[pl.ds(j * rows, rows)], moved[i].at[pl.ds(j * rows, rows)]
                moving.append(pltpu.make_async_copy(src, dst, move_sems.at[parts * i + j]))
        for copy in moving:
            copy.start()
        going = [
            Leaving(out_bufs[i], pltpu.make_async_copy(out_bufs[i], out_hbm[i], out_sems.at[i])) for i in range(nl)
        ]
        body(ins[:nn], pending, (*outputs, *going), own)
        for p in pending:
            p.get()
        for g in going:
            if not g.sent:
                g.send()
            g.copy.wait()
        for copy in moving:
            copy.wait()

    def pin(xs):
        return [pltpu.with_memory_space_constraint(x, pltpu.HBM) for x in xs]

    hbm, any_space = pl.BlockSpec(memory_space=pltpu.HBM), pl.BlockSpec(memory_space=pl.ANY)
    return pl.pallas_call(
        kernel,
        name=name,
        out_shape=list(outs)
        + [pltpu.HBM(x.shape, x.dtype) for x in leaving]
        + [sds(x.shape, x.dtype) for x in moves],
        in_specs=[VM] * nn + [hbm] * nf + [any_space] * na + [hbm] * nm,
        out_specs=[VM] * no + [hbm] * nl + [VM] * nm,
        scratch_shapes=[pltpu.VMEM(x.shape, x.dtype) for x in (*far, *leaving)]
        + [pltpu.SemaphoreType.DMA((max(n, 1),)) for n in (nf, nm * parts, nl)]
        + list(scratch),
        compiler_params=VLIM,
    )(*near, *pin(far), *after, *pin(moves))


def sds(shape, dtype):
    return jax.ShapeDtypeStruct(shape, dtype)


def iota(shape, dim):
    return lax.broadcasted_iota(jnp.int32, shape, dim)


def core_id():
    return lax.axis_index("c")


def head_id():
    return lax.axis_index("head")


def dot(a, b):
    return jnp.dot(a, b, preferred_element_type=F32)


def hi_lo(x):
    hi = x.astype(BF16)
    return hi, (x - hi.astype(F32)).astype(BF16)


def hits(routes, expert):
    hit = jnp.zeros(expert.shape, F32)
    for k in range(routes.shape[1]):
        hit = hit + jnp.where(routes[:, k : k + 1] == expert, 1.0, 0.0)
    return hit


def cell_map(routes, expert, lane):
    hit = hits(routes, expert)
    hit = jnp.where(rank_of(hit) == (lane % 4).astype(F32), hit, 0.0)
    left = lane % 8 < 4
    return jnp.concatenate([jnp.where(left, hit, 0.0), jnp.where(left, 0.0, hit)], axis=0).astype(BF16)


def outset_body(near, far, outs, own):
    chips, _, width = outs[0].shape
    rows = far[0].buf.shape[0]
    routes = flip(far[2].get()[...], 1)
    lane = iota((rows, chips * 16), 1)
    expert = (lane // 16) * 2 + (core_id() + (lane // 8) % 2) % 2
    pick = cell_map(routes, expert.astype(F32), lane)
    first = pl.multiple_of(head_id() * 2 * width, 2 * width)
    res = far[1].get()
    both = jnp.concatenate([res[:, pl.ds(first, width)], res[:, pl.ds(first + width, width)]], axis=0)
    out = lax.dot_general(pick, both, (((0,), (0,)), ((), ())), preferred_element_type=F32)
    outs[0][:, 16:32, :] = out.astype(BF16).reshape(chips, 16, width)
    q = far[0].get()[...]
    outs[0][:, 0:16, :] = jnp.broadcast_to(q[None], (chips,) + q.shape)


def outset(queries, residual, routes, chips):
    out = sds((chips, 32, queries.shape[1]), BF16)
    return run(outset_body, "outset", [out], [], [queries, residual, routes.T])[0]


def tables_body(near, far, outs, own, page):
    pick_ref, count_ref, same_ref, mine_ref, spread_ref, spread16_ref = outs
    req = far[0].get()[...]
    slots, total = pick_ref.shape
    half = total // 2
    place = jnp.where((req // 16) % 2 == core_id(), 0, half) + (req // 32) * 16 + req % 16
    spread_ref[...] = jnp.where(iota((total, slots), 0) == place, 1.0, 0.0).astype(BF16)
    spread16_ref[...] = jnp.where(iota((total, slots), 0) // 16 == place // 16, 1.0, 0.0).astype(BF16)
    eye = iota((slots, slots), 0) == iota((slots, slots), 1)

    def to_col(row):
        return jnp.sum(jnp.where(eye, row.astype(F32), 0.0), axis=1, keepdims=True)

    req_col = to_col(req)
    same = req_col == req.astype(F32)
    same_ref[...] = jnp.where(same, 1.0, 0.0)
    slot_row = iota((slots, slots), 1).astype(F32)
    first = jnp.min(jnp.where(same, slot_row, 9999.0), axis=1, keepdims=True)
    leader = first == iota((slots, 1), 0).astype(F32)
    mine = (iota((slots, HD), 1) % 16).astype(F32) == to_col(req % 16)
    mine_ref[...] = jnp.where(mine & leader, 1.0, 0.0)
    lane_total = iota((slots, total), 1).astype(F32)
    pick_ref[...] = jnp.where(to_col(place) == lane_total, 1.0, 0.0).astype(BF16)
    lengths = far[3].get()[...].astype(F32)
    len_col = jnp.sum(jnp.where(req_col == lane_total, lengths, 0.0), axis=1, keepdims=True)
    count = jnp.clip(len_col - to_col(far[1].get()[...]) * page, 0.0, float(page))
    count = jnp.where(to_col(far[2].get()[...]) == 1.0, count, 0.0)
    count_ref[...] = jnp.broadcast_to(count, (slots, HD))


def slot_tables(slot_request, slot_page, slot_used, lengths, kv_cache, after):
    slots = kv_cache.shape[0]
    total = lengths.shape[0]
    return run(
        functools.partial(tables_body, page=kv_cache.shape[2]),
        "slot_tables",
        [
            sds((slots, total), BF16),
            sds((slots, HD), F32),
            sds((slots, slots), F32),
            sds((slots, HD), F32),
            sds((total, slots), BF16),
            sds((total, slots), BF16),
        ],
        [],
        [slot_request.reshape(1, slots), slot_page.reshape(1, slots), slot_used.reshape(1, slots), lengths.reshape(1, total)],
        after=after,
        moves=[kv_cache],
    )


def attn_body(near, far, outs, own):
    pick_ref, count_ref, same_ref, mine_ref, spread_ref, spread16_ref, kv_ref, qa_ref, qb_ref = near
    keep_ref, send_ref, res = outs
    n_scr, m_scr, l_scr = own
    core = core_id()
    res.buf[:, core] = qa_ref[:, 16:24, :]
    res.buf[:, 1 - core] = qb_ref[:, 24:32, :]
    res.send()
    slots = kv_ref.shape[0]
    page = kv_ref.shape[2]
    half = qa_ref.shape[0] * 16
    qa, qb = (r[:, 0:16, :].reshape(half, 2 * HD) for r in (qa_ref, qb_ref))
    chosen = dot(pick_ref[:, :half], qa) + dot(pick_ref[:, half:], qb)
    low_lanes = iota((8, 2 * HD), 1) < HD
    rel = iota((16, 8 * page), 1) - (iota((16, 8 * page), 0) % 8) * page
    rel = rel.astype(F32)
    for b in range(slots // 8):
        q8 = chosen[b * 8 : b * 8 + 8]
        q16 = jnp.concatenate([jnp.where(low_lanes, q8, 0.0), jnp.where(low_lanes, 0.0, q8)], axis=0).astype(BF16)
        keys = kv_ref[b * 8 : b * 8 + 8, 0].reshape(8 * page, 2 * HD)
        vals = kv_ref[b * 8 : b * 8 + 8, 1].reshape(8 * page, 2 * HD)
        s = lax.dot_general(q16, keys, (((1,), (1,)), ((), ())), preferred_element_type=F32) * SCALE
        c8 = count_ref[b * 8 : b * 8 + 8, :1]
        ok = (rel >= 0.0) & (rel < jnp.concatenate([c8, c8], axis=0))
        s = jnp.where(ok, s, FLOOR)
        m = jnp.max(s, axis=1, keepdims=True)
        w = jnp.where(ok, jnp.exp(s - m), 0.0).astype(BF16)
        l = jnp.sum(w.astype(F32), axis=1, keepdims=True)
        n = dot(w, vals)
        for h in range(2):
            n_scr[h, b * 8 : b * 8 + 8, :] = n[8 * h : 8 * h + 8, HD * h : HD * h + HD]
            m_scr[h, b * 8 : b * 8 + 8, :] = jnp.broadcast_to(m[8 * h : 8 * h + 8], (8, slots))
            l_scr[h, b * 8 : b * 8 + 8, :] = jnp.broadcast_to(l[8 * h : 8 * h + 8], (8, slots))

    eye = iota((slots, slots), 0) == iota((slots, slots), 1)
    same = same_ref[...] > 0.0

    def to_row(wide):
        return jnp.sum(jnp.where(eye, wide, 0.0), axis=0, keepdims=True)

    group = iota((slots, HD), 1) // 16
    board = jnp.zeros((slots, HD), F32)
    for h in range(2):
        m_wide = m_scr[h]
        m_ref = jnp.max(jnp.where(same, to_row(m_wide), FLOOR), axis=1, keepdims=True)
        m_ref = m_ref.astype(BF16).astype(F32)
        lift = jnp.exp(m_wide - m_ref)
        n_hi, n_lo = hi_lo(n_scr[h] * lift)
        l_sum = jnp.sum(jnp.where(same, to_row(l_scr[h] * lift), 0.0), axis=1, keepdims=True)
        out = (dot(spread_ref[...], n_hi) + dot(spread_ref[...], n_lo)).astype(BF16)
        keep_ref[:, 16 * h : 16 * h + 16, :] = out[:half].reshape(half // 16, 16, HD)
        send_ref[:, 16 * h : 16 * h + 16, :] = out[half:].reshape(half // 16, 16, HD)
        l_hi = l_sum.astype(BF16).astype(F32)
        for i, stat in enumerate((m_ref, l_hi, l_sum - l_hi)):
            board = jnp.where(group == 2 * i + h, stat, board)
    board = jnp.where(mine_ref[...] > 0.0, board, 0.0).astype(BF16)
    out = dot(spread16_ref[...], board).astype(BF16)
    keep_ref[:, 32:48, :] = out[:half].reshape(half // 16, 16, HD)
    send_ref[:, 32:48, :] = out[half:].reshape(half // 16, 16, HD)


def attend_pages(tables, qa, qb):
    slots, total = tables[0].shape
    scratch = [pltpu.VMEM((2, slots, n), F32) for n in (HD, slots, slots)]
    outs = [sds((total // 32, 48, HD), BF16)] * 2
    leaving = [sds((total // 32, 2, 8, 2 * HD), BF16)]
    return run(attn_body, "attend_pages", outs, [*tables, qa, qb], [], scratch, leaving=leaving)


def merge_body(near, far, outs, own):
    (a_ref, b_ref), out_ref = near, outs[0].buf
    a, b = a_ref[:, 32:48, :].astype(F32), b_ref[:, 32:48, :].astype(F32)
    lane, row = iota(a.shape, 2), iota(a.shape, 1)
    board = jnp.zeros(a.shape, F32)
    for h in range(2):
        (ma, la), (mb, lb) = read_stats(a, h), read_stats(b, h)
        m = jnp.maximum(ma, mb)
        fa, fb = jnp.exp(ma - m), jnp.exp(mb - m)
        rows = slice(16 * h, 16 * h + 16)
        out_ref[:, rows, :] = (a_ref[:, rows, :].astype(F32) * fa + b_ref[:, rows, :].astype(F32) * fb).astype(BF16)
        l = la * fa + lb * fb
        l_hi = l.astype(BF16).astype(F32)
        for i, stat in enumerate((m, l_hi, l - l_hi)):
            board = jnp.where(lane == row + 32 * i + 16 * h, stat, board)
    out_ref[:, 32:48, :] = board.astype(BF16)


def merge(a, b):
    return run(merge_body, "merge", [], [a, b], [], leaving=[sds(a.shape, BF16)])[0]


def fetch(after, *arrays):
    return run(lambda *_: None, "fetch", [], [], [], after=[after], moves=arrays)


def column_kernel(w_ref, after_ref, out_ref, sem):
    width = out_ref.shape[1]
    cols = pl.ds(pl.multiple_of(head_id() * width, width), width)
    copy = pltpu.make_async_copy(w_ref.at[:, cols], out_ref, sem)
    copy.start()
    copy.wait()


def fetch_columns(after, w):
    return pl.pallas_call(
        column_kernel,
        name="fetch_columns",
        out_shape=sds((w.shape[0], w.shape[1] // 4), w.dtype),
        in_specs=[pl.BlockSpec(memory_space=pltpu.HBM), pl.BlockSpec(memory_space=pl.ANY)],
        out_specs=VM,
        scratch_shapes=[pltpu.SemaphoreType.DMA],
        compiler_params=VLIM,
    )(pltpu.with_memory_space_constraint(w, pltpu.HBM), after)


def cells_body(near, far, outs, own):
    rows = outs[0].shape[0] // 2
    lane = iota((rows, outs[0].shape[1]), 1)
    outs[0][...] = cell_map(flip(far[0].get()[...], 1), (lane // 8).astype(F32), lane)


def cells_table(routes, experts, after):
    out = sds((2 * routes.shape[0], experts * 8), BF16)
    return run(cells_body, "cells_table", [out], [], [routes.T], after=[after])[0]


def mix_body(near, far, outs, own):
    routes, share = flip(far[0].get()[...], 1), flip(far[1].get()[...], 3)
    rows, cells = outs[0].shape
    lane = iota((rows, cells), 1)
    expert = (lane // 4).astype(F32)
    mix = jnp.zeros((rows, cells), F32)
    for k in range(routes.shape[1]):
        mix = mix + jnp.where(routes[:, k : k + 1] == expert, share[:, k : k + 1], 0.0)
    mix = jnp.where(rank_of(hits(routes, expert)) == (lane % 4).astype(F32), mix, 0.0)
    outs[0][...], outs[1][...] = hi_lo(mix)


def mix_table(routes, route_weights, experts, after):
    out = sds((routes.shape[0], experts * 4), BF16)
    return run(mix_body, "mix_table", [out, out], [], [routes.T, route_weights.T], after=[after])


def read_stats(board, h):
    lane, row = iota(board.shape, 2), iota(board.shape, 1) + 16 * h
    m = jnp.sum(jnp.where(lane == row, board, 0.0), axis=2, keepdims=True)
    l = jnp.sum(jnp.where((lane == row + 32) | (lane == row + 64), board, 0.0), axis=2, keepdims=True)
    return jnp.where(l > 0.0, m, FLOOR), l


def owner_body(near, far, outs, own_scratch):
    part_ref = near[0]
    board = part_ref[:, 32:48, :].astype(F32)
    q = far[0].get()[...].astype(F32)
    nkv = far[1].get()[...].astype(F32)
    nkv = jnp.concatenate([nkv[:, 0, :], nkv[:, 1, :]], axis=1)
    att = []
    for h in range(2):
        m, l = read_stats(board, h)
        own = jnp.sum(q[:, HD * h : HD * h + HD] * nkv[:, HD * h : HD * h + HD], axis=1, keepdims=True) * SCALE
        top = jnp.maximum(jnp.max(m, axis=0), own)
        lift = jnp.exp(m - top[None])
        n = jnp.sum(part_ref[:, 16 * h : 16 * h + 16, :].astype(F32) * lift, axis=0)
        den = jnp.sum(l * lift, axis=0)
        new = jnp.exp(own - top)
        v = nkv[:, 2 * HD + HD * h : 2 * HD + HD * h + HD]
        att.append((n + new * v) / (den + new))
    att_ref, disp_ref = outs
    att_ref[...] = jnp.concatenate(att, axis=1).astype(BF16)
    both = jnp.concatenate(att, axis=0).astype(BF16)
    out = lax.dot_general(far[2].get()[...], both, (((0,), (0,)), ((), ())), preferred_element_type=F32)
    disp_ref[...] = out.astype(BF16).reshape(disp_ref.shape)


def owner_part(parts, queries, new_kv, cells, experts):
    outs = [sds(queries.shape, BF16), sds((experts, 8, HD), BF16)]
    return run(owner_body, "owner_part", outs, [parts], [queries, new_kv, cells])


def flip(x, terms):
    n = x.shape[1]
    eye = jnp.where(iota((n, n), 0) == iota((n, n), 1), 1.0, 0.0).astype(BF16)
    x = x.astype(F32)
    out = jnp.zeros((n, x.shape[0]), F32)
    for _ in range(terms):
        part = x.astype(BF16)
        out = out + lax.dot_general(eye, part, (((1,), (1,)), ((), ())), preferred_element_type=F32)
        x = x - part.astype(F32)
    return out


def rank_of(hit):
    rows = hit.shape[0]
    before = jnp.where(iota((rows, rows), 0) > iota((rows, rows), 1), 1.0, 0.0).astype(BF16)
    return dot(before, hit.astype(BF16))


def unfold(x):
    n, _, w = x.shape
    x = x.reshape(n // 2, 2, 8, w)
    a, b = x[:, 0], x[:, 1]
    top = iota(a.shape, 1) < 4
    left = jnp.where(top, a, pltpu.roll(b, 4, 1))
    right = jnp.where(top, pltpu.roll(a, 4, 1), b)
    return left.reshape(n * 4, w), right.reshape(n * 4, w)


def fold(left, right):
    rows, w = left.shape
    left, right = left.reshape(rows // 8, 8, w), right.reshape(rows // 8, 8, w)
    top = iota(left.shape, 1) < 4
    a = jnp.where(top, left, pltpu.roll(right, 4, 1))
    b = jnp.where(top, pltpu.roll(left, 4, 1), right)
    return a, b


def head_blocks(size):
    return [pl.multiple_of(((head_id() + 4 - k) % 4) * size, size) for k in range(4)]


def early_body(near, far, outs, own):
    tok_ref, wo_ref = near
    xs = outs[0]
    eff, w = 2 * HD, xs.shape[2]
    att = jnp.concatenate(unfold(tok_ref[...].astype(F32)), axis=1).astype(BF16)
    rows = pl.ds(head_blocks(eff)[0], eff)
    for k, first in enumerate(head_blocks(2 * w)):
        pair = unfold(far[k].get()[...].astype(F32))
        for f in range(2):
            xs[2 * k + f] = pair[f] + dot(att, wo_ref[rows, pl.ds(first + f * w, w)])


def early_rows(tokens, out_weight, res):
    n = tokens.shape[0]
    w = res[0].shape[2]
    return run(early_body, "early_rows", [sds((8, n * 4, w), F32)], [tokens, out_weight], res)[0]


def expert_body(near, far, outs, own):
    inner_ref, hid = outs
    hs = own[0]
    att, (xs, wo_ref, wg_ref, wu_ref) = near[:3], near[3:]
    gain, mine, own_res = far[0], far[1:5], far[5]
    n = inner_ref.shape[0]
    eff = 2 * HD
    w = xs.shape[2]
    att = [jnp.concatenate(unfold(a[...].astype(F32)), axis=1).astype(BF16) for a in att]
    block = head_blocks(eff)
    firsts = [first + f * w for first in head_blocks(2 * w) for f in range(2)]
    cols = pl.ds(head_blocks(2 * w)[0], 2 * w)
    acc = own_res.get()[:, cols].astype(F32)
    acc = acc + sum(dot(mine[i].get()[...], wo_ref[pl.ds(block[i], eff), cols]) for i in range(4))
    hid.buf[...] = acc.astype(BF16)
    hid.send()
    total = jnp.zeros((n, 1), F32)
    for j, first in enumerate(firsts):
        acc = xs[j]
        for i in range(3):
            acc = acc + dot(att[i], wo_ref[pl.ds(block[i + 1], eff), pl.ds(first, w)])
        part = acc.astype(BF16)
        hs[j] = part
        part = part.astype(F32)
        total = total + jnp.sum(part * part, axis=1, keepdims=True)
    scale = lax.rsqrt(total / (8 * w) + EPS)
    gain_ref = gain.get()
    gate = jnp.zeros((n, wg_ref.shape[1]), F32)
    up = jnp.zeros((n, wg_ref.shape[1]), F32)
    for j, first in enumerate(firsts):
        normed = (hs[j].astype(F32) * scale * gain_ref[:, pl.ds(first, w)]).astype(BF16)
        gate = gate + dot(normed, wg_ref[pl.ds(first, w), :])
        up = up + dot(normed, wu_ref[pl.ds(first, w), :])
    inner_ref[...] = (gate / (1.0 + jnp.exp(-gate)) * up).astype(BF16)


def expert_rows(tokens, early, out_weight, w_gate, w_up, gain, mine, residual):
    _, n, w = early.shape
    outs, leaving = [sds((n, w_gate.shape[1]), BF16)], [sds((residual.shape[0], 2 * w), BF16)]
    near = [*tokens, early, out_weight, w_gate, w_up]
    scratch = [pltpu.VMEM((8, n, w), BF16)]
    far = [gain.reshape(1, -1), *mine, residual]
    return run(expert_body, "expert_rows", outs, near, far, scratch, leaving=leaving)


def down_body(near, far, outs, own):
    w_ref, out_ref = near[4], outs[0]
    block = head_blocks(near[0].shape[1])
    acc = sum(dot(near[k][...], w_ref[pl.ds(block[k], near[k].shape[1]), :]) for k in range(4))
    width = acc.shape[1]
    a, b = fold(acc[:, : width // 2], acc[:, width // 2 :])
    out_ref[:, 0] = a.astype(BF16)
    out_ref[:, 1] = b.astype(BF16)


def down(inners, w_cols, after):
    rows = inners[0].shape[0]
    width = w_cols.shape[1]
    out = run(down_body, "down", [sds((rows // 8, 2, 8, width // 2), BF16)], [*inners, w_cols], [], after=[after])[0]
    return out.reshape(rows // 4, 8, width // 2)


def blend_body(near, far, outs, own):
    y_ref, hi_ref, low_ref = near
    w = y_ref.shape[2]
    hid_ref = far[0].get()
    for f, part in enumerate(unfold(y_ref[...].astype(F32))):
        part = part.astype(BF16)
        hid = hid_ref[:, f * w : f * w + w].astype(F32)
        moe = dot(hi_ref[...], part) + dot(low_ref[...], part)
        outs[0][:, f * w : f * w + w] = (hid + moe).astype(BF16)


def blend(returned, mix, hidden):
    return run(blend_body, "blend", [sds(hidden.shape, BF16)], [returned, *mix], [hidden])[0]


def norm_body(near, far, outs, own):
    head = head_id()
    w = near[0].shape[1]
    parts = [s[...].astype(F32) for s in (far[1].get(), *near)]
    total = sum(jnp.sum(p * p, axis=1, keepdims=True) for p in parts)
    scale = lax.rsqrt(total / (4 * w) + EPS)
    gain_ref = far[0].get()
    for k, p in enumerate(parts):
        cols = pl.ds(pl.multiple_of(((head + 4 - k) % 4) * w, w), w)
        outs[0][:, cols] = (p * scale * gain_ref[:, cols]).astype(BF16)


def norm_parts(parts, gain):
    rows, w = parts[0].shape
    return run(norm_body, "norm_parts", [sds((rows, 4 * w), BF16)], parts[1:], [gain.reshape(1, -1), parts[0]])[0]


def from_heads(x):
    n = lax.axis_size("head")
    return [x] + [lax.ppermute(x, "head", [(i, (i + k) % n) for i in range(n)]) for k in range(1, n)]


def to_heads(xs):
    n = lax.axis_size("head")
    return [xs[0]] + [lax.ppermute(xs[k], "head", [(i, (i + k) % n) for i in range(n)]) for k in range(1, n)]


def swap_core(x):
    return lax.ppermute(x, "c", [(0, 1), (1, 0)])


def local(
    residual, queries, new_kv, kv_cache, lengths, slot_request, slot_page, slot_used, out_weight,
    norm_gain, routes, route_weights, w_gate, w_up, w_down, next_gain, next_weight,
):
    rows = queries.shape[0]
    experts = lax.axis_size(REQ)
    chips = experts // 2
    out_weight = lax.all_gather(out_weight, "head", axis=0, tiled=True)
    w_down_all = lax.all_gather(w_down[0], "head", axis=0, tiled=True)
    qa = lax.all_to_all(outset(queries, residual, routes, chips), ("z", "y"), 0, 0, tiled=True)
    tables = slot_tables(slot_request, slot_page, slot_used, lengths, kv_cache, [qa])
    keep, send, res = attend_pages(tables, qa, swap_core(qa))
    merged = merge(keep, swap_core(send))
    cells = cells_table(routes, experts, merged)
    res = from_heads(res.reshape(experts, 8, -1))
    arrived = lax.all_to_all(merged, ("z", "y"), 0, 0, tiled=True)
    arrived, res, cells = lax.optimization_barrier((arrived, res, cells))
    attended, disp = owner_part(arrived, queries, new_kv, cells, experts)
    tokens = lax.all_to_all(disp, REQ, 0, 0, tiled=True)
    tokens, attended = lax.optimization_barrier((tokens, attended))
    out_weight, w_gate, w_up = fetch(tokens, out_weight, w_gate[0], w_up[0])
    early = early_rows(tokens, out_weight, res)
    others, mine = from_heads(tokens)[1:], from_heads(attended)
    inner, hidden = expert_rows(others, early, out_weight, w_gate, w_up, norm_gain, mine, residual)
    w_cols = fetch_columns(inner, w_down_all)
    mix = mix_table(routes, route_weights, experts, inner)
    expert_out = down(from_heads(inner), w_cols, mix[0])
    returned = lax.all_to_all(expert_out, REQ, 0, 0, tiled=True)
    stream = blend(returned, mix, hidden)
    normed = norm_parts(from_heads(stream), next_gain)
    next_qkv = jnp.einsum("td,dcf->tcf", normed, next_weight, preferred_element_type=F32).astype(BF16)
    return stream, next_qkv


def solution(mesh):
    split = Mesh(mesh.devices.reshape(8, 4, 2, 4), ("z", "y", "c", "head"))
    placed = (
        P(REQ, None),
        P(REQ, "head"),
        P(REQ, None, "head"),
        P(REQ, None, None, "head"),
        P(),
        P(REQ),
        P(REQ),
        P(REQ),
        P("head", None),
        P(),
        P(REQ, None),
        P(REQ, None),
        P(REQ, None, "head"),
        P(REQ, None, "head"),
        P(REQ, "head", None),
        P(),
        P(None, None, "head"),
    )
    return jax.shard_map(
        local,
        mesh=split,
        in_specs=placed,
        out_specs=(P(REQ, "head"), P(REQ, None, "head")),
        check_vma=False,
    )
```

```python
import functools
import math

import jax
import jax.numpy as jnp
from jax import lax
from jax.experimental import pallas as pl
from jax.experimental.pallas import tpu as pltpu
from jax.sharding import Mesh, PartitionSpec as P

HD = 128
EPS = 1e-06
FLOOR = -(2.0**99)
SCALE = 1.0 / math.sqrt(HD)
F32 = jnp.float32
BF16 = jnp.bfloat16
REQ = ("z", "y", "c")
VLIM = pltpu.CompilerParams(vmem_limit_bytes=24 * 1024 * 1024)
VM = pl.BlockSpec(memory_space=pltpu.VMEM)


class Pending:
    def __init__(self, buf, copy):
        self.buf, self.copy, self.done = buf, copy, False

    def get(self):
        if not self.done:
            self.copy.wait()
            self.done = True
        return self.buf


def pin(xs):
    return [pltpu.with_memory_space_constraint(x, pltpu.HBM) for x in xs]


class Leaving:
    def __init__(self, buf, copy):
        self.buf, self.copy, self.sent = buf, copy, False

    def send(self):
        self.copy.start()
        self.sent = True


def run(body, name, outs, near, far, scratch=(), after=(), moves=(), leaving=(), after_hbm=()):
    nn, nf, nm, no, nl = len(near), len(far), len(moves), len(outs), len(leaving)
    after = [*after, *pin(after_hbm)]
    na = len(after)
    nh = len(after_hbm)
    parts = 4

    def kernel(*refs):
        ins, refs = refs[: nn + nf + na + nm], refs[nn + nf + na + nm :]
        outputs, out_hbm, moved = refs[:no], refs[no : no + nl], refs[no + nl : no + nl + nm]
        rest = refs[no + nl + nm :]
        bufs, out_bufs, rest = rest[:nf], rest[nf : nf + nl], rest[nf + nl :]
        sems, move_sems, out_sems, own = rest[0], rest[1], rest[2], rest[3:]
        copies = [pltpu.make_async_copy(ins[nn + i], bufs[i], sems.at[i]) for i in range(nf)]
        for copy in copies:
            copy.start()
        pending = [Pending(b, c) for b, c in zip(bufs, copies)]
        moving = []
        for i in range(nm):
            rows = moved[i].shape[0] // parts
            for j in range(parts):
                src, dst = ins[nn + nf + na + i].at[pl.ds(j * rows, rows)], moved[i].at[pl.ds(j * rows, rows)]
                moving.append(pltpu.make_async_copy(src, dst, move_sems.at[parts * i + j]))
        for copy in moving:
            copy.start()
        going = [
            Leaving(out_bufs[i], pltpu.make_async_copy(out_bufs[i], out_hbm[i], out_sems.at[i])) for i in range(nl)
        ]
        body(ins[:nn], pending, (*outputs, *going), own)
        for p in pending:
            p.get()
        for g in going:
            if not g.sent:
                g.send()
            g.copy.wait()
        for copy in moving:
            copy.wait()

    hbm, any_space = pl.BlockSpec(memory_space=pltpu.HBM), pl.BlockSpec(memory_space=pl.ANY)
    return pl.pallas_call(
        kernel,
        name=name,
        out_shape=list(outs)
        + [pltpu.HBM(x.shape, x.dtype) for x in leaving]
        + [sds(x.shape, x.dtype) for x in moves],
        in_specs=[VM] * nn + [hbm] * nf + [any_space] * (na - nh) + [hbm] * (nh + nm),
        out_specs=[VM] * no + [hbm] * nl + [VM] * nm,
        scratch_shapes=[pltpu.VMEM(x.shape, x.dtype) for x in (*far, *leaving)]
        + [pltpu.SemaphoreType.DMA((max(n, 1),)) for n in (nf, nm * parts, nl)]
        + list(scratch),
        compiler_params=VLIM,
    )(*near, *pin(far), *after, *pin(moves))


def sds(shape, dtype):
    return jax.ShapeDtypeStruct(shape, dtype)


def iota(shape, dim):
    return lax.broadcasted_iota(jnp.int32, shape, dim)


def core_id():
    return lax.axis_index("c")


def head_id():
    return lax.axis_index("head")


def dot(a, b):
    return jnp.dot(a, b, preferred_element_type=F32)


def hi_lo(x):
    hi = x.astype(BF16)
    return hi, (x - hi.astype(F32)).astype(BF16)


def hits(routes, expert):
    hit = jnp.zeros(expert.shape, F32)
    for k in range(routes.shape[1]):
        hit = hit + jnp.where(routes[:, k : k + 1] == expert, 1.0, 0.0)
    return hit


def cell_map(routes, expert, lane):
    hit = hits(routes, expert)
    hit = jnp.where(rank_of(hit) == (lane % 4).astype(F32), hit, 0.0)
    left = lane % 8 < 4
    return jnp.concatenate([jnp.where(left, hit, 0.0), jnp.where(left, 0.0, hit)], axis=0).astype(BF16)


def outset_body(near, far, outs, own):
    chips, _, width = outs[0].shape
    rows = far[0].buf.shape[0]
    routes = flip(far[2].get()[...], 1)
    lane = iota((rows, chips * 16), 1)
    expert = (lane // 16) * 2 + (core_id() + (lane // 8) % 2) % 2
    pick = cell_map(routes, expert.astype(F32), lane)
    first = pl.multiple_of(head_id() * 2 * width, 2 * width)
    res = far[1].get()
    both = jnp.concatenate([res[:, pl.ds(first, width)], res[:, pl.ds(first + width, width)]], axis=0)
    out = lax.dot_general(pick, both, (((0,), (0,)), ((), ())), preferred_element_type=F32)
    outs[0][:, 16:32, :] = out.astype(BF16).reshape(chips, 16, width)
    q = far[0].get()[...]
    outs[0][:, 0:16, :] = jnp.broadcast_to(q[None], (chips,) + q.shape)


def outset(queries, residual, routes, chips):
    out = sds((chips, 32, queries.shape[1]), BF16)
    return run(outset_body, "outset", [out], [], [queries, residual, routes.T])[0]


def tables_body(near, far, outs, own, page):
    pick_ref, count_ref, same_ref, mine_ref, spread_ref, spread16_ref = outs
    req = far[0].get()[...]
    slots, total = pick_ref.shape
    half = total // 2
    place = jnp.where((req // 16) % 2 == core_id(), 0, half) + (req // 32) * 16 + req % 16
    spread_ref[...] = jnp.where(iota((total, slots), 0) == place, 1.0, 0.0).astype(BF16)
    spread16_ref[...] = jnp.where(iota((total, slots), 0) // 16 == place // 16, 1.0, 0.0).astype(BF16)
    eye = iota((slots, slots), 0) == iota((slots, slots), 1)

    def to_col(row):
        return jnp.sum(jnp.where(eye, row.astype(F32), 0.0), axis=1, keepdims=True)

    req_col = to_col(req)
    same = req_col == req.astype(F32)
    same_ref[...] = jnp.where(same, 1.0, 0.0)
    slot_row = iota((slots, slots), 1).astype(F32)
    first = jnp.min(jnp.where(same, slot_row, 9999.0), axis=1, keepdims=True)
    leader = first == iota((slots, 1), 0).astype(F32)
    mine = (iota((slots, HD), 1) % 16).astype(F32) == to_col(req % 16)
    mine_ref[...] = jnp.where(mine & leader, 1.0, 0.0)
    lane_total = iota((slots, total), 1).astype(F32)
    pick_ref[...] = jnp.where(to_col(place) == lane_total, 1.0, 0.0).astype(BF16)
    lengths = far[3].get()[...].astype(F32)
    len_col = jnp.sum(jnp.where(req_col == lane_total, lengths, 0.0), axis=1, keepdims=True)
    count = jnp.clip(len_col - to_col(far[1].get()[...]) * page, 0.0, float(page))
    count = jnp.where(to_col(far[2].get()[...]) == 1.0, count, 0.0)
    count_ref[...] = jnp.broadcast_to(count, (slots, HD))


def slot_tables(slot_request, slot_page, slot_used, lengths, kv_cache, after):
    slots = kv_cache.shape[0]
    total = lengths.shape[0]
    return run(
        functools.partial(tables_body, page=kv_cache.shape[2]),
        "slot_tables",
        [
            sds((slots, total), BF16),
            sds((slots, HD), F32),
            sds((slots, slots), F32),
            sds((slots, HD), F32),
            sds((total, slots), BF16),
            sds((total, slots), BF16),
        ],
        [],
        [slot_request.reshape(1, slots), slot_page.reshape(1, slots), slot_used.reshape(1, slots), lengths.reshape(1, total)],
        after=after,
        moves=[kv_cache],
    )


def attn_body(near, far, outs, own):
    pick_ref, count_ref, same_ref, mine_ref, spread_ref, spread16_ref, kv_ref, qa_ref, qb_ref = near
    keep_ref, send_ref, res = outs
    n_scr, m_scr, l_scr = own
    core = core_id()
    res.buf[:, core] = qa_ref[:, 16:24, :]
    res.buf[:, 1 - core] = qb_ref[:, 24:32, :]
    res.send()
    slots = kv_ref.shape[0]
    page = kv_ref.shape[2]
    half = qa_ref.shape[0] * 16
    qa, qb = (r[:, 0:16, :].reshape(half, 2 * HD) for r in (qa_ref, qb_ref))
    chosen = dot(pick_ref[:, :half], qa) + dot(pick_ref[:, half:], qb)
    low_lanes = iota((8, 2 * HD), 1) < HD
    rel = iota((16, 8 * page), 1) - (iota((16, 8 * page), 0) % 8) * page
    rel = rel.astype(F32)
    for b in range(slots // 8):
        q8 = chosen[b * 8 : b * 8 + 8]
        q16 = jnp.concatenate([jnp.where(low_lanes, q8, 0.0), jnp.where(low_lanes, 0.0, q8)], axis=0).astype(BF16)
        keys = kv_ref[b * 8 : b * 8 + 8, 0].reshape(8 * page, 2 * HD)
        vals = kv_ref[b * 8 : b * 8 + 8, 1].reshape(8 * page, 2 * HD)
        s = lax.dot_general(q16, keys, (((1,), (1,)), ((), ())), preferred_element_type=F32) * SCALE
        c8 = count_ref[b * 8 : b * 8 + 8, :1]
        ok = (rel >= 0.0) & (rel < jnp.concatenate([c8, c8], axis=0))
        s = jnp.where(ok, s, FLOOR)
        m = jnp.max(s, axis=1, keepdims=True)
        w = jnp.where(ok, jnp.exp(s - m), 0.0).astype(BF16)
        l = jnp.sum(w.astype(F32), axis=1, keepdims=True)
        n = dot(w, vals)
        for h in range(2):
            n_scr[h, b * 8 : b * 8 + 8, :] = n[8 * h : 8 * h + 8, HD * h : HD * h + HD]
            m_scr[h, b * 8 : b * 8 + 8, :] = jnp.broadcast_to(m[8 * h : 8 * h + 8], (8, slots))
            l_scr[h, b * 8 : b * 8 + 8, :] = jnp.broadcast_to(l[8 * h : 8 * h + 8], (8, slots))

    eye = iota((slots, slots), 0) == iota((slots, slots), 1)
    same = same_ref[...] > 0.0

    def to_row(wide):
        return jnp.sum(jnp.where(eye, wide, 0.0), axis=0, keepdims=True)

    group = iota((slots, HD), 1) // 16
    board = jnp.zeros((slots, HD), F32)
    for h in range(2):
        m_wide = m_scr[h]
        m_ref = jnp.max(jnp.where(same, to_row(m_wide), FLOOR), axis=1, keepdims=True)
        m_ref = m_ref.astype(BF16).astype(F32)
        lift = jnp.exp(m_wide - m_ref)
        n_hi, n_lo = hi_lo(n_scr[h] * lift)
        l_sum = jnp.sum(jnp.where(same, to_row(l_scr[h] * lift), 0.0), axis=1, keepdims=True)
        out = (dot(spread_ref[...], n_hi) + dot(spread_ref[...], n_lo)).astype(BF16)
        keep_ref[:, 16 * h : 16 * h + 16, :] = out[:half].reshape(half // 16, 16, HD)
        send_ref[:, 16 * h : 16 * h + 16, :] = out[half:].reshape(half // 16, 16, HD)
        l_hi = l_sum.astype(BF16).astype(F32)
        for i, stat in enumerate((m_ref, l_hi, l_sum - l_hi)):
            board = jnp.where(group == 2 * i + h, stat, board)
    board = jnp.where(mine_ref[...] > 0.0, board, 0.0).astype(BF16)
    out = dot(spread16_ref[...], board).astype(BF16)
    keep_ref[:, 32:48, :] = out[:half].reshape(half // 16, 16, HD)
    send_ref[:, 32:48, :] = out[half:].reshape(half // 16, 16, HD)


def attend_pages(tables, qa, qb):
    slots, total = tables[0].shape
    scratch = [pltpu.VMEM((2, slots, n), F32) for n in (HD, slots, slots)]
    outs = [sds((total // 32, 48, HD), BF16)] * 2
    leaving = [sds((total // 32, 2, 8, 2 * HD), BF16)]
    return run(attn_body, "attend_pages", outs, [*tables, qa, qb], [], scratch, leaving=leaving)


def merge_body(near, far, outs, own):
    (a_ref, b_ref), out_ref = near, outs[0].buf
    a, b = a_ref[:, 32:48, :].astype(F32), b_ref[:, 32:48, :].astype(F32)
    lane, row = iota(a.shape, 2), iota(a.shape, 1)
    board = jnp.zeros(a.shape, F32)
    for h in range(2):
        (ma, la), (mb, lb) = read_stats(a, h), read_stats(b, h)
        m = jnp.maximum(ma, mb)
        fa, fb = jnp.exp(ma - m), jnp.exp(mb - m)
        rows = slice(16 * h, 16 * h + 16)
        out_ref[:, rows, :] = (a_ref[:, rows, :].astype(F32) * fa + b_ref[:, rows, :].astype(F32) * fb).astype(BF16)
        l = la * fa + lb * fb
        l_hi = l.astype(BF16).astype(F32)
        for i, stat in enumerate((m, l_hi, l - l_hi)):
            board = jnp.where(lane == row + 32 * i + 16 * h, stat, board)
    out_ref[:, 32:48, :] = board.astype(BF16)


def merge(a, b):
    return run(merge_body, "merge", [], [a, b], [], leaving=[sds(a.shape, BF16)])[0]


def fetch(after, *arrays):
    return run(lambda *_: None, "fetch", [], [], [], after=[after], moves=arrays)


def split_kernel(w_ref, after_ref, *refs):
    outs, sems = refs[:4], refs[4]
    width = outs[0].shape[1]
    copies = []
    for k in range(4):
        cols = pl.ds(pl.multiple_of(((head_id() + k) % 4) * width, width), width)
        copies.append(pltpu.make_async_copy(w_ref.at[:, cols], outs[k], sems.at[k]))
    for copy in copies:
        copy.start()
    for copy in copies:
        copy.wait()


def split_columns(w, after):
    hbm = pl.BlockSpec(memory_space=pltpu.HBM)
    return pl.pallas_call(
        split_kernel,
        name="split_columns",
        out_shape=[pltpu.HBM((w.shape[0], w.shape[1] // 4), w.dtype)] * 4,
        in_specs=[hbm] * 2,
        out_specs=[hbm] * 4,
        scratch_shapes=[pltpu.SemaphoreType.DMA((4,))],
        compiler_params=VLIM,
    )(*pin([w, after]))


def cells_body(near, far, outs, own):
    rows = outs[0].shape[0] // 2
    lane = iota((rows, outs[0].shape[1]), 1)
    outs[0][...] = cell_map(flip(far[0].get()[...], 1), (lane // 8).astype(F32), lane)


def cells_table(routes, experts, after):
    out = sds((2 * routes.shape[0], experts * 8), BF16)
    return run(cells_body, "cells_table", [out], [], [routes.T], after_hbm=[after])[0]


def mix_body(near, far, outs, own):
    routes, share = flip(far[0].get()[...], 1), flip(far[1].get()[...], 3)
    rows, cells = outs[0].shape
    lane = iota((rows, cells), 1)
    expert = (lane // 4).astype(F32)
    mix = jnp.zeros((rows, cells), F32)
    for k in range(routes.shape[1]):
        mix = mix + jnp.where(routes[:, k : k + 1] == expert, share[:, k : k + 1], 0.0)
    mix = jnp.where(rank_of(hits(routes, expert)) == (lane % 4).astype(F32), mix, 0.0)
    outs[0][...], outs[1][...] = hi_lo(mix)


def mix_table(routes, route_weights, experts, after):
    out = sds((routes.shape[0], experts * 4), BF16)
    return run(mix_body, "mix_table", [out, out], [], [routes.T, route_weights.T], after=[after])


def read_stats(board, h):
    lane, row = iota(board.shape, 2), iota(board.shape, 1) + 16 * h
    m = jnp.sum(jnp.where(lane == row, board, 0.0), axis=2, keepdims=True)
    l = jnp.sum(jnp.where((lane == row + 32) | (lane == row + 64), board, 0.0), axis=2, keepdims=True)
    return jnp.where(l > 0.0, m, FLOOR), l


def owner_body(near, far, outs, own_scratch):
    part_ref = near[0]
    board = part_ref[:, 32:48, :].astype(F32)
    q = far[0].get()[...].astype(F32)
    nkv = far[1].get()[...].astype(F32)
    nkv = jnp.concatenate([nkv[:, 0, :], nkv[:, 1, :]], axis=1)
    att = []
    for h in range(2):
        m, l = read_stats(board, h)
        own = jnp.sum(q[:, HD * h : HD * h + HD] * nkv[:, HD * h : HD * h + HD], axis=1, keepdims=True) * SCALE
        top = jnp.maximum(jnp.max(m, axis=0), own)
        lift = jnp.exp(m - top[None])
        n = jnp.sum(part_ref[:, 16 * h : 16 * h + 16, :].astype(F32) * lift, axis=0)
        den = jnp.sum(l * lift, axis=0)
        new = jnp.exp(own - top)
        v = nkv[:, 2 * HD + HD * h : 2 * HD + HD * h + HD]
        att.append((n + new * v) / (den + new))
    att_ref, disp = outs
    disp_ref = disp.buf
    att_ref[...] = jnp.concatenate(att, axis=1).astype(BF16)
    both = jnp.concatenate(att, axis=0).astype(BF16)
    out = lax.dot_general(far[2].get()[...], both, (((0,), (0,)), ((), ())), preferred_element_type=F32)
    disp_ref[...] = out.astype(BF16).reshape(disp_ref.shape)


def owner_part(parts, queries, new_kv, cells, experts):
    outs, leaving = [sds(queries.shape, BF16)], [sds((experts, 8, HD), BF16)]
    return run(owner_body, "owner_part", outs, [parts], [queries, new_kv, cells], leaving=leaving)


def flip(x, terms):
    n = x.shape[1]
    eye = jnp.where(iota((n, n), 0) == iota((n, n), 1), 1.0, 0.0).astype(BF16)
    x = x.astype(F32)
    out = jnp.zeros((n, x.shape[0]), F32)
    for _ in range(terms):
        part = x.astype(BF16)
        out = out + lax.dot_general(eye, part, (((1,), (1,)), ((), ())), preferred_element_type=F32)
        x = x - part.astype(F32)
    return out


def rank_of(hit):
    rows = hit.shape[0]
    before = jnp.where(iota((rows, rows), 0) > iota((rows, rows), 1), 1.0, 0.0).astype(BF16)
    return dot(before, hit.astype(BF16))


def unfold(x):
    n, _, w = x.shape
    x = x.reshape(n // 2, 2, 8, w)
    a, b = x[:, 0], x[:, 1]
    top = iota(a.shape, 1) < 4
    left = jnp.where(top, a, pltpu.roll(b, 4, 1))
    right = jnp.where(top, pltpu.roll(a, 4, 1), b)
    return left.reshape(n * 4, w), right.reshape(n * 4, w)


def fold(left, right):
    rows, w = left.shape
    left, right = left.reshape(rows // 8, 8, w), right.reshape(rows // 8, 8, w)
    top = iota(left.shape, 1) < 4
    a = jnp.where(top, left, pltpu.roll(right, 4, 1))
    b = jnp.where(top, pltpu.roll(left, 4, 1), right)
    return a, b


def head_blocks(size):
    return [pl.multiple_of(((head_id() + 4 - k) % 4) * size, size) for k in range(4)]


def early_body(near, far, outs, own):
    tok_ref, wo_ref = near
    xs = outs[0]
    eff, w = 2 * HD, xs.shape[2]
    att = jnp.concatenate(unfold(tok_ref[...].astype(F32)), axis=1).astype(BF16)
    rows = pl.ds(head_blocks(eff)[0], eff)
    for k, first in enumerate(head_blocks(2 * w)):
        pair = unfold(far[k].get()[...].astype(F32))
        for f in range(2):
            xs[2 * k + f] = pair[f] + dot(att, wo_ref[rows, pl.ds(first + f * w, w)])


def early_rows(tokens, out_weight, res):
    n = tokens.shape[0]
    w = res[0].shape[2]
    return run(early_body, "early_rows", [sds((8, n * 4, w), F32)], [tokens, out_weight], res)[0]


def expert_body(near, far, outs, own):
    inner_ref, hid = outs
    hs = own[0]
    att, (xs, wo_ref, wg_ref, wu_ref) = near[:3], near[3:]
    gain, mine, own_res = far[0], far[1:5], far[5]
    n = inner_ref.shape[0]
    eff = 2 * HD
    w = xs.shape[2]
    att = [jnp.concatenate(unfold(a[...].astype(F32)), axis=1).astype(BF16) for a in att]
    block = head_blocks(eff)
    firsts = [first + f * w for first in head_blocks(2 * w) for f in range(2)]
    cols = pl.ds(head_blocks(2 * w)[0], 2 * w)
    acc = own_res.get()[:, cols].astype(F32)
    acc = acc + sum(dot(mine[i].get()[...], wo_ref[pl.ds(block[i], eff), cols]) for i in range(4))
    hid.buf[...] = acc.astype(BF16)
    hid.send()
    total = jnp.zeros((n, 1), F32)
    for j, first in enumerate(firsts):
        acc = xs[j]
        for i in range(3):
            acc = acc + dot(att[i], wo_ref[pl.ds(block[i + 1], eff), pl.ds(first, w)])
        part = acc.astype(BF16)
        hs[j] = part
        part = part.astype(F32)
        total = total + jnp.sum(part * part, axis=1, keepdims=True)
    scale = lax.rsqrt(total / (8 * w) + EPS)
    gain_ref = gain.get()
    gate = jnp.zeros((n, wg_ref.shape[1]), F32)
    up = jnp.zeros((n, wg_ref.shape[1]), F32)
    for j, first in enumerate(firsts):
        normed = (hs[j].astype(F32) * scale * gain_ref[:, pl.ds(first, w)]).astype(BF16)
        gate = gate + dot(normed, wg_ref[pl.ds(first, w), :])
        up = up + dot(normed, wu_ref[pl.ds(first, w), :])
    inner_ref[...] = (gate / (1.0 + jnp.exp(-gate)) * up).astype(BF16)


def expert_rows(tokens, early, out_weight, w_gate, w_up, gain, mine, residual):
    _, n, w = early.shape
    outs, leaving = [sds((n, w_gate.shape[1]), BF16)], [sds((residual.shape[0], 2 * w), BF16)]
    near = [*tokens, early, out_weight, w_gate, w_up]
    scratch = [pltpu.VMEM((8, n, w), BF16)]
    far = [gain.reshape(1, -1), *mine, residual]
    return run(expert_body, "expert_rows", outs, near, far, scratch, leaving=leaving)


def down_body(near, far, outs, own):
    out_ref = outs[0]
    acc = sum(dot(near[k][...], near[4 + k][...]) for k in range(4))
    width = acc.shape[1]
    a, b = fold(acc[:, : width // 2], acc[:, width // 2 :])
    out_ref[:, 0] = a.astype(BF16)
    out_ref[:, 1] = b.astype(BF16)


def down(inners, w_cols, after):
    rows = inners[0].shape[0]
    width = w_cols[0].shape[1]
    out = run(down_body, "down", [sds((rows // 8, 2, 8, width // 2), BF16)], [*inners, *w_cols], [], after=[after])[0]
    return out.reshape(rows // 4, 8, width // 2)


def blend_body(near, far, outs, own):
    y_ref, hi_ref, low_ref = near
    w = y_ref.shape[2]
    hid_ref = far[0].get()
    for f, part in enumerate(unfold(y_ref[...].astype(F32))):
        part = part.astype(BF16)
        hid = hid_ref[:, f * w : f * w + w].astype(F32)
        moe = dot(hi_ref[...], part) + dot(low_ref[...], part)
        outs[0][:, f * w : f * w + w] = (hid + moe).astype(BF16)


def blend(returned, mix, hidden):
    return run(blend_body, "blend", [sds(hidden.shape, BF16)], [returned, *mix], [hidden])[0]


def norm_body(near, far, outs, own):
    head = head_id()
    w = near[0].shape[1]
    parts = [s[...].astype(F32) for s in (far[1].get(), *near)]
    total = sum(jnp.sum(p * p, axis=1, keepdims=True) for p in parts)
    scale = lax.rsqrt(total / (4 * w) + EPS)
    gain_ref = far[0].get()
    for k, p in enumerate(parts):
        cols = pl.ds(pl.multiple_of(((head + 4 - k) % 4) * w, w), w)
        outs[0][:, cols] = (p * scale * gain_ref[:, cols]).astype(BF16)


def norm_parts(parts, gain):
    rows, w = parts[0].shape
    return run(norm_body, "norm_parts", [sds((rows, 4 * w), BF16)], parts[1:], [gain.reshape(1, -1), parts[0]])[0]


def from_heads(x):
    n = lax.axis_size("head")
    return [x] + [lax.ppermute(x, "head", [(i, (i + k) % n) for i in range(n)]) for k in range(1, n)]


def to_heads(xs):
    n = lax.axis_size("head")
    return [xs[0]] + [lax.ppermute(xs[k], "head", [(i, (i + k) % n) for i in range(n)]) for k in range(1, n)]


def swap_core(x):
    return lax.ppermute(x, "c", [(0, 1), (1, 0)])


def local(
    residual, queries, new_kv, kv_cache, lengths, slot_request, slot_page, slot_used, out_weight,
    norm_gain, routes, route_weights, w_gate, w_up, w_down, next_gain, next_weight,
):
    rows = queries.shape[0]
    experts = lax.axis_size(REQ)
    chips = experts // 2
    out_weight = lax.all_gather(out_weight, "head", axis=0, tiled=True)
    qa = lax.all_to_all(outset(queries, residual, routes, chips), ("z", "y"), 0, 0, tiled=True)
    tables = slot_tables(slot_request, slot_page, slot_used, lengths, kv_cache, [qa])
    keep, send, res = attend_pages(tables, qa, swap_core(qa))
    merged = merge(keep, swap_core(send))
    w_cols = to_heads(split_columns(w_down[0], merged))
    cells = cells_table(routes, experts, merged)
    res = from_heads(res.reshape(experts, 8, -1))
    arrived = lax.all_to_all(merged, ("z", "y"), 0, 0, tiled=True)
    arrived, cells = lax.optimization_barrier((arrived, cells))
    attended, disp = owner_part(arrived, queries, new_kv, cells, experts)
    tokens = lax.all_to_all(disp, REQ, 0, 0, tiled=True)
    tokens, attended, res, w_cols = lax.optimization_barrier((tokens, attended, res, w_cols))
    out_weight, w_gate, w_up = fetch(tokens, out_weight, w_gate[0], w_up[0])
    early = early_rows(tokens, out_weight, res)
    others, mine = from_heads(tokens)[1:], from_heads(attended)
    inner, hidden = expert_rows(others, early, out_weight, w_gate, w_up, norm_gain, mine, residual)
    w_cols = fetch(inner, *w_cols)
    mix = mix_table(routes, route_weights, experts, inner)
    expert_out = down(from_heads(inner), w_cols, mix[0])
    returned = lax.all_to_all(expert_out, REQ, 0, 0, tiled=True)
    stream = blend(returned, mix, hidden)
    normed = norm_parts(from_heads(stream), next_gain)
    next_qkv = jnp.einsum("td,dcf->tcf", normed, next_weight, preferred_element_type=F32).astype(BF16)
    return stream, next_qkv


def solution(mesh):
    split = Mesh(mesh.devices.reshape(8, 4, 2, 4), ("z", "y", "c", "head"))
    placed = (
        P(REQ, None),
        P(REQ, "head"),
        P(REQ, None, "head"),
        P(REQ, None, None, "head"),
        P(),
        P(REQ),
        P(REQ),
        P(REQ),
        P("head", None),
        P(),
        P(REQ, None),
        P(REQ, None),
        P(REQ, None, "head"),
        P(REQ, None, "head"),
        P(REQ, "head", None),
        P(),
        P(None, None, "head"),
    )
    return jax.shard_map(
        local,
        mesh=split,
        in_specs=placed,
        out_specs=(P(REQ, "head"), P(REQ, None, "head")),
        check_vma=False,
    )
```

```python
import functools
import math

import jax
import jax.numpy as jnp
from jax import lax
from jax.experimental import pallas as pl
from jax.experimental.pallas import tpu as pltpu
from jax.sharding import Mesh, PartitionSpec as P

HD = 128
EPS = 1e-06
FLOOR = -(2.0**99)
SCALE = 1.0 / math.sqrt(HD)
F32 = jnp.float32
BF16 = jnp.bfloat16
REQ = ("z", "y", "c")
VLIM = pltpu.CompilerParams(vmem_limit_bytes=24 * 1024 * 1024)
VM = pl.BlockSpec(memory_space=pltpu.VMEM)


class Pending:
    def __init__(self, buf, copy):
        self.buf, self.copy, self.done = buf, copy, False

    def get(self):
        if not self.done:
            self.copy.wait()
            self.done = True
        return self.buf


def pin(xs):
    return [pltpu.with_memory_space_constraint(x, pltpu.HBM) for x in xs]


class Leaving:
    def __init__(self, buf, copy):
        self.buf, self.copy, self.sent = buf, copy, False

    def send(self):
        self.copy.start()
        self.sent = True


def run(body, name, outs, near, far, scratch=(), after=(), moves=(), leaving=(), after_hbm=()):
    nn, nf, nm, no, nl = len(near), len(far), len(moves), len(outs), len(leaving)
    after = [*after, *pin(after_hbm)]
    na = len(after)
    nh = len(after_hbm)
    parts = 4

    def kernel(*refs):
        ins, refs = refs[: nn + nf + na + nm], refs[nn + nf + na + nm :]
        outputs, out_hbm, moved = refs[:no], refs[no : no + nl], refs[no + nl : no + nl + nm]
        rest = refs[no + nl + nm :]
        bufs, out_bufs, rest = rest[:nf], rest[nf : nf + nl], rest[nf + nl :]
        sems, move_sems, out_sems, own = rest[0], rest[1], rest[2], rest[3:]
        copies = [pltpu.make_async_copy(ins[nn + i], bufs[i], sems.at[i]) for i in range(nf)]
        for copy in copies:
            copy.start()
        pending = [Pending(b, c) for b, c in zip(bufs, copies)]
        moving = []
        for i in range(nm):
            rows = moved[i].shape[0] // parts
            for j in range(parts):
                src, dst = ins[nn + nf + na + i].at[pl.ds(j * rows, rows)], moved[i].at[pl.ds(j * rows, rows)]
                moving.append(pltpu.make_async_copy(src, dst, move_sems.at[parts * i + j]))
        for copy in moving:
            copy.start()
        going = [
            Leaving(out_bufs[i], pltpu.make_async_copy(out_bufs[i], out_hbm[i], out_sems.at[i])) for i in range(nl)
        ]
        body(ins[:nn], pending, (*outputs, *going), own)
        for p in pending:
            p.get()
        for g in going:
            if not g.sent:
                g.send()
            g.copy.wait()
        for copy in moving:
            copy.wait()

    hbm, any_space = pl.BlockSpec(memory_space=pltpu.HBM), pl.BlockSpec(memory_space=pl.ANY)
    return pl.pallas_call(
        kernel,
        name=name,
        out_shape=list(outs)
        + [pltpu.HBM(x.shape, x.dtype) for x in leaving]
        + [sds(x.shape, x.dtype) for x in moves],
        in_specs=[VM] * nn + [hbm] * nf + [any_space] * (na - nh) + [hbm] * (nh + nm),
        out_specs=[VM] * no + [hbm] * nl + [VM] * nm,
        scratch_shapes=[pltpu.VMEM(x.shape, x.dtype) for x in (*far, *leaving)]
        + [pltpu.SemaphoreType.DMA((max(n, 1),)) for n in (nf, nm * parts, nl)]
        + list(scratch),
        compiler_params=VLIM,
    )(*near, *pin(far), *after, *pin(moves))


def sds(shape, dtype):
    return jax.ShapeDtypeStruct(shape, dtype)


def iota(shape, dim):
    return lax.broadcasted_iota(jnp.int32, shape, dim)


def core_id():
    return lax.axis_index("c")


def head_id():
    return lax.axis_index("head")


def dot(a, b):
    return jnp.dot(a, b, preferred_element_type=F32)


def hi_lo(x):
    hi = x.astype(BF16)
    return hi, (x - hi.astype(F32)).astype(BF16)


def hits(routes, expert):
    hit = jnp.zeros(expert.shape, F32)
    for k in range(routes.shape[1]):
        hit = hit + jnp.where(routes[:, k : k + 1] == expert, 1.0, 0.0)
    return hit


def cell_map(routes, expert, lane):
    hit = hits(routes, expert)
    hit = jnp.where(rank_of(hit) == (lane % 4).astype(F32), hit, 0.0)
    left = lane % 8 < 4
    return jnp.concatenate([jnp.where(left, hit, 0.0), jnp.where(left, 0.0, hit)], axis=0).astype(BF16)


def outset_body(near, far, outs, own):
    chips, _, width = outs[0].shape
    rows = far[0].buf.shape[0]
    routes = flip(far[2].get()[...], 1)
    lane = iota((rows, chips * 16), 1)
    expert = (lane // 16) * 2 + (core_id() + (lane // 8) % 2) % 2
    pick = cell_map(routes, expert.astype(F32), lane)
    first = pl.multiple_of(head_id() * 2 * width, 2 * width)
    res = far[1].get()
    both = jnp.concatenate([res[:, pl.ds(first, width)], res[:, pl.ds(first + width, width)]], axis=0)
    out = lax.dot_general(pick, both, (((0,), (0,)), ((), ())), preferred_element_type=F32)
    outs[0][:, 16:32, :] = out.astype(BF16).reshape(chips, 16, width)
    q = far[0].get()[...]
    outs[0][:, 0:16, :] = jnp.broadcast_to(q[None], (chips,) + q.shape)


def outset(queries, residual, routes, chips):
    out = sds((chips, 32, queries.shape[1]), BF16)
    return run(outset_body, "outset", [out], [], [queries, residual, routes.T])[0]


def tables_body(near, far, outs, own, page):
    pick_ref, count_ref, same_ref, mine_ref, spread_ref, spread16_ref = outs
    req = far[0].get()[...]
    slots, total = pick_ref.shape
    half = total // 2
    place = jnp.where((req // 16) % 2 == core_id(), 0, half) + (req // 32) * 16 + req % 16
    spread_ref[...] = jnp.where(iota((total, slots), 0) == place, 1.0, 0.0).astype(BF16)
    spread16_ref[...] = jnp.where(iota((total, slots), 0) // 16 == place // 16, 1.0, 0.0).astype(BF16)
    eye = iota((slots, slots), 0) == iota((slots, slots), 1)

    def to_col(row):
        return jnp.sum(jnp.where(eye, row.astype(F32), 0.0), axis=1, keepdims=True)

    req_col = to_col(req)
    same = req_col == req.astype(F32)
    same_ref[...] = jnp.where(same, 1.0, 0.0)
    slot_row = iota((slots, slots), 1).astype(F32)
    first = jnp.min(jnp.where(same, slot_row, 9999.0), axis=1, keepdims=True)
    leader = first == iota((slots, 1), 0).astype(F32)
    mine = (iota((slots, HD), 1) % 16).astype(F32) == to_col(req % 16)
    mine_ref[...] = jnp.where(mine & leader, 1.0, 0.0)
    lane_total = iota((slots, total), 1).astype(F32)
    pick_ref[...] = jnp.where(to_col(place) == lane_total, 1.0, 0.0).astype(BF16)
    lengths = far[3].get()[...].astype(F32)
    len_col = jnp.sum(jnp.where(req_col == lane_total, lengths, 0.0), axis=1, keepdims=True)
    count = jnp.clip(len_col - to_col(far[1].get()[...]) * page, 0.0, float(page))
    count = jnp.where(to_col(far[2].get()[...]) == 1.0, count, 0.0)
    count_ref[...] = jnp.broadcast_to(count, (slots, HD))


def slot_tables(slot_request, slot_page, slot_used, lengths, kv_cache, after):
    slots = kv_cache.shape[0]
    total = lengths.shape[0]
    return run(
        functools.partial(tables_body, page=kv_cache.shape[2]),
        "slot_tables",
        [
            sds((slots, total), BF16),
            sds((slots, HD), F32),
            sds((slots, slots), F32),
            sds((slots, HD), F32),
            sds((total, slots), BF16),
            sds((total, slots), BF16),
        ],
        [],
        [slot_request.reshape(1, slots), slot_page.reshape(1, slots), slot_used.reshape(1, slots), lengths.reshape(1, total)],
        after=after,
        moves=[kv_cache],
    )


def attn_body(near, far, outs, own):
    pick_ref, count_ref, same_ref, mine_ref, spread_ref, spread16_ref, kv_ref, qa_ref, qb_ref = near
    keep_ref, send_ref, res = outs
    n_scr, m_scr, l_scr = own
    core = core_id()
    res.buf[:, core] = qa_ref[:, 16:24, :]
    res.buf[:, 1 - core] = qb_ref[:, 24:32, :]
    res.send()
    slots = kv_ref.shape[0]
    page = kv_ref.shape[2]
    half = qa_ref.shape[0] * 16
    qa, qb = (r[:, 0:16, :].reshape(half, 2 * HD) for r in (qa_ref, qb_ref))
    chosen = dot(pick_ref[:, :half], qa) + dot(pick_ref[:, half:], qb)
    low_lanes = iota((8, 2 * HD), 1) < HD
    rel = iota((16, 8 * page), 1) - (iota((16, 8 * page), 0) % 8) * page
    rel = rel.astype(F32)
    for b in range(slots // 8):
        q8 = chosen[b * 8 : b * 8 + 8]
        q16 = jnp.concatenate([jnp.where(low_lanes, q8, 0.0), jnp.where(low_lanes, 0.0, q8)], axis=0).astype(BF16)
        keys = kv_ref[b * 8 : b * 8 + 8, 0].reshape(8 * page, 2 * HD)
        vals = kv_ref[b * 8 : b * 8 + 8, 1].reshape(8 * page, 2 * HD)
        s = lax.dot_general(q16, keys, (((1,), (1,)), ((), ())), preferred_element_type=F32) * SCALE
        c8 = count_ref[b * 8 : b * 8 + 8, :1]
        ok = (rel >= 0.0) & (rel < jnp.concatenate([c8, c8], axis=0))
        s = jnp.where(ok, s, FLOOR)
        m = jnp.max(s, axis=1, keepdims=True)
        w = jnp.where(ok, jnp.exp(s - m), 0.0).astype(BF16)
        l = jnp.sum(w.astype(F32), axis=1, keepdims=True)
        n = dot(w, vals)
        for h in range(2):
            n_scr[h, b * 8 : b * 8 + 8, :] = n[8 * h : 8 * h + 8, HD * h : HD * h + HD]
            m_scr[h, b * 8 : b * 8 + 8, :] = jnp.broadcast_to(m[8 * h : 8 * h + 8], (8, slots))
            l_scr[h, b * 8 : b * 8 + 8, :] = jnp.broadcast_to(l[8 * h : 8 * h + 8], (8, slots))

    eye = iota((slots, slots), 0) == iota((slots, slots), 1)
    same = same_ref[...] > 0.0

    def to_row(wide):
        return jnp.sum(jnp.where(eye, wide, 0.0), axis=0, keepdims=True)

    group = iota((slots, HD), 1) // 16
    board = jnp.zeros((slots, HD), F32)
    for h in range(2):
        m_wide = m_scr[h]
        m_ref = jnp.max(jnp.where(same, to_row(m_wide), FLOOR), axis=1, keepdims=True)
        m_ref = m_ref.astype(BF16).astype(F32)
        lift = jnp.exp(m_wide - m_ref)
        n_hi, n_lo = hi_lo(n_scr[h] * lift)
        l_sum = jnp.sum(jnp.where(same, to_row(l_scr[h] * lift), 0.0), axis=1, keepdims=True)
        out = (dot(spread_ref[...], n_hi) + dot(spread_ref[...], n_lo)).astype(BF16)
        keep_ref[:, 16 * h : 16 * h + 16, :] = out[:half].reshape(half // 16, 16, HD)
        send_ref[:, 16 * h : 16 * h + 16, :] = out[half:].reshape(half // 16, 16, HD)
        l_hi = l_sum.astype(BF16).astype(F32)
        for i, stat in enumerate((m_ref, l_hi, l_sum - l_hi)):
            board = jnp.where(group == 2 * i + h, stat, board)
    board = jnp.where(mine_ref[...] > 0.0, board, 0.0).astype(BF16)
    out = dot(spread16_ref[...], board).astype(BF16)
    keep_ref[:, 32:48, :] = out[:half].reshape(half // 16, 16, HD)
    send_ref[:, 32:48, :] = out[half:].reshape(half // 16, 16, HD)


def attend_pages(tables, qa, qb):
    slots, total = tables[0].shape
    scratch = [pltpu.VMEM((2, slots, n), F32) for n in (HD, slots, slots)]
    outs = [sds((total // 32, 48, HD), BF16)] * 2
    leaving = [sds((total // 32, 2, 8, 2 * HD), BF16)]
    return run(attn_body, "attend_pages", outs, [*tables, qa, qb], [], scratch, leaving=leaving)


def merge_body(near, far, outs, own):
    (a_ref, b_ref), out_ref = near, outs[0].buf
    a, b = a_ref[:, 32:48, :].astype(F32), b_ref[:, 32:48, :].astype(F32)
    lane, row = iota(a.shape, 2), iota(a.shape, 1)
    board = jnp.zeros(a.shape, F32)
    for h in range(2):
        (ma, la), (mb, lb) = read_stats(a, h), read_stats(b, h)
        m = jnp.maximum(ma, mb)
        fa, fb = jnp.exp(ma - m), jnp.exp(mb - m)
        rows = slice(16 * h, 16 * h + 16)
        out_ref[:, rows, :] = (a_ref[:, rows, :].astype(F32) * fa + b_ref[:, rows, :].astype(F32) * fb).astype(BF16)
        l = la * fa + lb * fb
        l_hi = l.astype(BF16).astype(F32)
        for i, stat in enumerate((m, l_hi, l - l_hi)):
            board = jnp.where(lane == row + 32 * i + 16 * h, stat, board)
    out_ref[:, 32:48, :] = board.astype(BF16)


def merge(a, b, after):
    return run(merge_body, "merge", [], [a, b], [], after_hbm=[after], leaving=[sds(a.shape, BF16)])[0]


def fetch(after, *arrays):
    return run(lambda *_: None, "fetch", [], [], [], after=[after], moves=arrays)


def split_kernel(w_ref, after_ref, *refs):
    outs, bufs, sems = refs[:4], refs[4:8], refs[8]
    width = outs[0].shape[1]
    cuts, writes = [], []
    for k in range(4):
        cols = pl.ds(pl.multiple_of(((head_id() + k) % 4) * width, width), width)
        cuts.append(pltpu.make_async_copy(w_ref.at[:, cols], bufs[k], sems.at[k]))
        writes.append(pltpu.make_async_copy(bufs[k], outs[k], sems.at[4 + k]))
    for cut in cuts:
        cut.start()
    for cut, write in zip(cuts, writes):
        cut.wait()
        write.start()
    for write in writes:
        write.wait()


def split_columns(w, after):
    hbm = pl.BlockSpec(memory_space=pltpu.HBM)
    shape = (w.shape[0], w.shape[1] // 4)
    return pl.pallas_call(
        split_kernel,
        name="split_columns",
        out_shape=[pltpu.HBM(shape, w.dtype)] * 4,
        in_specs=[hbm, pl.BlockSpec(memory_space=pl.ANY)],
        out_specs=[hbm] * 4,
        scratch_shapes=[pltpu.VMEM(shape, w.dtype)] * 4 + [pltpu.SemaphoreType.DMA((8,))],
        compiler_params=VLIM,
    )(*pin([w]), after)


def mix_body(near, far, outs, own):
    routes, share = flip(far[0].get()[...], 1), flip(far[1].get()[...], 3)
    rows, cells = outs[0].shape
    lane = iota((rows, cells), 1)
    expert = (lane // 4).astype(F32)
    mix = jnp.zeros((rows, cells), F32)
    for k in range(routes.shape[1]):
        mix = mix + jnp.where(routes[:, k : k + 1] == expert, share[:, k : k + 1], 0.0)
    mix = jnp.where(rank_of(hits(routes, expert)) == (lane % 4).astype(F32), mix, 0.0)
    outs[0][...], outs[1][...] = hi_lo(mix)


def mix_table(routes, route_weights, experts, after):
    out = sds((routes.shape[0], experts * 4), BF16)
    return run(mix_body, "mix_table", [out, out], [], [routes.T, route_weights.T], after=[after])


def read_stats(board, h):
    lane, row = iota(board.shape, 2), iota(board.shape, 1) + 16 * h
    m = jnp.sum(jnp.where(lane == row, board, 0.0), axis=2, keepdims=True)
    l = jnp.sum(jnp.where((lane == row + 32) | (lane == row + 64), board, 0.0), axis=2, keepdims=True)
    return jnp.where(l > 0.0, m, FLOOR), l


def owner_body(near, far, outs, own_scratch):
    part_ref = near[0]
    board = part_ref[:, 32:48, :].astype(F32)
    q = far[0].get()[...].astype(F32)
    nkv = far[1].get()[...].astype(F32)
    nkv = jnp.concatenate([nkv[:, 0, :], nkv[:, 1, :]], axis=1)
    att = []
    for h in range(2):
        m, l = read_stats(board, h)
        own = jnp.sum(q[:, HD * h : HD * h + HD] * nkv[:, HD * h : HD * h + HD], axis=1, keepdims=True) * SCALE
        top = jnp.maximum(jnp.max(m, axis=0), own)
        lift = jnp.exp(m - top[None])
        n = jnp.sum(part_ref[:, 16 * h : 16 * h + 16, :].astype(F32) * lift, axis=0)
        den = jnp.sum(l * lift, axis=0)
        new = jnp.exp(own - top)
        v = nkv[:, 2 * HD + HD * h : 2 * HD + HD * h + HD]
        att.append((n + new * v) / (den + new))
    att_ref, disp = outs
    disp_ref = disp.buf
    att_ref[...] = jnp.concatenate(att, axis=1).astype(BF16)
    rows = att_ref.shape[0]
    lane = iota((rows, disp_ref.shape[0] * 8), 1)
    pick = cell_map(flip(far[2].get()[...], 1), (lane // 8).astype(F32), lane)
    both = jnp.concatenate(att, axis=0).astype(BF16)
    out = lax.dot_general(pick, both, (((0,), (0,)), ((), ())), preferred_element_type=F32)
    disp_ref[...] = out.astype(BF16).reshape(disp_ref.shape)


def owner_part(parts, queries, new_kv, routes, experts):
    outs, leaving = [sds(queries.shape, BF16)], [sds((experts, 8, HD), BF16)]
    return run(owner_body, "owner_part", outs, [parts], [queries, new_kv, routes.T], leaving=leaving)


def flip(x, terms):
    n = x.shape[1]
    eye = jnp.where(iota((n, n), 0) == iota((n, n), 1), 1.0, 0.0).astype(BF16)
    x = x.astype(F32)
    out = jnp.zeros((n, x.shape[0]), F32)
    for _ in range(terms):
        part = x.astype(BF16)
        out = out + lax.dot_general(eye, part, (((1,), (1,)), ((), ())), preferred_element_type=F32)
        x = x - part.astype(F32)
    return out


def rank_of(hit):
    rows = hit.shape[0]
    before = jnp.where(iota((rows, rows), 0) > iota((rows, rows), 1), 1.0, 0.0).astype(BF16)
    return dot(before, hit.astype(BF16))


def unfold(x):
    n, _, w = x.shape
    x = x.reshape(n // 2, 2, 8, w)
    a, b = x[:, 0], x[:, 1]
    top = iota(a.shape, 1) < 4
    left = jnp.where(top, a, pltpu.roll(b, 4, 1))
    right = jnp.where(top, pltpu.roll(a, 4, 1), b)
    return left.reshape(n * 4, w), right.reshape(n * 4, w)


def fold(left, right):
    rows, w = left.shape
    left, right = left.reshape(rows // 8, 8, w), right.reshape(rows // 8, 8, w)
    top = iota(left.shape, 1) < 4
    a = jnp.where(top, left, pltpu.roll(right, 4, 1))
    b = jnp.where(top, pltpu.roll(left, 4, 1), right)
    return a, b


def head_blocks(size):
    return [pl.multiple_of(((head_id() + 4 - k) % 4) * size, size) for k in range(4)]


def early_body(near, far, outs, own):
    tok_ref, wo_ref = near
    xs = outs[0]
    eff, w = 2 * HD, xs.shape[2]
    att = jnp.concatenate(unfold(tok_ref[...].astype(F32)), axis=1).astype(BF16)
    rows = pl.ds(head_blocks(eff)[0], eff)
    for k, first in enumerate(head_blocks(2 * w)):
        pair = unfold(far[k].get()[...].astype(F32))
        for f in range(2):
            xs[2 * k + f] = pair[f] + dot(att, wo_ref[rows, pl.ds(first + f * w, w)])


def early_rows(tokens, out_weight, res):
    n = tokens.shape[0]
    w = res[0].shape[2]
    return run(early_body, "early_rows", [sds((8, n * 4, w), F32)], [tokens, out_weight], res)[0]


def expert_body(near, far, outs, own):
    inner_ref, hid = outs
    hs = own[0]
    att, (xs, wo_ref, wg_ref, wu_ref) = near[:3], near[3:]
    gain, mine, own_res = far[0], far[1:5], far[5]
    n = inner_ref.shape[0]
    eff = 2 * HD
    w = xs.shape[2]
    att = [jnp.concatenate(unfold(a[...].astype(F32)), axis=1).astype(BF16) for a in att]
    block = head_blocks(eff)
    firsts = [first + f * w for first in head_blocks(2 * w) for f in range(2)]
    cols = pl.ds(head_blocks(2 * w)[0], 2 * w)
    acc = own_res.get()[:, cols].astype(F32)
    acc = acc + sum(dot(mine[i].get()[...], wo_ref[pl.ds(block[i], eff), cols]) for i in range(4))
    hid.buf[...] = acc.astype(BF16)
    hid.send()
    total = jnp.zeros((n, 1), F32)
    for j, first in enumerate(firsts):
        acc = xs[j]
        for i in range(3):
            acc = acc + dot(att[i], wo_ref[pl.ds(block[i + 1], eff), pl.ds(first, w)])
        part = acc.astype(BF16)
        hs[j] = part
        part = part.astype(F32)
        total = total + jnp.sum(part * part, axis=1, keepdims=True)
    scale = lax.rsqrt(total / (8 * w) + EPS)
    gain_ref = gain.get()
    gate = jnp.zeros((n, wg_ref.shape[1]), F32)
    up = jnp.zeros((n, wg_ref.shape[1]), F32)
    for j, first in enumerate(firsts):
        normed = (hs[j].astype(F32) * scale * gain_ref[:, pl.ds(first, w)]).astype(BF16)
        gate = gate + dot(normed, wg_ref[pl.ds(first, w), :])
        up = up + dot(normed, wu_ref[pl.ds(first, w), :])
    inner_ref[...] = (gate / (1.0 + jnp.exp(-gate)) * up).astype(BF16)


def expert_rows(tokens, early, out_weight, w_gate, w_up, gain, mine, residual):
    _, n, w = early.shape
    outs, leaving = [sds((n, w_gate.shape[1]), BF16)], [sds((residual.shape[0], 2 * w), BF16)]
    near = [*tokens, early, out_weight, w_gate, w_up]
    scratch = [pltpu.VMEM((8, n, w), BF16)]
    far = [gain.reshape(1, -1), *mine, residual]
    return run(expert_body, "expert_rows", outs, near, far, scratch, leaving=leaving)


def down_body(near, far, outs, own):
    out_ref = outs[0]
    acc = sum(dot(near[k][...], near[4 + k][...]) for k in range(4))
    width = acc.shape[1]
    a, b = fold(acc[:, : width // 2], acc[:, width // 2 :])
    out_ref[:, 0] = a.astype(BF16)
    out_ref[:, 1] = b.astype(BF16)


def down(inners, w_cols, after):
    rows = inners[0].shape[0]
    width = w_cols[0].shape[1]
    out = run(down_body, "down", [sds((rows // 8, 2, 8, width // 2), BF16)], [*inners, *w_cols], [], after=[after])[0]
    return out.reshape(rows // 4, 8, width // 2)


def blend_body(near, far, outs, own):
    y_ref, hi_ref, low_ref = near
    w = y_ref.shape[2]
    hid_ref = far[0].get()
    for f, part in enumerate(unfold(y_ref[...].astype(F32))):
        part = part.astype(BF16)
        hid = hid_ref[:, f * w : f * w + w].astype(F32)
        moe = dot(hi_ref[...], part) + dot(low_ref[...], part)
        outs[0][:, f * w : f * w + w] = (hid + moe).astype(BF16)


def blend(returned, mix, hidden):
    return run(blend_body, "blend", [sds(hidden.shape, BF16)], [returned, *mix], [hidden])[0]


def norm_body(near, far, outs, own):
    head = head_id()
    w = near[0].shape[1]
    parts = [s[...].astype(F32) for s in (far[1].get(), *near)]
    total = sum(jnp.sum(p * p, axis=1, keepdims=True) for p in parts)
    scale = lax.rsqrt(total / (4 * w) + EPS)
    gain_ref = far[0].get()
    for k, p in enumerate(parts):
        cols = pl.ds(pl.multiple_of(((head + 4 - k) % 4) * w, w), w)
        outs[0][:, cols] = (p * scale * gain_ref[:, cols]).astype(BF16)


def norm_parts(parts, gain):
    rows, w = parts[0].shape
    return run(norm_body, "norm_parts", [sds((rows, 4 * w), BF16)], parts[1:], [gain.reshape(1, -1), parts[0]])[0]


def from_heads(x):
    n = lax.axis_size("head")
    return [x] + [lax.ppermute(x, "head", [(i, (i + k) % n) for i in range(n)]) for k in range(1, n)]


def to_heads(xs):
    n = lax.axis_size("head")
    return [xs[0]] + [lax.ppermute(xs[k], "head", [(i, (i + k) % n) for i in range(n)]) for k in range(1, n)]


def swap_core(x):
    return lax.ppermute(x, "c", [(0, 1), (1, 0)])


def local(
    residual, queries, new_kv, kv_cache, lengths, slot_request, slot_page, slot_used, out_weight,
    norm_gain, routes, route_weights, w_gate, w_up, w_down, next_gain, next_weight,
):
    rows = queries.shape[0]
    experts = lax.axis_size(REQ)
    chips = experts // 2
    out_weight = lax.all_gather(out_weight, "head", axis=0, tiled=True)
    qa = lax.all_to_all(outset(queries, residual, routes, chips), ("z", "y"), 0, 0, tiled=True)
    tables = slot_tables(slot_request, slot_page, slot_used, lengths, kv_cache, [qa])
    keep, send, res = attend_pages(tables, qa, swap_core(qa))
    blocks = split_columns(w_down[0], send)
    merged = merge(keep, swap_core(send), blocks[0])
    w_cols = to_heads(blocks)
    res = from_heads(res.reshape(experts, 8, -1))
    arrived = lax.all_to_all(merged, ("z", "y"), 0, 0, tiled=True)
    attended, disp = owner_part(arrived, queries, new_kv, routes, experts)
    tokens = lax.all_to_all(disp, REQ, 0, 0, tiled=True)
    mine = from_heads(attended)
    tokens, mine, res, w_cols = lax.optimization_barrier((tokens, mine, res, w_cols))
    out_weight, w_gate, w_up = fetch(tokens, out_weight, w_gate[0], w_up[0])
    early = early_rows(tokens, out_weight, res)
    others = from_heads(tokens)[1:]
    inner, hidden = expert_rows(others, early, out_weight, w_gate, w_up, norm_gain, mine, residual)
    w_cols = fetch(inner, *w_cols)
    mix = mix_table(routes, route_weights, experts, inner)
    expert_out = down(from_heads(inner), w_cols, mix[0])
    returned = lax.all_to_all(expert_out, REQ, 0, 0, tiled=True)
    stream = blend(returned, mix, hidden)
    normed = norm_parts(from_heads(stream), next_gain)
    next_qkv = jnp.einsum("td,dcf->tcf", normed, next_weight, preferred_element_type=F32).astype(BF16)
    return stream, next_qkv


def solution(mesh):
    split = Mesh(mesh.devices.reshape(8, 4, 2, 4), ("z", "y", "c", "head"))
    placed = (
        P(REQ, None),
        P(REQ, "head"),
        P(REQ, None, "head"),
        P(REQ, None, None, "head"),
        P(),
        P(REQ),
        P(REQ),
        P(REQ),
        P("head", None),
        P(),
        P(REQ, None),
        P(REQ, None),
        P(REQ, None, "head"),
        P(REQ, None, "head"),
        P(REQ, "head", None),
        P(),
        P(None, None, "head"),
    )
    return jax.shard_map(
        local,
        mesh=split,
        in_specs=placed,
        out_specs=(P(REQ, "head"), P(REQ, None, "head")),
        check_vma=False,
    )
```

```python
import functools
import math

import jax
import jax.numpy as jnp
from jax import lax
from jax.experimental import pallas as pl
from jax.experimental.pallas import tpu as pltpu
from jax.sharding import Mesh, PartitionSpec as P

HD = 128
EPS = 1e-06
FLOOR = -(2.0**99)
SCALE = 1.0 / math.sqrt(HD)
F32 = jnp.float32
BF16 = jnp.bfloat16
REQ = ("z", "y", "c")
VLIM = pltpu.CompilerParams(vmem_limit_bytes=24 * 1024 * 1024)
VM = pl.BlockSpec(memory_space=pltpu.VMEM)


class Pending:
    def __init__(self, buf, copy):
        self.buf, self.copy, self.done = buf, copy, False

    def get(self):
        if not self.done:
            self.copy.wait()
            self.done = True
        return self.buf


def pin(xs):
    return [pltpu.with_memory_space_constraint(x, pltpu.HBM) for x in xs]


PIECES = 4


class Leaving:
    def __init__(self, buf, out, sems, base):
        rows = buf.shape[0] // PIECES
        parts = [pl.ds(j * rows, rows) for j in range(PIECES)]
        self.buf, self.sent = buf, 0
        self.copies = [pltpu.make_async_copy(buf.at[p], out.at[p], sems.at[base + j]) for j, p in enumerate(parts)]

    def send(self):
        self.copies[self.sent].start()
        self.sent += 1

    def finish(self):
        while self.sent < PIECES:
            self.send()
        for copy in self.copies:
            copy.wait()


def part_of(x):
    return x if isinstance(x, tuple) else (x, 0, x.shape[0])


def run(body, name, outs, near, far, scratch=(), after=(), moves=(), leaving=(), after_hbm=()):
    after = [*after, *pin(after_hbm)]
    far, moves = [part_of(x) for x in far], [part_of(x) for x in moves]
    na, nh, nn, nf, nm = len(after), len(after_hbm), len(near), len(far), len(moves)
    no, nl = len(outs), len(leaving)

    def kernel(*refs):
        ins, refs = refs[: nn + nf + na + nm], refs[nn + nf + na + nm :]
        outputs, out_hbm, moved = refs[:no], refs[no : no + nl], refs[no + nl : no + nl + nm]
        rest = refs[no + nl + nm :]
        bufs, out_bufs, rest = rest[:nf], rest[nf : nf + nl], rest[nf + nl :]
        sems, move_sems, out_sems, own = rest[0], rest[1], rest[2], rest[3:]
        pending = []
        for i, (x, first, rows) in enumerate(far):
            src = ins[nn + i] if rows == x.shape[0] else ins[nn + i].at[pl.ds(first, rows)]
            copy = pltpu.make_async_copy(src, bufs[i], sems.at[i])
            copy.start()
            pending.append(Pending(bufs[i], copy))
        moving = []
        for i, (x, first, rows) in enumerate(moves):
            rows = rows // PIECES
            for j in range(PIECES):
                src = ins[nn + nf + na + i].at[pl.ds(first + j * rows, rows)]
                dst = moved[i].at[pl.ds(j * rows, rows)]
                moving.append(pltpu.make_async_copy(src, dst, move_sems.at[PIECES * i + j]))
        for copy in moving:
            copy.start()
        going = [Leaving(out_bufs[i], out_hbm[i], out_sems, PIECES * i) for i in range(nl)]
        body(ins[:nn], pending, (*outputs, *going), own)
        for p in pending:
            p.get()
        for g in going:
            g.finish()
        for copy in moving:
            copy.wait()

    hbm, any_space = pl.BlockSpec(memory_space=pltpu.HBM), pl.BlockSpec(memory_space=pl.ANY)
    far_shapes = [((r,) + x.shape[1:], x.dtype) for x, _, r in far]
    return pl.pallas_call(
        kernel,
        name=name,
        out_shape=list(outs)
        + [pltpu.HBM(x.shape, x.dtype) for x in leaving]
        + [sds((r,) + x.shape[1:], x.dtype) for x, _, r in moves],
        in_specs=[VM] * nn + [hbm] * nf + [any_space] * (na - nh) + [hbm] * (nh + nm),
        out_specs=[VM] * no + [hbm] * nl + [VM] * nm,
        scratch_shapes=[pltpu.VMEM(*f) for f in far_shapes]
        + [pltpu.VMEM(x.shape, x.dtype) for x in leaving]
        + [pltpu.SemaphoreType.DMA((max(n, 1),)) for n in (nf, nm * PIECES, nl * PIECES)]
        + list(scratch),
        compiler_params=VLIM,
    )(*near, *pin([x for x, _, _ in far]), *after, *pin([x for x, _, _ in moves]))


def sds(shape, dtype):
    return jax.ShapeDtypeStruct(shape, dtype)


def iota(shape, dim):
    return lax.broadcasted_iota(jnp.int32, shape, dim)


def core_id():
    return lax.axis_index("c")


def head_id():
    return lax.axis_index("head")


def dot(a, b):
    return jnp.dot(a, b, preferred_element_type=F32)


def hi_lo(x):
    hi = x.astype(BF16)
    return hi, (x - hi.astype(F32)).astype(BF16)


def hits(routes, expert):
    hit = jnp.zeros(expert.shape, F32)
    for k in range(routes.shape[1]):
        hit = hit + jnp.where(routes[:, k : k + 1] == expert, 1.0, 0.0)
    return hit


def cell_map(routes, expert, lane):
    hit = hits(routes, expert)
    hit = jnp.where(rank_of(hit) == (lane % 4).astype(F32), hit, 0.0)
    left = lane % 8 < 4
    return jnp.concatenate([jnp.where(left, hit, 0.0), jnp.where(left, 0.0, hit)], axis=0).astype(BF16)


def outset_body(near, far, outs, own):
    chips, _, width = outs[0].shape
    rows = far[0].buf.shape[0]
    routes = flip(far[2].get()[...], 1)
    lane = iota((rows, chips * 16), 1)
    expert = (lane // 16) * 2 + (core_id() + (lane // 8) % 2) % 2
    pick = cell_map(routes, expert.astype(F32), lane)
    first = pl.multiple_of(head_id() * 2 * width, 2 * width)
    res = far[1].get()
    both = jnp.concatenate([res[:, pl.ds(first, width)], res[:, pl.ds(first + width, width)]], axis=0)
    out = lax.dot_general(pick, both, (((0,), (0,)), ((), ())), preferred_element_type=F32)
    outs[0][:, 16:32, :] = out.astype(BF16).reshape(chips, 16, width)
    q = far[0].get()[...]
    outs[0][:, 0:16, :] = jnp.broadcast_to(q[None], (chips,) + q.shape)


def outset(queries, residual, routes, chips):
    out = sds((chips, 32, queries.shape[1]), BF16)
    return run(outset_body, "outset", [out], [], [queries, residual, routes.T])[0]


def tables_body(near, far, outs, own, page):
    pick_ref, count_ref, same_ref, mine_ref, spread_ref, spread16_ref = outs
    req = far[0].get()[...]
    slots, total = pick_ref.shape
    half = total // 2
    place = jnp.where((req // 16) % 2 == core_id(), 0, half) + (req // 32) * 16 + req % 16
    spread_ref[...] = jnp.where(iota((total, slots), 0) == place, 1.0, 0.0).astype(BF16)
    spread16_ref[...] = jnp.where(iota((total, slots), 0) // 16 == place // 16, 1.0, 0.0).astype(BF16)
    eye = iota((slots, slots), 0) == iota((slots, slots), 1)

    def to_col(row):
        return jnp.sum(jnp.where(eye, row.astype(F32), 0.0), axis=1, keepdims=True)

    req_col = to_col(req)
    same = req_col == req.astype(F32)
    same_ref[...] = jnp.where(same, 1.0, 0.0)
    slot_row = iota((slots, slots), 1).astype(F32)
    first = jnp.min(jnp.where(same, slot_row, 9999.0), axis=1, keepdims=True)
    leader = first == iota((slots, 1), 0).astype(F32)
    mine = (iota((slots, HD), 1) % 16).astype(F32) == to_col(req % 16)
    mine_ref[...] = jnp.where(mine & leader, 1.0, 0.0)
    lane_total = iota((slots, total), 1).astype(F32)
    pick_ref[...] = jnp.where(to_col(place) == lane_total, 1.0, 0.0).astype(BF16)
    lengths = far[3].get()[...].astype(F32)
    len_col = jnp.sum(jnp.where(req_col == lane_total, lengths, 0.0), axis=1, keepdims=True)
    count = jnp.clip(len_col - to_col(far[1].get()[...]) * page, 0.0, float(page))
    count = jnp.where(to_col(far[2].get()[...]) == 1.0, count, 0.0)
    count_ref[...] = jnp.broadcast_to(count, (slots, HD))


def slot_tables(slot_request, slot_page, slot_used, lengths, kv_cache, after):
    slots = kv_cache.shape[0]
    total = lengths.shape[0]
    return run(
        functools.partial(tables_body, page=kv_cache.shape[2]),
        "slot_tables",
        [
            sds((slots, total), BF16),
            sds((slots, HD), F32),
            sds((slots, slots), F32),
            sds((slots, HD), F32),
            sds((total, slots), BF16),
            sds((total, slots), BF16),
        ],
        [],
        [slot_request.reshape(1, slots), slot_page.reshape(1, slots), slot_used.reshape(1, slots), lengths.reshape(1, total)],
        after=after,
        moves=[kv_cache],
    )


def attn_body(near, far, outs, own):
    pick_ref, count_ref, same_ref, mine_ref, spread_ref, spread16_ref, kv_ref, qa_ref, qb_ref = near
    keep_ref, send_ref = outs
    n_scr, m_scr, l_scr = own
    slots = kv_ref.shape[0]
    page = kv_ref.shape[2]
    half = qa_ref.shape[0] * 16
    qa, qb = (r[:, 0:16, :].reshape(half, 2 * HD) for r in (qa_ref, qb_ref))
    chosen = dot(pick_ref[:, :half], qa) + dot(pick_ref[:, half:], qb)
    low_lanes = iota((8, 2 * HD), 1) < HD
    rel = iota((16, 8 * page), 1) - (iota((16, 8 * page), 0) % 8) * page
    rel = rel.astype(F32)
    for b in range(slots // 8):
        q8 = chosen[b * 8 : b * 8 + 8]
        q16 = jnp.concatenate([jnp.where(low_lanes, q8, 0.0), jnp.where(low_lanes, 0.0, q8)], axis=0).astype(BF16)
        keys = kv_ref[b * 8 : b * 8 + 8, 0].reshape(8 * page, 2 * HD)
        vals = kv_ref[b * 8 : b * 8 + 8, 1].reshape(8 * page, 2 * HD)
        s = lax.dot_general(q16, keys, (((1,), (1,)), ((), ())), preferred_element_type=F32) * SCALE
        c8 = count_ref[b * 8 : b * 8 + 8, :1]
        ok = (rel >= 0.0) & (rel < jnp.concatenate([c8, c8], axis=0))
        s = jnp.where(ok, s, FLOOR)
        m = jnp.max(s, axis=1, keepdims=True)
        w = jnp.where(ok, jnp.exp(s - m), 0.0).astype(BF16)
        l = jnp.sum(w.astype(F32), axis=1, keepdims=True)
        n = dot(w, vals)
        for h in range(2):
            n_scr[h, b * 8 : b * 8 + 8, :] = n[8 * h : 8 * h + 8, HD * h : HD * h + HD]
            m_scr[h, b * 8 : b * 8 + 8, :] = jnp.broadcast_to(m[8 * h : 8 * h + 8], (8, slots))
            l_scr[h, b * 8 : b * 8 + 8, :] = jnp.broadcast_to(l[8 * h : 8 * h + 8], (8, slots))

    eye = iota((slots, slots), 0) == iota((slots, slots), 1)
    same = same_ref[...] > 0.0

    def to_row(wide):
        return jnp.sum(jnp.where(eye, wide, 0.0), axis=0, keepdims=True)

    group = iota((slots, HD), 1) // 16
    board = jnp.zeros((slots, HD), F32)
    for h in range(2):
        m_wide = m_scr[h]
        m_ref = jnp.max(jnp.where(same, to_row(m_wide), FLOOR), axis=1, keepdims=True)
        m_ref = m_ref.astype(BF16).astype(F32)
        lift = jnp.exp(m_wide - m_ref)
        n_hi, n_lo = hi_lo(n_scr[h] * lift)
        l_sum = jnp.sum(jnp.where(same, to_row(l_scr[h] * lift), 0.0), axis=1, keepdims=True)
        out = (dot(spread_ref[...], n_hi) + dot(spread_ref[...], n_lo)).astype(BF16)
        keep_ref[:, 16 * h : 16 * h + 16, :] = out[:half].reshape(half // 16, 16, HD)
        send_ref[:, 16 * h : 16 * h + 16, :] = out[half:].reshape(half // 16, 16, HD)
        l_hi = l_sum.astype(BF16).astype(F32)
        for i, stat in enumerate((m_ref, l_hi, l_sum - l_hi)):
            board = jnp.where(group == 2 * i + h, stat, board)
    board = jnp.where(mine_ref[...] > 0.0, board, 0.0).astype(BF16)
    out = dot(spread16_ref[...], board).astype(BF16)
    keep_ref[:, 32:48, :] = out[:half].reshape(half // 16, 16, HD)
    send_ref[:, 32:48, :] = out[half:].reshape(half // 16, 16, HD)


def attend_pages(tables, qa, qb):
    slots, total = tables[0].shape
    scratch = [pltpu.VMEM((2, slots, n), F32) for n in (HD, slots, slots)]
    outs = [sds((total // 32, 48, HD), BF16)] * 2
    return run(attn_body, "attend_pages", outs, [*tables, qa, qb], [], scratch)


def merge_body(near, far, outs, own):
    chips = near[0].shape[0] // PIECES
    for piece in range(PIECES):
        part = slice(piece * chips, piece * chips + chips)
        a_ref, b_ref, out_ref = near[0].at[part], near[1].at[part], outs[0].buf.at[part]
        a, b = a_ref[:, 32:48, :].astype(F32), b_ref[:, 32:48, :].astype(F32)
        lane, row = iota(a.shape, 2), iota(a.shape, 1)
        board = jnp.zeros(a.shape, F32)
        for h in range(2):
            (ma, la), (mb, lb) = read_stats(a, h), read_stats(b, h)
            m = jnp.maximum(ma, mb)
            fa, fb = jnp.exp(ma - m), jnp.exp(mb - m)
            rows = slice(16 * h, 16 * h + 16)
            out_ref[:, rows, :] = (a_ref[:, rows, :].astype(F32) * fa + b_ref[:, rows, :].astype(F32) * fb).astype(BF16)
            l = la * fa + lb * fb
            l_hi = l.astype(BF16).astype(F32)
            for i, stat in enumerate((m, l_hi, l - l_hi)):
                board = jnp.where(lane == row + 32 * i + 16 * h, stat, board)
        out_ref[:, 32:48, :] = board.astype(BF16)
        outs[0].send()


def merge(a, b, after):
    return run(merge_body, "merge", [], [a, b], [], after_hbm=[after], leaving=[sds(a.shape, BF16)])[0]


def fetch(after, *arrays):
    return run(lambda *_: None, "fetch", [], [], [], after=[after], moves=arrays)


def pack_kernel(w_ref, qa_ref, qb_ref, after_ref, *refs):
    outs, res_buf, bufs, sems = refs[:4], refs[4], refs[5:9], refs[9]
    rows, width = bufs[0].shape[0] // 2, bufs[0].shape[1]
    held = res_buf.shape[0]
    cuts, writes = [], []
    for k in range(4):
        first = pl.multiple_of(((head_id() + k) % 4) * 2 * width, 2 * width)
        for f in range(2):
            src = w_ref.at[:, pl.ds(first + f * width, width)]
            cuts.append(pltpu.make_async_copy(src, bufs[k].at[pl.ds(f * rows, rows)], sems.at[2 * k + f]))
        writes.append(pltpu.make_async_copy(bufs[k], outs[k].at[pl.ds(held, 2 * rows)], sems.at[8 + k]))
    for cut in cuts:
        cut.start()
    mine, other = qa_ref[:, 16:24, :].astype(F32), qb_ref[:, 24:32, :].astype(F32)
    first = core_id() == 0
    both = [jnp.where(first, mine, other), jnp.where(first, other, mine)]
    res_buf[...] = jnp.stack(both, axis=1).reshape(res_buf.shape).astype(BF16)
    for k in range(4):
        writes.append(pltpu.make_async_copy(res_buf, outs[k].at[pl.ds(0, held)], sems.at[12 + k]))
        writes[-1].start()
    for k in range(4):
        cuts[2 * k].wait()
        cuts[2 * k + 1].wait()
        writes[k].start()
    for write in writes:
        write.wait()


def pack(w_down, qa, qb, after):
    hbm = pl.BlockSpec(memory_space=pltpu.HBM)
    rows, width = w_down.shape[0], w_down.shape[1] // 8
    held = qa.shape[0] * 16
    return pl.pallas_call(
        pack_kernel,
        name="pack",
        out_shape=[pltpu.HBM((held + 2 * rows, width), BF16)] * 4,
        in_specs=[hbm, VM, VM, pl.BlockSpec(memory_space=pl.ANY)],
        out_specs=[hbm] * 4,
        scratch_shapes=[pltpu.VMEM((held, width), BF16)]
        + [pltpu.VMEM((2 * rows, width), BF16)] * 4
        + [pltpu.SemaphoreType.DMA((16,))],
        compiler_params=VLIM,
    )(*pin([w_down]), qa, qb, after)


def cells_body(near, far, outs, own):
    buf = outs[0].buf
    lane = iota((buf.shape[0] // 2, buf.shape[1]), 1)
    buf[...] = cell_map(flip(far[0].get()[...], 1), (lane // 8).astype(F32), lane)


def cells_table(routes, experts, after):
    out = sds((2 * routes.shape[0], experts * 8), BF16)
    return run(cells_body, "cells_table", [], [], [routes.T], after_hbm=[after], leaving=[out])[0]


def mix_body(near, far, outs, own):
    routes, share = flip(far[0].get()[...], 1), flip(far[1].get()[...], 3)
    rows, cells = outs[0].shape
    lane = iota((rows, cells), 1)
    expert = (lane // 4).astype(F32)
    mix = jnp.zeros((rows, cells), F32)
    for k in range(routes.shape[1]):
        mix = mix + jnp.where(routes[:, k : k + 1] == expert, share[:, k : k + 1], 0.0)
    mix = jnp.where(rank_of(hits(routes, expert)) == (lane % 4).astype(F32), mix, 0.0)
    outs[0][...], outs[1][...] = hi_lo(mix)


def mix_table(routes, route_weights, experts, after):
    out = sds((routes.shape[0], experts * 4), BF16)
    return run(mix_body, "mix_table", [out, out], [], [routes.T, route_weights.T], after=[after])


def read_stats(board, h):
    lane, row = iota(board.shape, 2), iota(board.shape, 1) + 16 * h
    m = jnp.sum(jnp.where(lane == row, board, 0.0), axis=2, keepdims=True)
    l = jnp.sum(jnp.where((lane == row + 32) | (lane == row + 64), board, 0.0), axis=2, keepdims=True)
    return jnp.where(l > 0.0, m, FLOOR), l


def owner_body(near, far, outs, own_scratch):
    part_ref = near[0]
    board = part_ref[:, 32:48, :].astype(F32)
    q = far[0].get()[...].astype(F32)
    nkv = far[1].get()[...].astype(F32)
    nkv = jnp.concatenate([nkv[:, 0, :], nkv[:, 1, :]], axis=1)
    att = []
    for h in range(2):
        m, l = read_stats(board, h)
        own = jnp.sum(q[:, HD * h : HD * h + HD] * nkv[:, HD * h : HD * h + HD], axis=1, keepdims=True) * SCALE
        top = jnp.maximum(jnp.max(m, axis=0), own)
        lift = jnp.exp(m - top[None])
        n = jnp.sum(part_ref[:, 16 * h : 16 * h + 16, :].astype(F32) * lift, axis=0)
        den = jnp.sum(l * lift, axis=0)
        new = jnp.exp(own - top)
        v = nkv[:, 2 * HD + HD * h : 2 * HD + HD * h + HD]
        att.append((n + new * v) / (den + new))
    att_ref, disp = outs
    disp_ref = disp.buf
    att_ref[...] = jnp.concatenate(att, axis=1).astype(BF16)
    both = jnp.concatenate(att, axis=0).astype(BF16)
    out = lax.dot_general(far[2].get()[...], both, (((0,), (0,)), ((), ())), preferred_element_type=F32)
    disp_ref[...] = out.astype(BF16).reshape(disp_ref.shape)


def owner_part(parts, queries, new_kv, cells, experts):
    outs, leaving = [sds(queries.shape, BF16)], [sds((experts, 8, HD), BF16)]
    return run(owner_body, "owner_part", outs, [parts], [queries, new_kv, cells], leaving=leaving)


def flip(x, terms):
    n = x.shape[1]
    eye = jnp.where(iota((n, n), 0) == iota((n, n), 1), 1.0, 0.0).astype(BF16)
    x = x.astype(F32)
    out = jnp.zeros((n, x.shape[0]), F32)
    for _ in range(terms):
        part = x.astype(BF16)
        out = out + lax.dot_general(eye, part, (((1,), (1,)), ((), ())), preferred_element_type=F32)
        x = x - part.astype(F32)
    return out


def rank_of(hit):
    rows = hit.shape[0]
    before = jnp.where(iota((rows, rows), 0) > iota((rows, rows), 1), 1.0, 0.0).astype(BF16)
    return dot(before, hit.astype(BF16))


def unfold(x):
    n, _, w = x.shape
    x = x.reshape(n // 2, 2, 8, w)
    a, b = x[:, 0], x[:, 1]
    top = iota(a.shape, 1) < 4
    left = jnp.where(top, a, pltpu.roll(b, 4, 1))
    right = jnp.where(top, pltpu.roll(a, 4, 1), b)
    return left.reshape(n * 4, w), right.reshape(n * 4, w)


def fold(left, right):
    rows, w = left.shape
    left, right = left.reshape(rows // 8, 8, w), right.reshape(rows // 8, 8, w)
    top = iota(left.shape, 1) < 4
    a = jnp.where(top, left, pltpu.roll(right, 4, 1))
    b = jnp.where(top, pltpu.roll(left, 4, 1), right)
    return a, b


def head_blocks(size):
    return [pl.multiple_of(((head_id() + 4 - k) % 4) * size, size) for k in range(4)]


def early_body(near, far, outs, own):
    tok_ref, wo_ref = near
    xs = outs[0]
    eff, w = 2 * HD, xs.shape[2]
    att = jnp.concatenate(unfold(tok_ref[...].astype(F32)), axis=1).astype(BF16)
    rows = pl.ds(head_blocks(eff)[0], eff)
    for k, first in enumerate(head_blocks(2 * w)):
        res = far[k].get()[...].astype(F32)
        pair = unfold(res.reshape(res.shape[0] // 8, 8, w))
        for f in range(2):
            xs[2 * k + f] = pair[f] + dot(att, wo_ref[rows, pl.ds(first + f * w, w)])


def early_rows(tokens, out_weight, res):
    n = tokens.shape[0]
    w = res[0][0].shape[1]
    return run(early_body, "early_rows", [sds((8, n * 4, w), F32)], [tokens, out_weight], res)[0]


def expert_body(near, far, outs, own):
    inner_ref, hid = outs
    hs = own[0]
    att, (xs, wo_ref, wg_ref, wu_ref) = near[:3], near[3:]
    gain, mine, own_res = far[0], far[1:5], far[5]
    n = inner_ref.shape[0]
    eff = 2 * HD
    w = xs.shape[2]
    att = [jnp.concatenate(unfold(a[...].astype(F32)), axis=1).astype(BF16) for a in att]
    block = head_blocks(eff)
    firsts = [first + f * w for first in head_blocks(2 * w) for f in range(2)]
    cols = pl.ds(head_blocks(2 * w)[0], 2 * w)
    acc = own_res.get()[:, cols].astype(F32)
    acc = acc + sum(dot(mine[i].get()[...], wo_ref[pl.ds(block[i], eff), cols]) for i in range(4))
    hid.buf[...] = acc.astype(BF16)
    for _ in range(PIECES):
        hid.send()
    total = jnp.zeros((n, 1), F32)
    for j, first in enumerate(firsts):
        acc = xs[j]
        for i in range(3):
            acc = acc + dot(att[i], wo_ref[pl.ds(block[i + 1], eff), pl.ds(first, w)])
        part = acc.astype(BF16)
        hs[j] = part
        part = part.astype(F32)
        total = total + jnp.sum(part * part, axis=1, keepdims=True)
    scale = lax.rsqrt(total / (8 * w) + EPS)
    gain_ref = gain.get()
    gate = jnp.zeros((n, wg_ref.shape[1]), F32)
    up = jnp.zeros((n, wg_ref.shape[1]), F32)
    for j, first in enumerate(firsts):
        normed = (hs[j].astype(F32) * scale * gain_ref[:, pl.ds(first, w)]).astype(BF16)
        gate = gate + dot(normed, wg_ref[pl.ds(first, w), :])
        up = up + dot(normed, wu_ref[pl.ds(first, w), :])
    inner_ref[...] = (gate / (1.0 + jnp.exp(-gate)) * up).astype(BF16)


def expert_rows(tokens, early, out_weight, w_gate, w_up, gain, mine, residual):
    _, n, w = early.shape
    outs, leaving = [sds((n, w_gate.shape[1]), BF16)], [sds((residual.shape[0], 2 * w), BF16)]
    near = [*tokens, early, out_weight, w_gate, w_up]
    scratch = [pltpu.VMEM((8, n, w), BF16)]
    far = [gain.reshape(1, -1), *mine, residual]
    return run(expert_body, "expert_rows", outs, near, far, scratch, leaving=leaving)


def down_body(near, far, outs, own):
    out_ref = outs[0]
    k_rows = near[0].shape[1]
    left = sum(dot(near[k][...], near[4 + k][0:k_rows]) for k in range(4))
    right = sum(dot(near[k][...], near[4 + k][k_rows : 2 * k_rows]) for k in range(4))
    a, b = fold(left, right)
    out_ref[:, 0] = a.astype(BF16)
    out_ref[:, 1] = b.astype(BF16)


def down(inners, w_cols, after):
    rows = inners[0].shape[0]
    width = w_cols[0].shape[1]
    out = run(down_body, "down", [sds((rows // 8, 2, 8, width), BF16)], [*inners, *w_cols], [], after=[after])[0]
    return out.reshape(rows // 4, 8, width)


def blend_body(near, far, outs, own):
    y_ref, hi_ref, low_ref = near
    w = y_ref.shape[2]
    hid_ref = far[0].get()
    for f, part in enumerate(unfold(y_ref[...].astype(F32))):
        part = part.astype(BF16)
        hid = hid_ref[:, f * w : f * w + w].astype(F32)
        moe = dot(hi_ref[...], part) + dot(low_ref[...], part)
        outs[0][:, f * w : f * w + w] = (hid + moe).astype(BF16)


def blend(returned, mix, hidden):
    return run(blend_body, "blend", [sds(hidden.shape, BF16)], [returned, *mix], [hidden])[0]


def qkv_body(near, far, outs, own):
    w_ref = near[3]
    w = near[0].shape[1]
    parts = [s[...].astype(F32) for s in (far[1].get(), *near[:3])]
    total = sum(jnp.sum(p * p, axis=1, keepdims=True) for p in parts)
    scale = lax.rsqrt(total / (4 * w) + EPS)
    gain_ref = far[0].get()
    cols = [pl.ds(first, w) for first in head_blocks(w)]
    normed = [(p * scale * gain_ref[:, c]).astype(BF16) for p, c in zip(parts, cols)]
    for i in range(outs[0].shape[0]):
        acc = sum(dot(n, w_ref[i, c, :]) for n, c in zip(normed, cols))
        outs[0][i] = acc.astype(BF16)


def next_proj(parts, gain, weight):
    kinds, _, width = weight.shape
    out = sds((kinds, parts[0].shape[0], width), BF16)
    return run(qkv_body, "next_proj", [out], [*parts[1:], weight], [gain.reshape(1, -1), parts[0]])[0]


def from_heads(x):
    n = lax.axis_size("head")
    return [x] + [lax.ppermute(x, "head", [(i, (i + k) % n) for i in range(n)]) for k in range(1, n)]


def to_heads(xs):
    n = lax.axis_size("head")
    return [xs[0]] + [lax.ppermute(xs[k], "head", [(i, (i + k) % n) for i in range(n)]) for k in range(1, n)]


def swap_core(x):
    return lax.ppermute(x, "c", [(0, 1), (1, 0)])


def local(
    residual, queries, new_kv, kv_cache, lengths, slot_request, slot_page, slot_used, out_weight,
    norm_gain, routes, route_weights, w_gate, w_up, w_down, next_gain, next_weight,
):
    rows = queries.shape[0]
    experts = lax.axis_size(REQ)
    chips = experts // 2
    out_weight = lax.all_gather(out_weight, "head", axis=0, tiled=True)
    qa = lax.all_to_all(outset(queries, residual, routes, chips), ("z", "y"), 0, 0, tiled=True)
    tables = slot_tables(slot_request, slot_page, slot_used, lengths, kv_cache, [qa])
    qb = swap_core(qa)
    keep, send = attend_pages(tables, qa, qb)
    packs = pack(w_down[0], qa, qb, send)
    merged = merge(keep, swap_core(send), packs[0])
    packs = to_heads(packs)
    cells = cells_table(routes, experts, merged)
    arrived = lax.all_to_all(merged, ("z", "y"), 0, 0, tiled=True)
    arrived, cells = lax.optimization_barrier((arrived, cells))
    attended, disp = owner_part(arrived, queries, new_kv, cells, experts)
    tokens = lax.all_to_all(disp, REQ, 0, 0, tiled=True)
    mine = from_heads(attended)
    tokens, mine, packs = lax.optimization_barrier((tokens, mine, packs))
    held = experts * 8
    res = [(p, 0, held) for p in packs]
    out_weight, w_gate, w_up = fetch(tokens, out_weight, w_gate[0], w_up[0])
    early = early_rows(tokens, out_weight, res)
    others = from_heads(tokens)[1:]
    inner, hidden = expert_rows(others, early, out_weight, w_gate, w_up, norm_gain, mine, residual)
    w_cols = fetch(inner, *[(p, held, p.shape[0] - held) for p in packs])
    mix = mix_table(routes, route_weights, experts, inner)
    expert_out = down(from_heads(inner), w_cols, mix[0])
    returned = lax.all_to_all(expert_out, REQ, 0, 0, tiled=True)
    stream = blend(returned, mix, hidden)
    next_qkv = next_proj(from_heads(stream), next_gain, next_weight.transpose(1, 0, 2)).transpose(1, 0, 2)
    return stream, next_qkv


def solution(mesh):
    split = Mesh(mesh.devices.reshape(8, 4, 2, 4), ("z", "y", "c", "head"))
    placed = (
        P(REQ, None),
        P(REQ, "head"),
        P(REQ, None, "head"),
        P(REQ, None, None, "head"),
        P(),
        P(REQ),
        P(REQ),
        P(REQ),
        P("head", None),
        P(),
        P(REQ, None),
        P(REQ, None),
        P(REQ, None, "head"),
        P(REQ, None, "head"),
        P(REQ, "head", None),
        P(),
        P(None, None, "head"),
    )
    return jax.shard_map(
        local,
        mesh=split,
        in_specs=placed,
        out_specs=(P(REQ, "head"), P(REQ, None, "head")),
        check_vma=False,
    )
```

```python
import functools
import math

import jax
import jax.numpy as jnp
from jax import lax
from jax.experimental import pallas as pl
from jax.experimental.pallas import tpu as pltpu
from jax.sharding import Mesh, PartitionSpec as P

HD = 128
EPS = 1e-06
FLOOR = -(2.0**99)
SCALE = 1.0 / math.sqrt(HD)
F32 = jnp.float32
BF16 = jnp.bfloat16
REQ = ("z", "y", "c")
VLIM = pltpu.CompilerParams(vmem_limit_bytes=24 * 1024 * 1024)
VM = pl.BlockSpec(memory_space=pltpu.VMEM)


class Pending:
    def __init__(self, buf, copy):
        self.buf, self.copy, self.done = buf, copy, False

    def get(self):
        if not self.done:
            self.copy.wait()
            self.done = True
        return self.buf


def pin(xs):
    return [pltpu.with_memory_space_constraint(x, pltpu.HBM) for x in xs]


PIECES = 4


class Leaving:
    def __init__(self, buf, out, sems, base):
        rows = buf.shape[0] // PIECES
        parts = [pl.ds(j * rows, rows) for j in range(PIECES)]
        self.buf, self.sent = buf, 0
        self.copies = [pltpu.make_async_copy(buf.at[p], out.at[p], sems.at[base + j]) for j, p in enumerate(parts)]

    def send(self):
        self.copies[self.sent].start()
        self.sent += 1

    def finish(self):
        while self.sent < PIECES:
            self.send()
        for copy in self.copies:
            copy.wait()


class Moved:
    def __init__(self, buf, copies):
        self.buf, self.copies, self.done = buf, copies, False

    def get(self):
        if not self.done:
            for copy in self.copies:
                copy.wait()
            self.done = True
        return self.buf


def part_of(x):
    return x if isinstance(x, tuple) else (x, 0, x.shape[0])


def run(body, name, outs, near, far, scratch=(), after=(), moves=(), leaving=(), after_hbm=()):
    after = [*after, *pin(after_hbm)]
    far, moves = [part_of(x) for x in far], [part_of(x) for x in moves]
    na, nh, nn, nf, nm = len(after), len(after_hbm), len(near), len(far), len(moves)
    no, nl = len(outs), len(leaving)

    def kernel(*refs):
        ins, refs = refs[: nn + nf + na + nm], refs[nn + nf + na + nm :]
        outputs, out_hbm, moved = refs[:no], refs[no : no + nl], refs[no + nl : no + nl + nm]
        rest = refs[no + nl + nm :]
        bufs, out_bufs, rest = rest[:nf], rest[nf : nf + nl], rest[nf + nl :]
        sems, move_sems, out_sems, own = rest[0], rest[1], rest[2], rest[3:]
        pending = []
        for i, (x, first, rows) in enumerate(far):
            src = ins[nn + i] if rows == x.shape[0] else ins[nn + i].at[pl.ds(first, rows)]
            copy = pltpu.make_async_copy(src, bufs[i], sems.at[i])
            copy.start()
            pending.append(Pending(bufs[i], copy))
        moving = []
        for i, (x, first, rows) in enumerate(moves):
            rows, copies = rows // PIECES, []
            for j in range(PIECES):
                src = ins[nn + nf + na + i].at[pl.ds(first + j * rows, rows)]
                dst = moved[i].at[pl.ds(j * rows, rows)]
                copies.append(pltpu.make_async_copy(src, dst, move_sems.at[PIECES * i + j]))
                copies[-1].start()
            moving.append(Moved(moved[i], copies))
        going = [Leaving(out_bufs[i], out_hbm[i], out_sems, PIECES * i) for i in range(nl)]
        body(ins[:nn], pending, (*outputs, *going, *moving), own)
        for p in pending:
            p.get()
        for g in going:
            g.finish()
        for m in moving:
            m.get()

    hbm, any_space = pl.BlockSpec(memory_space=pltpu.HBM), pl.BlockSpec(memory_space=pl.ANY)
    far_shapes = [((r,) + x.shape[1:], x.dtype) for x, _, r in far]
    return pl.pallas_call(
        kernel,
        name=name,
        out_shape=list(outs)
        + [pltpu.HBM(x.shape, x.dtype) for x in leaving]
        + [sds((r,) + x.shape[1:], x.dtype) for x, _, r in moves],
        in_specs=[VM] * nn + [hbm] * nf + [any_space] * (na - nh) + [hbm] * (nh + nm),
        out_specs=[VM] * no + [hbm] * nl + [VM] * nm,
        scratch_shapes=[pltpu.VMEM(*f) for f in far_shapes]
        + [pltpu.VMEM(x.shape, x.dtype) for x in leaving]
        + [pltpu.SemaphoreType.DMA((max(n, 1),)) for n in (nf, nm * PIECES, nl * PIECES)]
        + list(scratch),
        compiler_params=VLIM,
    )(*near, *pin([x for x, _, _ in far]), *after, *pin([x for x, _, _ in moves]))


def sds(shape, dtype):
    return jax.ShapeDtypeStruct(shape, dtype)


def iota(shape, dim):
    return lax.broadcasted_iota(jnp.int32, shape, dim)


def core_id():
    return lax.axis_index("c")


def head_id():
    return lax.axis_index("head")


def dot(a, b):
    return jnp.dot(a, b, preferred_element_type=F32)


def hi_lo(x):
    hi = x.astype(BF16)
    return hi, (x - hi.astype(F32)).astype(BF16)


def hits(routes, expert):
    hit = jnp.zeros(expert.shape, F32)
    for k in range(routes.shape[1]):
        hit = hit + jnp.where(routes[:, k : k + 1] == expert, 1.0, 0.0)
    return hit


def cell_map(routes, expert, lane):
    hit = hits(routes, expert)
    hit = jnp.where(rank_of(hit) == (lane % 4).astype(F32), hit, 0.0)
    left = lane % 8 < 4
    return jnp.concatenate([jnp.where(left, hit, 0.0), jnp.where(left, 0.0, hit)], axis=0).astype(BF16)


def outset_body(near, far, outs, own):
    chips, _, width = outs[0].shape
    rows = far[0].buf.shape[0]
    routes = flip(far[2].get()[...], 1)
    lane = iota((rows, chips * 16), 1)
    expert = (lane // 16) * 2 + (core_id() + (lane // 8) % 2) % 2
    pick = cell_map(routes, expert.astype(F32), lane)
    first = pl.multiple_of(head_id() * 2 * width, 2 * width)
    res = far[1].get()
    both = jnp.concatenate([res[:, pl.ds(first, width)], res[:, pl.ds(first + width, width)]], axis=0)
    out = lax.dot_general(pick, both, (((0,), (0,)), ((), ())), preferred_element_type=F32)
    outs[0][:, 16:32, :] = out.astype(BF16).reshape(chips, 16, width)
    q = far[0].get()[...]
    outs[0][:, 0:16, :] = jnp.broadcast_to(q[None], (chips,) + q.shape)


def outset(queries, residual, routes, chips):
    out = sds((chips, 32, queries.shape[1]), BF16)
    return run(outset_body, "outset", [out], [], [queries, residual, routes.T])[0]


def tables_body(near, far, outs, own, page):
    pick_ref, count_ref, same_ref, mine_ref, spread_ref, spread16_ref = outs[:6]
    req = far[0].get()[...]
    slots, total = pick_ref.shape
    half = total // 2
    place = jnp.where((req // 16) % 2 == core_id(), 0, half) + (req // 32) * 16 + req % 16
    spread_ref[...] = jnp.where(iota((total, slots), 0) == place, 1.0, 0.0).astype(BF16)
    spread16_ref[...] = jnp.where(iota((total, slots), 0) // 16 == place // 16, 1.0, 0.0).astype(BF16)
    eye = iota((slots, slots), 0) == iota((slots, slots), 1)

    def to_col(row):
        return jnp.sum(jnp.where(eye, row.astype(F32), 0.0), axis=1, keepdims=True)

    req_col = to_col(req)
    same = req_col == req.astype(F32)
    same_ref[...] = jnp.where(same, 1.0, 0.0)
    slot_row = iota((slots, slots), 1).astype(F32)
    first = jnp.min(jnp.where(same, slot_row, 9999.0), axis=1, keepdims=True)
    leader = first == iota((slots, 1), 0).astype(F32)
    mine = (iota((slots, HD), 1) % 16).astype(F32) == to_col(req % 16)
    mine_ref[...] = jnp.where(mine & leader, 1.0, 0.0)
    lane_total = iota((slots, total), 1).astype(F32)
    pick_ref[...] = jnp.where(to_col(place) == lane_total, 1.0, 0.0).astype(BF16)
    lengths = far[3].get()[...].astype(F32)
    len_col = jnp.sum(jnp.where(req_col == lane_total, lengths, 0.0), axis=1, keepdims=True)
    count = jnp.clip(len_col - to_col(far[1].get()[...]) * page, 0.0, float(page))
    count = jnp.where(to_col(far[2].get()[...]) == 1.0, count, 0.0)
    count_ref[...] = jnp.broadcast_to(count, (slots, HD))


def slot_tables(slot_request, slot_page, slot_used, lengths, kv_cache, after):
    slots = kv_cache.shape[0]
    total = lengths.shape[0]
    return run(
        functools.partial(tables_body, page=kv_cache.shape[2]),
        "slot_tables",
        [
            sds((slots, total), BF16),
            sds((slots, HD), F32),
            sds((slots, slots), F32),
            sds((slots, HD), F32),
            sds((total, slots), BF16),
            sds((total, slots), BF16),
        ],
        [],
        [slot_request.reshape(1, slots), slot_page.reshape(1, slots), slot_used.reshape(1, slots), lengths.reshape(1, total)],
        after=after,
        moves=[kv_cache],
    )


def attn_body(near, far, outs, own):
    pick_ref, count_ref, same_ref, mine_ref, spread_ref, spread16_ref, kv_ref, qa_ref, qb_ref = near
    keep_ref, send_ref = outs
    n_scr, m_scr, l_scr = own
    slots = kv_ref.shape[0]
    page = kv_ref.shape[2]
    half = qa_ref.shape[0] * 16
    qa, qb = (r[:, 0:16, :].reshape(half, 2 * HD) for r in (qa_ref, qb_ref))
    chosen = dot(pick_ref[:, :half], qa) + dot(pick_ref[:, half:], qb)
    low_lanes = iota((8, 2 * HD), 1) < HD
    rel = iota((16, 8 * page), 1) - (iota((16, 8 * page), 0) % 8) * page
    rel = rel.astype(F32)
    for b in range(slots // 8):
        q8 = chosen[b * 8 : b * 8 + 8]
        q16 = jnp.concatenate([jnp.where(low_lanes, q8, 0.0), jnp.where(low_lanes, 0.0, q8)], axis=0).astype(BF16)
        keys = kv_ref[b * 8 : b * 8 + 8, 0].reshape(8 * page, 2 * HD)
        vals = kv_ref[b * 8 : b * 8 + 8, 1].reshape(8 * page, 2 * HD)
        s = lax.dot_general(q16, keys, (((1,), (1,)), ((), ())), preferred_element_type=F32) * SCALE
        c8 = count_ref[b * 8 : b * 8 + 8, :1]
        ok = (rel >= 0.0) & (rel < jnp.concatenate([c8, c8], axis=0))
        s = jnp.where(ok, s, FLOOR)
        m = jnp.max(s, axis=1, keepdims=True)
        w = jnp.where(ok, jnp.exp(s - m), 0.0).astype(BF16)
        l = jnp.sum(w.astype(F32), axis=1, keepdims=True)
        n = dot(w, vals)
        for h in range(2):
            n_scr[h, b * 8 : b * 8 + 8, :] = n[8 * h : 8 * h + 8, HD * h : HD * h + HD]
            m_scr[h, b * 8 : b * 8 + 8, :] = jnp.broadcast_to(m[8 * h : 8 * h + 8], (8, slots))
            l_scr[h, b * 8 : b * 8 + 8, :] = jnp.broadcast_to(l[8 * h : 8 * h + 8], (8, slots))

    eye = iota((slots, slots), 0) == iota((slots, slots), 1)
    same = same_ref[...] > 0.0

    def to_row(wide):
        return jnp.sum(jnp.where(eye, wide, 0.0), axis=0, keepdims=True)

    group = iota((slots, HD), 1) // 16
    board = jnp.zeros((slots, HD), F32)
    for h in range(2):
        m_wide = m_scr[h]
        m_ref = jnp.max(jnp.where(same, to_row(m_wide), FLOOR), axis=1, keepdims=True)
        m_ref = m_ref.astype(BF16).astype(F32)
        lift = jnp.exp(m_wide - m_ref)
        n_hi, n_lo = hi_lo(n_scr[h] * lift)
        l_sum = jnp.sum(jnp.where(same, to_row(l_scr[h] * lift), 0.0), axis=1, keepdims=True)
        out = (dot(spread_ref[...], n_hi) + dot(spread_ref[...], n_lo)).astype(BF16)
        keep_ref[:, 16 * h : 16 * h + 16, :] = out[:half].reshape(half // 16, 16, HD)
        send_ref[:, 16 * h : 16 * h + 16, :] = out[half:].reshape(half // 16, 16, HD)
        l_hi = l_sum.astype(BF16).astype(F32)
        for i, stat in enumerate((m_ref, l_hi, l_sum - l_hi)):
            board = jnp.where(group == 2 * i + h, stat, board)
    board = jnp.where(mine_ref[...] > 0.0, board, 0.0).astype(BF16)
    out = dot(spread16_ref[...], board).astype(BF16)
    keep_ref[:, 32:48, :] = out[:half].reshape(half // 16, 16, HD)
    send_ref[:, 32:48, :] = out[half:].reshape(half // 16, 16, HD)


def attend_pages(tables, qa, qb):
    slots, total = tables[0].shape
    scratch = [pltpu.VMEM((2, slots, n), F32) for n in (HD, slots, slots)]
    outs = [sds((total // 32, 48, HD), BF16)] * 2
    return run(attn_body, "attend_pages", outs, [*tables, qa, qb], [], scratch)


def merge_body(near, far, outs, own):
    chips = near[0].shape[0] // PIECES
    for piece in range(PIECES):
        part = slice(piece * chips, piece * chips + chips)
        a_ref, b_ref, out_ref = near[0].at[part], near[1].at[part], outs[0].buf.at[part]
        a, b = a_ref[:, 32:48, :].astype(F32), b_ref[:, 32:48, :].astype(F32)
        lane, row = iota(a.shape, 2), iota(a.shape, 1)
        board = jnp.zeros(a.shape, F32)
        for h in range(2):
            (ma, la), (mb, lb) = read_stats(a, h), read_stats(b, h)
            m = jnp.maximum(ma, mb)
            fa, fb = jnp.exp(ma - m), jnp.exp(mb - m)
            rows = slice(16 * h, 16 * h + 16)
            out_ref[:, rows, :] = (a_ref[:, rows, :].astype(F32) * fa + b_ref[:, rows, :].astype(F32) * fb).astype(BF16)
            l = la * fa + lb * fb
            l_hi = l.astype(BF16).astype(F32)
            for i, stat in enumerate((m, l_hi, l - l_hi)):
                board = jnp.where(lane == row + 32 * i + 16 * h, stat, board)
        out_ref[:, 32:48, :] = board.astype(BF16)
        outs[0].send()


def merge(a, b):
    return run(merge_body, "merge", [], [a, b], [], leaving=[sds(a.shape, BF16)])[0]


def fetch(after, *arrays):
    return run(lambda *_: None, "fetch", [], [], [], after=[after], moves=arrays)


def pack_kernel(w_ref, qa_ref, qb_ref, after_ref, *refs):
    outs, res_buf, in_a, in_b, bufs, sems = refs[:4], refs[4], refs[5], refs[6], refs[7:11], refs[11]
    rows, width = bufs[0].shape[0] // 2, bufs[0].shape[1]
    held = res_buf.shape[0]
    reads = [
        pltpu.make_async_copy(qa_ref.at[:, pl.ds(16, 8), :], in_a, sems.at[16]),
        pltpu.make_async_copy(qb_ref.at[:, pl.ds(24, 8), :], in_b, sems.at[17]),
    ]
    for read in reads:
        read.start()
    cuts, writes = [], []
    for k in range(4):
        first = pl.multiple_of(((head_id() + k) % 4) * 2 * width, 2 * width)
        for f in range(2):
            src = w_ref.at[:, pl.ds(first + f * width, width)]
            cuts.append(pltpu.make_async_copy(src, bufs[k].at[pl.ds(f * rows, rows)], sems.at[2 * k + f]))
        writes.append(pltpu.make_async_copy(bufs[k], outs[k].at[pl.ds(held, 2 * rows)], sems.at[8 + k]))
    for cut in cuts:
        cut.start()
    for read in reads:
        read.wait()
    mine, other = in_a[...].astype(F32), in_b[...].astype(F32)
    first = core_id() == 0
    both = [jnp.where(first, mine, other), jnp.where(first, other, mine)]
    res_buf[...] = jnp.stack(both, axis=1).reshape(res_buf.shape).astype(BF16)
    for k in range(4):
        writes.append(pltpu.make_async_copy(res_buf, outs[k].at[pl.ds(0, held)], sems.at[12 + k]))
        writes[-1].start()
    for k in range(4):
        cuts[2 * k].wait()
        cuts[2 * k + 1].wait()
        writes[k].start()
    for write in writes:
        write.wait()


def pack(w_down, qa, qb, after):
    hbm = pl.BlockSpec(memory_space=pltpu.HBM)
    rows, width = w_down.shape[0], w_down.shape[1] // 8
    chips = qa.shape[0]
    held = chips * 16
    return pl.pallas_call(
        pack_kernel,
        name="pack",
        out_shape=[pltpu.HBM((held + 2 * rows, width), BF16)] * 4,
        in_specs=[hbm] * 4,
        out_specs=[hbm] * 4,
        scratch_shapes=[pltpu.VMEM((held, width), BF16)]
        + [pltpu.VMEM((chips, 8, width), BF16)] * 2
        + [pltpu.VMEM((2 * rows, width), BF16)] * 4
        + [pltpu.SemaphoreType.DMA((18,))],
        compiler_params=VLIM,
    )(*pin([w_down, qa, qb, after]))


def cells_body(near, far, outs, own):
    buf = outs[0].buf
    lane = iota((buf.shape[0] // 2, buf.shape[1]), 1)
    buf[...] = cell_map(flip(far[0].get()[...], 1), (lane // 8).astype(F32), lane)


def cells_table(routes, experts, after):
    out = sds((2 * routes.shape[0], experts * 8), BF16)
    return run(cells_body, "cells_table", [], [], [routes.T], after_hbm=[after], leaving=[out])[0]


def mix_body(near, far, outs, own):
    routes, share = flip(far[0].get()[...], 1), flip(far[1].get()[...], 3)
    rows, cells = outs[0].shape
    lane = iota((rows, cells), 1)
    expert = (lane // 4).astype(F32)
    mix = jnp.zeros((rows, cells), F32)
    for k in range(routes.shape[1]):
        mix = mix + jnp.where(routes[:, k : k + 1] == expert, share[:, k : k + 1], 0.0)
    mix = jnp.where(rank_of(hits(routes, expert)) == (lane % 4).astype(F32), mix, 0.0)
    outs[0][...], outs[1][...] = hi_lo(mix)


def mix_table(routes, route_weights, experts, after):
    out = sds((routes.shape[0], experts * 4), BF16)
    return run(mix_body, "mix_table", [out, out], [], [routes.T, route_weights.T], after=[after])


def read_stats(board, h):
    lane, row = iota(board.shape, 2), iota(board.shape, 1) + 16 * h
    m = jnp.sum(jnp.where(lane == row, board, 0.0), axis=2, keepdims=True)
    l = jnp.sum(jnp.where((lane == row + 32) | (lane == row + 64), board, 0.0), axis=2, keepdims=True)
    return jnp.where(l > 0.0, m, FLOOR), l


def owner_body(near, far, outs, own_scratch):
    part_ref = near[0]
    board = part_ref[:, 32:48, :].astype(F32)
    q = far[0].get()[...].astype(F32)
    nkv = far[1].get()[...].astype(F32)
    nkv = jnp.concatenate([nkv[:, 0, :], nkv[:, 1, :]], axis=1)
    att = []
    for h in range(2):
        m, l = read_stats(board, h)
        own = jnp.sum(q[:, HD * h : HD * h + HD] * nkv[:, HD * h : HD * h + HD], axis=1, keepdims=True) * SCALE
        top = jnp.maximum(jnp.max(m, axis=0), own)
        lift = jnp.exp(m - top[None])
        n = jnp.sum(part_ref[:, 16 * h : 16 * h + 16, :].astype(F32) * lift, axis=0)
        den = jnp.sum(l * lift, axis=0)
        new = jnp.exp(own - top)
        v = nkv[:, 2 * HD + HD * h : 2 * HD + HD * h + HD]
        att.append((n + new * v) / (den + new))
    att_ref, disp = outs
    disp_ref = disp.buf
    att_ref[...] = jnp.concatenate(att, axis=1).astype(BF16)
    both = jnp.concatenate(att, axis=0).astype(BF16)
    out = lax.dot_general(far[2].get()[...], both, (((0,), (0,)), ((), ())), preferred_element_type=F32)
    disp_ref[...] = out.astype(BF16).reshape(disp_ref.shape)


def owner_part(parts, queries, new_kv, cells, experts):
    outs, leaving = [sds(queries.shape, BF16)], [sds((experts, 8, HD), BF16)]
    return run(owner_body, "owner_part", outs, [parts], [queries, new_kv, cells], leaving=leaving)


def flip(x, terms):
    n = x.shape[1]
    eye = jnp.where(iota((n, n), 0) == iota((n, n), 1), 1.0, 0.0).astype(BF16)
    x = x.astype(F32)
    out = jnp.zeros((n, x.shape[0]), F32)
    for _ in range(terms):
        part = x.astype(BF16)
        out = out + lax.dot_general(eye, part, (((1,), (1,)), ((), ())), preferred_element_type=F32)
        x = x - part.astype(F32)
    return out


def rank_of(hit):
    rows = hit.shape[0]
    before = jnp.where(iota((rows, rows), 0) > iota((rows, rows), 1), 1.0, 0.0).astype(BF16)
    return dot(before, hit.astype(BF16))


def unfold(x):
    n, _, w = x.shape
    x = x.reshape(n // 2, 2, 8, w)
    a, b = x[:, 0], x[:, 1]
    top = iota(a.shape, 1) < 4
    left = jnp.where(top, a, pltpu.roll(b, 4, 1))
    right = jnp.where(top, pltpu.roll(a, 4, 1), b)
    return left.reshape(n * 4, w), right.reshape(n * 4, w)


def fold(left, right):
    rows, w = left.shape
    left, right = left.reshape(rows // 8, 8, w), right.reshape(rows // 8, 8, w)
    top = iota(left.shape, 1) < 4
    a = jnp.where(top, left, pltpu.roll(right, 4, 1))
    b = jnp.where(top, pltpu.roll(left, 4, 1), right)
    return a, b


def head_blocks(size):
    return [pl.multiple_of(((head_id() + 4 - k) % 4) * size, size) for k in range(4)]


def early_body(near, far, outs, own):
    tok_ref = near[0]
    xs, wo = outs
    eff, w = 2 * HD, xs.shape[2]
    att = jnp.concatenate(unfold(tok_ref[...].astype(F32)), axis=1).astype(BF16)
    for k in range(4):
        res = far[k].get()[...].astype(F32)
        xs[2 * k], xs[2 * k + 1] = unfold(res.reshape(res.shape[0] // 8, 8, w))
    wo_ref = wo.get()
    rows = pl.ds(head_blocks(eff)[0], eff)
    for k, first in enumerate(head_blocks(2 * w)):
        for f in range(2):
            xs[2 * k + f] = xs[2 * k + f] + dot(att, wo_ref[rows, pl.ds(first + f * w, w)])


def early_rows(tokens, out_weight, res):
    n = tokens.shape[0]
    w = res[0][0].shape[1]
    return run(early_body, "early_rows", [sds((8, n * 4, w), F32)], [tokens], res, moves=[out_weight])


def expert_body(near, far, outs, own):
    inner_ref, hid = outs
    hs = own[0]
    att, (xs, wo_ref) = near[:3], near[3:]
    gain, mine, own_res, w_gate, w_up = far[0], far[1:5], *far[5:]
    n = inner_ref.shape[0]
    eff = 2 * HD
    w = xs.shape[2]
    att = [jnp.concatenate(unfold(a[...].astype(F32)), axis=1).astype(BF16) for a in att]
    block = head_blocks(eff)
    firsts = [first + f * w for first in head_blocks(2 * w) for f in range(2)]
    cols = pl.ds(head_blocks(2 * w)[0], 2 * w)
    acc = own_res.get()[:, cols].astype(F32)
    acc = acc + sum(dot(mine[i].get()[...], wo_ref[pl.ds(block[i], eff), cols]) for i in range(4))
    hid.buf[...] = acc.astype(BF16)
    for _ in range(PIECES):
        hid.send()
    total = jnp.zeros((n, 1), F32)
    for j, first in enumerate(firsts):
        acc = xs[j]
        for i in range(3):
            acc = acc + dot(att[i], wo_ref[pl.ds(block[i + 1], eff), pl.ds(first, w)])
        part = acc.astype(BF16)
        hs[j] = part
        part = part.astype(F32)
        total = total + jnp.sum(part * part, axis=1, keepdims=True)
    scale = lax.rsqrt(total / (8 * w) + EPS)
    gain_ref = gain.get()
    wg_ref, wu_ref = w_gate.get(), w_up.get()
    gate = jnp.zeros((n, wg_ref.shape[1]), F32)
    up = jnp.zeros((n, wg_ref.shape[1]), F32)
    for j, first in enumerate(firsts):
        normed = (hs[j].astype(F32) * scale * gain_ref[:, pl.ds(first, w)]).astype(BF16)
        gate = gate + dot(normed, wg_ref[pl.ds(first, w), :])
        up = up + dot(normed, wu_ref[pl.ds(first, w), :])
    inner_ref[...] = (gate / (1.0 + jnp.exp(-gate)) * up).astype(BF16)


def expert_rows(tokens, early, out_weight, w_gate, w_up, gain, mine, residual):
    _, n, w = early.shape
    outs, leaving = [sds((n, w_gate.shape[1]), BF16)], [sds((residual.shape[0], 2 * w), BF16)]
    near = [*tokens, early, out_weight]
    scratch = [pltpu.VMEM((8, n, w), BF16)]
    far = [gain.reshape(1, -1), *mine, residual, w_gate, w_up]
    return run(expert_body, "expert_rows", outs, near, far, scratch, leaving=leaving)


def down_body(near, far, outs, own):
    out_ref = outs[0]
    k_rows = near[0].shape[1]
    left = sum(dot(near[k][...], near[4 + k][0:k_rows]) for k in range(4))
    right = sum(dot(near[k][...], near[4 + k][k_rows : 2 * k_rows]) for k in range(4))
    a, b = fold(left, right)
    out_ref[:, 0] = a.astype(BF16)
    out_ref[:, 1] = b.astype(BF16)


def down(inners, w_cols, after):
    rows = inners[0].shape[0]
    width = w_cols[0].shape[1]
    out = run(down_body, "down", [sds((rows // 8, 2, 8, width), BF16)], [*inners, *w_cols], [], after=[after])[0]
    return out.reshape(rows // 4, 8, width)


def blend_body(near, far, outs, own):
    y_ref, hi_ref, low_ref = near
    w = y_ref.shape[2]
    hid_ref = far[0].get()
    for f, part in enumerate(unfold(y_ref[...].astype(F32))):
        part = part.astype(BF16)
        hid = hid_ref[:, f * w : f * w + w].astype(F32)
        moe = dot(hi_ref[...], part) + dot(low_ref[...], part)
        outs[0][:, f * w : f * w + w] = (hid + moe).astype(BF16)


def blend(returned, mix, hidden):
    return run(blend_body, "blend", [sds(hidden.shape, BF16)], [returned, *mix], [hidden])[0]


def proj_share(x, k, gain_ref, w_ref):
    w = x.shape[1]
    cols = pl.ds(head_blocks(w)[k], w)
    part = (x * gain_ref[:, cols]).astype(BF16)
    return [dot(part, w_ref[i, cols, :]) for i in range(w_ref.shape[0])], jnp.sum(x * x, axis=1, keepdims=True)


def own_proj_body(near, far, outs, own):
    shares, total = proj_share(far[1].get()[...].astype(F32), 0, far[0].get(), near[0])
    for i, share in enumerate(shares):
        outs[0][i] = share
    outs[1][...] = jnp.broadcast_to(total, outs[1].shape)


def proj_body(near, far, outs, own):
    others, w_ref, first_ref, total_ref = near[:3], near[3], near[4], near[5]
    total = total_ref[:, 0:1]
    accs = [first_ref[i] for i in range(w_ref.shape[0])]
    for k, s in enumerate(others):
        shares, add = proj_share(s[...].astype(F32), k + 1, far[0].get(), w_ref)
        accs, total = [a + b for a, b in zip(accs, shares)], total + add
    scale = lax.rsqrt(total / w_ref.shape[1] + EPS)
    for i, acc in enumerate(accs):
        outs[0][i] = (acc * scale).astype(BF16)


def next_proj(parts, gain, weight):
    kinds, _, width = weight.shape
    rows = parts[0].shape[0]
    shape = (kinds, rows, width)
    gain = gain.reshape(1, -1)
    first = run(own_proj_body, "own_proj", [sds(shape, F32), sds((rows, HD), F32)], [weight], [gain, parts[0]])
    return run(proj_body, "next_proj", [sds(shape, BF16)], [*parts[1:], weight, *first], [gain])[0]


def from_heads(x):
    n = lax.axis_size("head")
    return [x] + [lax.ppermute(x, "head", [(i, (i + k) % n) for i in range(n)]) for k in range(1, n)]


def to_heads(xs):
    n = lax.axis_size("head")
    return [xs[0]] + [lax.ppermute(xs[k], "head", [(i, (i + k) % n) for i in range(n)]) for k in range(1, n)]


def swap_core(x):
    return lax.ppermute(x, "c", [(0, 1), (1, 0)])


def local(
    residual, queries, new_kv, kv_cache, lengths, slot_request, slot_page, slot_used, out_weight,
    norm_gain, routes, route_weights, w_gate, w_up, w_down, next_gain, next_weight,
):
    rows = queries.shape[0]
    experts = lax.axis_size(REQ)
    chips = experts // 2
    out_weight = lax.all_gather(out_weight, "head", axis=0, tiled=True)
    qa = lax.all_to_all(outset(queries, residual, routes, chips), ("z", "y"), 0, 0, tiled=True)
    tables = slot_tables(slot_request, slot_page, slot_used, lengths, kv_cache, [qa])
    qb = swap_core(qa)
    keep, send = attend_pages(tables, qa, qb)
    merged = merge(keep, swap_core(send))
    packs = to_heads(pack(w_down[0], qa, qb, merged))
    cells = cells_table(routes, experts, merged)
    arrived = lax.all_to_all(merged, ("z", "y"), 0, 0, tiled=True)
    arrived, cells = lax.optimization_barrier((arrived, cells))
    attended, disp = owner_part(arrived, queries, new_kv, cells, experts)
    tokens = lax.all_to_all(disp, REQ, 0, 0, tiled=True)
    mine = from_heads(attended)
    tokens, mine, packs = lax.optimization_barrier((tokens, mine, packs))
    held = experts * 8
    res = [(p, 0, held) for p in packs]
    early, out_weight = early_rows(tokens, out_weight, res)
    others = from_heads(tokens)[1:]
    inner, hidden = expert_rows(others, early, out_weight, w_gate[0], w_up[0], norm_gain, mine, residual)
    w_cols = fetch(inner, *[(p, held, p.shape[0] - held) for p in packs])
    mix = mix_table(routes, route_weights, experts, inner)
    expert_out = down(from_heads(inner), w_cols, mix[0])
    returned = lax.all_to_all(expert_out, REQ, 0, 0, tiled=True)
    stream = blend(returned, mix, hidden)
    next_qkv = next_proj(from_heads(stream), next_gain, next_weight.transpose(1, 0, 2)).transpose(1, 0, 2)
    return stream, next_qkv


def solution(mesh):
    split = Mesh(mesh.devices.reshape(8, 4, 2, 4), ("z", "y", "c", "head"))
    placed = (
        P(REQ, None),
        P(REQ, "head"),
        P(REQ, None, "head"),
        P(REQ, None, None, "head"),
        P(),
        P(REQ),
        P(REQ),
        P(REQ),
        P("head", None),
        P(),
        P(REQ, None),
        P(REQ, None),
        P(REQ, None, "head"),
        P(REQ, None, "head"),
        P(REQ, "head", None),
        P(),
        P(None, None, "head"),
    )
    return jax.shard_map(
        local,
        mesh=split,
        in_specs=placed,
        out_specs=(P(REQ, "head"), P(REQ, None, "head")),
        check_vma=False,
    )
```

```python
import functools
import math

import jax
import jax.numpy as jnp
from jax import lax
from jax.experimental import pallas as pl
from jax.experimental.pallas import tpu as pltpu
from jax.sharding import Mesh, PartitionSpec as P

HD = 128
EPS = 1e-06
FLOOR = -(2.0**99)
SCALE = 1.0 / math.sqrt(HD)
F32 = jnp.float32
BF16 = jnp.bfloat16
REQ = ("z", "y", "c")
VLIM = pltpu.CompilerParams(vmem_limit_bytes=24 * 1024 * 1024)
VM = pl.BlockSpec(memory_space=pltpu.VMEM)


class Pending:
    def __init__(self, buf, copy):
        self.buf, self.copy, self.done = buf, copy, False

    def get(self):
        if not self.done:
            self.copy.wait()
            self.done = True
        return self.buf


def pin(xs):
    return [pltpu.with_memory_space_constraint(x, pltpu.HBM) for x in xs]


PIECES = 4


class Leaving:
    def __init__(self, buf, out, sems, base):
        rows = buf.shape[0] // PIECES
        parts = [pl.ds(j * rows, rows) for j in range(PIECES)]
        self.buf, self.sent = buf, 0
        self.copies = [pltpu.make_async_copy(buf.at[p], out.at[p], sems.at[base + j]) for j, p in enumerate(parts)]

    def send(self):
        self.copies[self.sent].start()
        self.sent += 1

    def finish(self):
        while self.sent < PIECES:
            self.send()
        for copy in self.copies:
            copy.wait()


class Moved:
    def __init__(self, buf, copies):
        self.buf, self.copies, self.done = buf, copies, False

    def get(self):
        if not self.done:
            for copy in self.copies:
                copy.wait()
            self.done = True
        return self.buf


def part_of(x):
    return x if isinstance(x, tuple) else (x, 0, x.shape[0])


def run(body, name, outs, near, far, scratch=(), after=(), moves=(), leaving=(), after_hbm=()):
    after = [*after, *pin(after_hbm)]
    far, moves = [part_of(x) for x in far], [part_of(x) for x in moves]
    na, nh, nn, nf, nm = len(after), len(after_hbm), len(near), len(far), len(moves)
    no, nl = len(outs), len(leaving)

    def kernel(*refs):
        ins, refs = refs[: nn + nf + na + nm], refs[nn + nf + na + nm :]
        outputs, out_hbm, moved = refs[:no], refs[no : no + nl], refs[no + nl : no + nl + nm]
        rest = refs[no + nl + nm :]
        bufs, out_bufs, rest = rest[:nf], rest[nf : nf + nl], rest[nf + nl :]
        sems, move_sems, out_sems, own = rest[0], rest[1], rest[2], rest[3:]
        pending = []
        for i, (x, first, rows) in enumerate(far):
            src = ins[nn + i] if rows == x.shape[0] else ins[nn + i].at[pl.ds(first, rows)]
            copy = pltpu.make_async_copy(src, bufs[i], sems.at[i])
            copy.start()
            pending.append(Pending(bufs[i], copy))
        moving = []
        for i, (x, first, rows) in enumerate(moves):
            rows, copies = rows // PIECES, []
            for j in range(PIECES):
                src = ins[nn + nf + na + i].at[pl.ds(first + j * rows, rows)]
                dst = moved[i].at[pl.ds(j * rows, rows)]
                copies.append(pltpu.make_async_copy(src, dst, move_sems.at[PIECES * i + j]))
                copies[-1].start()
            moving.append(Moved(moved[i], copies))
        going = [Leaving(out_bufs[i], out_hbm[i], out_sems, PIECES * i) for i in range(nl)]
        body(ins[:nn], pending, (*outputs, *going, *moving), own)
        for p in pending:
            p.get()
        for g in going:
            g.finish()
        for m in moving:
            m.get()

    hbm, any_space = pl.BlockSpec(memory_space=pltpu.HBM), pl.BlockSpec(memory_space=pl.ANY)
    far_shapes = [((r,) + x.shape[1:], x.dtype) for x, _, r in far]
    return pl.pallas_call(
        kernel,
        name=name,
        out_shape=list(outs)
        + [pltpu.HBM(x.shape, x.dtype) for x in leaving]
        + [sds((r,) + x.shape[1:], x.dtype) for x, _, r in moves],
        in_specs=[VM] * nn + [hbm] * nf + [any_space] * (na - nh) + [hbm] * (nh + nm),
        out_specs=[VM] * no + [hbm] * nl + [VM] * nm,
        scratch_shapes=[pltpu.VMEM(*f) for f in far_shapes]
        + [pltpu.VMEM(x.shape, x.dtype) for x in leaving]
        + [pltpu.SemaphoreType.DMA((max(n, 1),)) for n in (nf, nm * PIECES, nl * PIECES)]
        + list(scratch),
        compiler_params=VLIM,
    )(*near, *pin([x for x, _, _ in far]), *after, *pin([x for x, _, _ in moves]))


def sds(shape, dtype):
    return jax.ShapeDtypeStruct(shape, dtype)


def iota(shape, dim):
    return lax.broadcasted_iota(jnp.int32, shape, dim)


def core_id():
    return lax.axis_index("c")


def head_id():
    return lax.axis_index("head")


def dot(a, b):
    return jnp.dot(a, b, preferred_element_type=F32)


def hi_lo(x):
    hi = x.astype(BF16)
    return hi, (x - hi.astype(F32)).astype(BF16)


def hits(routes, expert):
    hit = jnp.zeros(expert.shape, F32)
    for k in range(routes.shape[1]):
        hit = hit + jnp.where(routes[:, k : k + 1] == expert, 1.0, 0.0)
    return hit


def cell_map(routes, expert, lane):
    hit = hits(routes, expert)
    hit = jnp.where(rank_of(hit) == (lane % 4).astype(F32), hit, 0.0)
    left = lane % 8 < 4
    return jnp.concatenate([jnp.where(left, hit, 0.0), jnp.where(left, 0.0, hit)], axis=0).astype(BF16)


def outset_body(near, far, outs, own):
    chips, _, width = outs[0].shape
    rows = far[0].buf.shape[0]
    routes = flip(far[2].get()[...], 1)
    lane = iota((rows, chips * 16), 1)
    expert = (lane // 16) * 2 + (core_id() + (lane // 8) % 2) % 2
    pick = cell_map(routes, expert.astype(F32), lane)
    first = pl.multiple_of(head_id() * 2 * width, 2 * width)
    res = far[1].get()
    both = jnp.concatenate([res[:, pl.ds(first, width)], res[:, pl.ds(first + width, width)]], axis=0)
    out = lax.dot_general(pick, both, (((0,), (0,)), ((), ())), preferred_element_type=F32)
    outs[0][:, 16:32, :] = out.astype(BF16).reshape(chips, 16, width)
    q = far[0].get()[...]
    outs[0][:, 0:16, :] = jnp.broadcast_to(q[None], (chips,) + q.shape)


def outset(queries, residual, routes, chips):
    out = sds((chips, 32, queries.shape[1]), BF16)
    return run(outset_body, "outset", [out], [], [queries, residual, routes.T])[0]


def tables_body(near, far, outs, own, page):
    pick_ref, count_ref, same_ref, mine_ref, spread_ref, spread8_ref = outs[:6]
    req = far[0].get()[...]
    slots, total = pick_ref.shape
    half = total // 2
    place = jnp.where((req // 16) % 2 == core_id(), 0, half) + (req // 32) * 16 + req % 16
    spread_ref[...] = jnp.where(iota((total, slots), 0) == place, 1.0, 0.0).astype(BF16)
    owners = jnp.where(iota((half, slots), 0) // 8 == place // 16, 1.0, 0.0)
    spread8_ref[...] = owners.astype(BF16)
    eye = iota((slots, slots), 0) == iota((slots, slots), 1)

    def to_col(row):
        return jnp.sum(jnp.where(eye, row.astype(F32), 0.0), axis=1, keepdims=True)

    req_col = to_col(req)
    same = req_col == req.astype(F32)
    same_ref[...] = jnp.where(same, 1.0, 0.0)
    slot_row = iota((slots, slots), 1).astype(F32)
    first = jnp.min(jnp.where(same, slot_row, 9999.0), axis=1, keepdims=True)
    leader = first == iota((slots, 1), 0).astype(F32)
    mine = (iota((slots, HD), 1) % 16).astype(F32) == to_col(req % 16)
    mine_ref[...] = jnp.where(mine & leader, 1.0, 0.0)
    lane_total = iota((slots, total), 1).astype(F32)
    pick_ref[...] = jnp.where(to_col(place) == lane_total, 1.0, 0.0).astype(BF16)
    lengths = far[3].get()[...].astype(F32)
    len_col = jnp.sum(jnp.where(req_col == lane_total, lengths, 0.0), axis=1, keepdims=True)
    count = jnp.clip(len_col - to_col(far[1].get()[...]) * page, 0.0, float(page))
    count = jnp.where(to_col(far[2].get()[...]) == 1.0, count, 0.0)
    count_ref[...] = jnp.broadcast_to(count, (slots, HD))


def slot_tables(slot_request, slot_page, slot_used, lengths, kv_cache, after):
    slots = kv_cache.shape[0]
    total = lengths.shape[0]
    return run(
        functools.partial(tables_body, page=kv_cache.shape[2]),
        "slot_tables",
        [
            sds((slots, total), BF16),
            sds((slots, HD), F32),
            sds((slots, slots), F32),
            sds((slots, HD), F32),
            sds((total, slots), BF16),
            sds((total // 2, slots), BF16),
        ],
        [],
        [slot_request.reshape(1, slots), slot_page.reshape(1, slots), slot_used.reshape(1, slots), lengths.reshape(1, total)],
        after=after,
        moves=[kv_cache],
    )


def attn_body(near, far, outs, own):
    pick_ref, count_ref, same_ref, mine_ref, spread_ref, spread8_ref, kv_ref, qa_ref, qb_ref = near
    keep_ref, send_ref = outs
    n_scr, m_scr, l_scr = own
    slots = kv_ref.shape[0]
    page = kv_ref.shape[2]
    half = qa_ref.shape[0] * 16
    qa, qb = (r[:, 0:16, :].reshape(half, 2 * HD) for r in (qa_ref, qb_ref))
    chosen = dot(pick_ref[:, :half], qa) + dot(pick_ref[:, half:], qb)
    low_lanes = iota((8, 2 * HD), 1) < HD
    rel = iota((16, 8 * page), 1) - (iota((16, 8 * page), 0) % 8) * page
    rel = rel.astype(F32)
    for b in range(slots // 8):
        q8 = chosen[b * 8 : b * 8 + 8]
        q16 = jnp.concatenate([jnp.where(low_lanes, q8, 0.0), jnp.where(low_lanes, 0.0, q8)], axis=0).astype(BF16)
        keys = kv_ref[b * 8 : b * 8 + 8, 0].reshape(8 * page, 2 * HD)
        vals = kv_ref[b * 8 : b * 8 + 8, 1].reshape(8 * page, 2 * HD)
        s = lax.dot_general(q16, keys, (((1,), (1,)), ((), ())), preferred_element_type=F32) * SCALE
        c8 = count_ref[b * 8 : b * 8 + 8, :1]
        ok = (rel >= 0.0) & (rel < jnp.concatenate([c8, c8], axis=0))
        s = jnp.where(ok, s, FLOOR)
        m = jnp.max(s, axis=1, keepdims=True)
        w = jnp.where(ok, jnp.exp(s - m), 0.0).astype(BF16)
        l = jnp.sum(w.astype(F32), axis=1, keepdims=True)
        n = dot(w, vals)
        for h in range(2):
            n_scr[h, b * 8 : b * 8 + 8, :] = n[8 * h : 8 * h + 8, HD * h : HD * h + HD]
            m_scr[h, b * 8 : b * 8 + 8, :] = jnp.broadcast_to(m[8 * h : 8 * h + 8], (8, slots))
            l_scr[h, b * 8 : b * 8 + 8, :] = jnp.broadcast_to(l[8 * h : 8 * h + 8], (8, slots))

    eye = iota((slots, slots), 0) == iota((slots, slots), 1)
    same = same_ref[...] > 0.0

    def to_row(wide):
        return jnp.sum(jnp.where(eye, wide, 0.0), axis=0, keepdims=True)

    group = iota((slots, HD), 1) // 16
    board = jnp.zeros((slots, HD), F32)
    for h in range(2):
        m_wide = m_scr[h]
        m_ref = jnp.max(jnp.where(same, to_row(m_wide), FLOOR), axis=1, keepdims=True)
        m_ref = m_ref.astype(BF16).astype(F32)
        lift = jnp.exp(m_wide - m_ref)
        n_hi, n_lo = hi_lo(n_scr[h] * lift)
        l_sum = jnp.sum(jnp.where(same, to_row(l_scr[h] * lift), 0.0), axis=1, keepdims=True)
        out = (dot(spread_ref[...], n_hi) + dot(spread_ref[...], n_lo)).astype(BF16)
        keep_ref[:, 16 * h : 16 * h + 16, :] = out[:half].reshape(half // 16, 16, HD)
        send_ref[:, 16 * h : 16 * h + 16, :] = out[half:].reshape(half // 16, 16, HD)
        l_hi = l_sum.astype(BF16).astype(F32)
        for i, stat in enumerate((m_ref, l_hi, l_sum - l_hi)):
            board = jnp.where(group == 2 * i + h, stat, board)
    board = jnp.where(mine_ref[...] > 0.0, board, 0.0).astype(BF16)
    out = dot(spread8_ref[...], board).astype(BF16)
    keep_ref[:, 32:40, :] = out[: half // 2].reshape(half // 16, 8, HD)
    send_ref[:, 32:40, :] = out[half // 2 :].reshape(half // 16, 8, HD)


def attend_pages(tables, qa, qb):
    slots, total = tables[0].shape
    scratch = [pltpu.VMEM((2, slots, n), F32) for n in (HD, slots, slots)]
    outs = [sds((total // 32, 40, HD), BF16)] * 2
    return run(attn_body, "attend_pages", outs, [*tables, qa, qb], [], scratch)


def merge_body(near, far, outs, own):
    chips = near[0].shape[0] // PIECES
    for piece in range(PIECES):
        part = slice(piece * chips, piece * chips + chips)
        a_ref, b_ref, out_ref = near[0].at[part], near[1].at[part], outs[0].buf.at[part]
        a, b = a_ref[:, 32:40, :].astype(F32), b_ref[:, 32:40, :].astype(F32)
        lane, row = iota(a.shape, 2), iota(a.shape, 1)
        board = jnp.zeros(a.shape, F32)
        for h in range(2):
            (ma, la), (mb, lb) = read_stats(a, h), read_stats(b, h)
            m = jnp.maximum(ma, mb)
            fa, fb = jnp.exp(ma - m), jnp.exp(mb - m)
            rows = slice(16 * h, 16 * h + 16)
            out_ref[:, rows, :] = (a_ref[:, rows, :].astype(F32) * fa + b_ref[:, rows, :].astype(F32) * fb).astype(BF16)
            l = la * fa + lb * fb
            l_hi = l.astype(BF16).astype(F32)
            for i, stat in enumerate((m, l_hi, l - l_hi)):
                for u in range(2):
                    at = row + 8 * u + 32 * i + 16 * h
                    board = jnp.where(lane == at, stat[:, 8 * u : 8 * u + 8], board)
        out_ref[:, 32:40, :] = board.astype(BF16)
        outs[0].send()


def merge(a, b):
    return run(merge_body, "merge", [], [a, b], [], leaving=[sds(a.shape, BF16)])[0]


def fetch(after, *arrays):
    return run(lambda *_: None, "fetch", [], [], [], after=[after], moves=arrays)


def pack_kernel(w_ref, qa_ref, qb_ref, after_ref, *refs):
    outs, res_buf, in_a, in_b, bufs, sems = refs[:4], refs[4], refs[5], refs[6], refs[7:11], refs[11]
    rows, width = bufs[0].shape[0] // 2, bufs[0].shape[1]
    held = res_buf.shape[0]
    reads = [
        pltpu.make_async_copy(qa_ref.at[:, pl.ds(16, 8), :], in_a, sems.at[16]),
        pltpu.make_async_copy(qb_ref.at[:, pl.ds(24, 8), :], in_b, sems.at[17]),
    ]
    for read in reads:
        read.start()
    cuts, writes = [], []
    for k in range(4):
        first = pl.multiple_of(((head_id() + k) % 4) * 2 * width, 2 * width)
        for f in range(2):
            src = w_ref.at[:, pl.ds(first + f * width, width)]
            cuts.append(pltpu.make_async_copy(src, bufs[k].at[pl.ds(f * rows, rows)], sems.at[2 * k + f]))
        writes.append(pltpu.make_async_copy(bufs[k], outs[k].at[pl.ds(held, 2 * rows)], sems.at[8 + k]))
    for cut in cuts:
        cut.start()
    for read in reads:
        read.wait()
    mine, other = in_a[...].astype(F32), in_b[...].astype(F32)
    first = core_id() == 0
    both = [jnp.where(first, mine, other), jnp.where(first, other, mine)]
    res_buf[...] = jnp.stack(both, axis=1).reshape(res_buf.shape).astype(BF16)
    for k in range(4):
        writes.append(pltpu.make_async_copy(res_buf, outs[k].at[pl.ds(0, held)], sems.at[12 + k]))
        writes[-1].start()
    for k in range(4):
        cuts[2 * k].wait()
        cuts[2 * k + 1].wait()
        writes[k].start()
    for write in writes:
        write.wait()


def pack(w_down, qa, qb, after):
    hbm = pl.BlockSpec(memory_space=pltpu.HBM)
    rows, width = w_down.shape[0], w_down.shape[1] // 8
    chips = qa.shape[0]
    held = chips * 16
    return pl.pallas_call(
        pack_kernel,
        name="pack",
        out_shape=[pltpu.HBM((held + 2 * rows, width), BF16)] * 4,
        in_specs=[hbm] * 4,
        out_specs=[hbm] * 4,
        scratch_shapes=[pltpu.VMEM((held, width), BF16)]
        + [pltpu.VMEM((chips, 8, width), BF16)] * 2
        + [pltpu.VMEM((2 * rows, width), BF16)] * 4
        + [pltpu.SemaphoreType.DMA((18,))],
        compiler_params=VLIM,
    )(*pin([w_down, qa, qb, after]))


def cells_body(near, far, outs, own):
    buf = outs[0].buf
    lane = iota((buf.shape[0] // 2, buf.shape[1]), 1)
    buf[...] = cell_map(flip(far[0].get()[...], 1), (lane // 8).astype(F32), lane)


def cells_table(routes, experts, after):
    out = sds((2 * routes.shape[0], experts * 8), BF16)
    return run(cells_body, "cells_table", [], [], [routes.T], after_hbm=[after], leaving=[out])[0]


def mix_body(near, far, outs, own):
    routes, share = flip(far[0].get()[...], 1), flip(far[1].get()[...], 3)
    rows, cells = outs[0].shape
    lane = iota((rows, cells), 1)
    expert = (lane // 4).astype(F32)
    mix = jnp.zeros((rows, cells), F32)
    for k in range(routes.shape[1]):
        mix = mix + jnp.where(routes[:, k : k + 1] == expert, share[:, k : k + 1], 0.0)
    mix = jnp.where(rank_of(hits(routes, expert)) == (lane % 4).astype(F32), mix, 0.0)
    outs[0][...], outs[1][...] = hi_lo(mix)


def mix_table(routes, route_weights, experts, after):
    out = sds((routes.shape[0], experts * 4), BF16)
    return run(mix_body, "mix_table", [out, out], [], [routes.T, route_weights.T], after=[after])


def read_stats(board, h):
    lane, row = iota(board.shape, 2), iota(board.shape, 1)
    ms, ls = [], []
    for u in range(2):
        at = row + 8 * u + 16 * h
        ms.append(jnp.sum(jnp.where(lane == at, board, 0.0), axis=2, keepdims=True))
        ls.append(jnp.sum(jnp.where((lane == at + 32) | (lane == at + 64), board, 0.0), axis=2, keepdims=True))
    m, l = jnp.concatenate(ms, axis=1), jnp.concatenate(ls, axis=1)
    return jnp.where(l > 0.0, m, FLOOR), l


def owner_body(near, far, outs, own_scratch):
    part_ref = near[0]
    att_ref, disp = outs
    board = part_ref[:, 32:40, :].astype(F32)
    stats = [read_stats(board, h) for h in range(2)]
    tops = [jnp.max(m, axis=0) for m, _ in stats]
    q = far[0].get()[...].astype(F32)
    nkv = far[1].get()[...].astype(F32)
    nkv = jnp.concatenate([nkv[:, 0, :], nkv[:, 1, :]], axis=1)
    att = []
    for h, (m, l) in enumerate(stats):
        own = jnp.sum(q[:, HD * h : HD * h + HD] * nkv[:, HD * h : HD * h + HD], axis=1, keepdims=True) * SCALE
        top = jnp.maximum(tops[h], own)
        lift = jnp.exp(m - top[None])
        n = jnp.sum(part_ref[:, 16 * h : 16 * h + 16, :].astype(F32) * lift, axis=0)
        den = jnp.sum(l * lift, axis=0)
        new = jnp.exp(own - top)
        v = nkv[:, 2 * HD + HD * h : 2 * HD + HD * h + HD]
        att.append((n + new * v) / (den + new))
    both = jnp.concatenate(att, axis=0).astype(BF16)
    pick = far[2].get()
    cells = pick.shape[1] // PIECES
    for j in range(PIECES):
        part = pick[:, j * cells : j * cells + cells]
        out = lax.dot_general(part, both, (((0,), (0,)), ((), ())), preferred_element_type=F32)
        disp.buf[j * cells // 8 : (j + 1) * cells // 8] = out.astype(BF16).reshape(cells // 8, 8, HD)
        disp.send()
    att_ref[...] = jnp.concatenate(att, axis=1).astype(BF16)


def owner_part(parts, queries, new_kv, cells, experts):
    outs, leaving = [sds(queries.shape, BF16)], [sds((experts, 8, HD), BF16)]
    return run(owner_body, "owner_part", outs, [parts], [queries, new_kv, cells], leaving=leaving)


def flip(x, terms):
    n = x.shape[1]
    eye = jnp.where(iota((n, n), 0) == iota((n, n), 1), 1.0, 0.0).astype(BF16)
    x = x.astype(F32)
    out = jnp.zeros((n, x.shape[0]), F32)
    for _ in range(terms):
        part = x.astype(BF16)
        out = out + lax.dot_general(eye, part, (((1,), (1,)), ((), ())), preferred_element_type=F32)
        x = x - part.astype(F32)
    return out


def rank_of(hit):
    rows = hit.shape[0]
    before = jnp.where(iota((rows, rows), 0) > iota((rows, rows), 1), 1.0, 0.0).astype(BF16)
    return dot(before, hit.astype(BF16))


def unfold(x):
    n, _, w = x.shape
    x = x.reshape(n // 2, 2, 8, w)
    a, b = x[:, 0], x[:, 1]
    top = iota(a.shape, 1) < 4
    left = jnp.where(top, a, pltpu.roll(b, 4, 1))
    right = jnp.where(top, pltpu.roll(a, 4, 1), b)
    return left.reshape(n * 4, w), right.reshape(n * 4, w)


def fold(left, right):
    rows, w = left.shape
    left, right = left.reshape(rows // 8, 8, w), right.reshape(rows // 8, 8, w)
    top = iota(left.shape, 1) < 4
    a = jnp.where(top, left, pltpu.roll(right, 4, 1))
    b = jnp.where(top, pltpu.roll(left, 4, 1), right)
    return a, b


def head_blocks(size):
    return [pl.multiple_of(((head_id() + 4 - k) % 4) * size, size) for k in range(4)]


def early_body(near, far, outs, own):
    tok_ref = near[0]
    xs, wo = outs
    eff, w = 2 * HD, xs.shape[2]
    att = jnp.concatenate(unfold(tok_ref[...].astype(F32)), axis=1).astype(BF16)
    for k in range(4):
        res = far[k].get()[...].astype(F32)
        xs[2 * k], xs[2 * k + 1] = unfold(res.reshape(res.shape[0] // 8, 8, w))
    wo_ref = wo.get()
    rows = pl.ds(head_blocks(eff)[0], eff)
    for k, first in enumerate(head_blocks(2 * w)):
        for f in range(2):
            xs[2 * k + f] = xs[2 * k + f] + dot(att, wo_ref[rows, pl.ds(first + f * w, w)])


def early_rows(tokens, out_weight, res):
    n = tokens.shape[0]
    w = res[0][0].shape[1]
    return run(early_body, "early_rows", [sds((8, n * 4, w), F32)], [tokens], res, moves=[out_weight])


def expert_body(near, far, outs, own):
    inner_ref, hid = outs
    hs = own[0]
    att, (xs, wo_ref) = near[:3], near[3:]
    gain, mine, own_res, w_gate, w_up = far[0], far[1:5], *far[5:]
    n = inner_ref.shape[0]
    eff = 2 * HD
    w = xs.shape[2]
    att = [jnp.concatenate(unfold(a[...].astype(F32)), axis=1).astype(BF16) for a in att]
    block = head_blocks(eff)
    firsts = [first + f * w for first in head_blocks(2 * w) for f in range(2)]
    total = jnp.zeros((n, 1), F32)
    for j, first in enumerate(firsts):
        acc = xs[j]
        for i in range(3):
            acc = acc + dot(att[i], wo_ref[pl.ds(block[i + 1], eff), pl.ds(first, w)])
        part = acc.astype(BF16)
        hs[j] = part
        part = part.astype(F32)
        total = total + jnp.sum(part * part, axis=1, keepdims=True)
    cols = pl.ds(head_blocks(2 * w)[0], 2 * w)
    acc = own_res.get()[:, cols].astype(F32)
    acc = acc + sum(dot(mine[i].get()[...], wo_ref[pl.ds(block[i], eff), cols]) for i in range(4))
    hid.buf[...] = acc.astype(BF16)
    for _ in range(PIECES):
        hid.send()
    scale = lax.rsqrt(total / (8 * w) + EPS)
    gain_ref = gain.get()
    wg_ref, wu_ref = w_gate.get(), w_up.get()
    gate = jnp.zeros((n, wg_ref.shape[1]), F32)
    up = jnp.zeros((n, wg_ref.shape[1]), F32)
    for j, first in enumerate(firsts):
        normed = (hs[j].astype(F32) * scale * gain_ref[:, pl.ds(first, w)]).astype(BF16)
        gate = gate + dot(normed, wg_ref[pl.ds(first, w), :])
        up = up + dot(normed, wu_ref[pl.ds(first, w), :])
    inner_ref[...] = (gate / (1.0 + jnp.exp(-gate)) * up).astype(BF16)


def expert_rows(tokens, early, out_weight, w_gate, w_up, gain, mine, residual):
    _, n, w = early.shape
    outs, leaving = [sds((n, w_gate.shape[1]), BF16)], [sds((residual.shape[0], 2 * w), BF16)]
    near = [*tokens, early, out_weight]
    scratch = [pltpu.VMEM((8, n, w), BF16)]
    far = [gain.reshape(1, -1), *mine, residual, w_gate, w_up]
    return run(expert_body, "expert_rows", outs, near, far, scratch, leaving=leaving)


def down_body(near, far, outs, own):
    out_ref = outs[0]
    k_rows = near[0].shape[1]
    left = sum(dot(near[k][...], near[4 + k][0:k_rows]) for k in range(4))
    right = sum(dot(near[k][...], near[4 + k][k_rows : 2 * k_rows]) for k in range(4))
    a, b = fold(left, right)
    out_ref[:, 0] = a.astype(BF16)
    out_ref[:, 1] = b.astype(BF16)


def down(inners, w_cols, after):
    rows = inners[0].shape[0]
    width = w_cols[0].shape[1]
    out = run(down_body, "down", [sds((rows // 8, 2, 8, width), BF16)], [*inners, *w_cols], [], after=[after])[0]
    return out.reshape(rows // 4, 8, width)


def blend_body(near, far, outs, own):
    y_ref, hi_ref, low_ref = near
    w = y_ref.shape[2]
    moe = []
    for part in unfold(y_ref[...].astype(F32)):
        part = part.astype(BF16)
        moe.append(dot(hi_ref[...], part) + dot(low_ref[...], part))
    hid_ref = far[0].get()
    for f in range(2):
        cols = slice(f * w, f * w + w)
        outs[0][:, cols] = (hid_ref[:, cols].astype(F32) + moe[f]).astype(BF16)


def blend(returned, mix, hidden):
    return run(blend_body, "blend", [sds(hidden.shape, BF16)], [returned, *mix], [hidden])[0]


def proj_share(x, k, gain_ref, w_ref):
    w = x.shape[1]
    cols = pl.ds(head_blocks(w)[k], w)
    part = (x * gain_ref[:, cols]).astype(BF16)
    return [dot(part, w_ref[i, cols, :]) for i in range(w_ref.shape[0])], jnp.sum(x * x, axis=1, keepdims=True)


def own_proj_body(near, far, outs, own):
    shares, total = proj_share(far[1].get()[...].astype(F32), 0, far[0].get(), near[0])
    for i, share in enumerate(shares):
        outs[0][i] = share
    outs[1][...] = jnp.broadcast_to(total, outs[1].shape)
    outs[2][...] = far[0].get()[...]


def proj_body(near, far, outs, own):
    others, (w_ref, first_ref, total_ref, gain_ref) = near[:3], near[3:]
    total = total_ref[:, 0:1]
    accs = [first_ref[i] for i in range(w_ref.shape[0])]
    for k, s in enumerate(others):
        shares, add = proj_share(s[...].astype(F32), k + 1, gain_ref, w_ref)
        accs, total = [a + b for a, b in zip(accs, shares)], total + add
    scale = lax.rsqrt(total / w_ref.shape[1] + EPS)
    for i, acc in enumerate(accs):
        outs[0][i] = (acc * scale).astype(BF16)


def next_proj(parts, gain, weight):
    kinds, _, width = weight.shape
    rows = parts[0].shape[0]
    shape = (kinds, rows, width)
    gain = gain.reshape(1, -1)
    outs = [sds(shape, F32), sds((rows, HD), F32), sds(gain.shape, F32)]
    first = run(own_proj_body, "own_proj", outs, [weight], [gain, parts[0]])
    return run(proj_body, "next_proj", [sds(shape, BF16)], [*parts[1:], weight, *first], [])[0]


def from_heads(x):
    n = lax.axis_size("head")
    return [x] + [lax.ppermute(x, "head", [(i, (i + k) % n) for i in range(n)]) for k in range(1, n)]


def to_heads(xs):
    n = lax.axis_size("head")
    return [xs[0]] + [lax.ppermute(xs[k], "head", [(i, (i + k) % n) for i in range(n)]) for k in range(1, n)]


def swap_core(x):
    return lax.ppermute(x, "c", [(0, 1), (1, 0)])


def local(
    residual, queries, new_kv, kv_cache, lengths, slot_request, slot_page, slot_used, out_weight,
    norm_gain, routes, route_weights, w_gate, w_up, w_down, next_gain, next_weight,
):
    rows = queries.shape[0]
    experts = lax.axis_size(REQ)
    chips = experts // 2
    out_weight = lax.all_gather(out_weight, "head", axis=0, tiled=True)
    qa = lax.all_to_all(outset(queries, residual, routes, chips), ("z", "y"), 0, 0, tiled=True)
    tables = slot_tables(slot_request, slot_page, slot_used, lengths, kv_cache, [qa])
    qb = swap_core(qa)
    keep, send = attend_pages(tables, qa, qb)
    merged = merge(keep, swap_core(send))
    packs = to_heads(pack(w_down[0], qa, qb, merged))
    cells = cells_table(routes, experts, merged)
    arrived = lax.all_to_all(merged, ("z", "y"), 0, 0, tiled=True)
    arrived, cells = lax.optimization_barrier((arrived, cells))
    attended, disp = owner_part(arrived, queries, new_kv, cells, experts)
    tokens = lax.all_to_all(disp, REQ, 0, 0, tiled=True)
    mine = from_heads(attended)
    tokens, mine, packs = lax.optimization_barrier((tokens, mine, packs))
    held = experts * 8
    res = [(p, 0, held) for p in packs]
    early, out_weight = early_rows(tokens, out_weight, res)
    others = from_heads(tokens)[1:]
    inner, hidden = expert_rows(others, early, out_weight, w_gate[0], w_up[0], norm_gain, mine, residual)
    w_cols = fetch(inner, *[(p, held, p.shape[0] - held) for p in packs])
    mix = mix_table(routes, route_weights, experts, inner)
    expert_out = down(from_heads(inner), w_cols, mix[0])
    returned = lax.all_to_all(expert_out, REQ, 0, 0, tiled=True)
    stream = blend(returned, mix, hidden)
    next_qkv = next_proj(from_heads(stream), next_gain, next_weight.transpose(1, 0, 2)).transpose(1, 0, 2)
    return stream, next_qkv


def solution(mesh):
    split = Mesh(mesh.devices.reshape(8, 4, 2, 4), ("z", "y", "c", "head"))
    placed = (
        P(REQ, None),
        P(REQ, "head"),
        P(REQ, None, "head"),
        P(REQ, None, None, "head"),
        P(),
        P(REQ),
        P(REQ),
        P(REQ),
        P("head", None),
        P(),
        P(REQ, None),
        P(REQ, None),
        P(REQ, None, "head"),
        P(REQ, None, "head"),
        P(REQ, "head", None),
        P(),
        P(None, None, "head"),
    )
    return jax.shard_map(
        local,
        mesh=split,
        in_specs=placed,
        out_specs=(P(REQ, "head"), P(REQ, None, "head")),
        check_vma=False,
    )
```

```python
import functools
import math

import jax
import jax.numpy as jnp
from jax import lax
from jax.experimental import pallas as pl
from jax.experimental.pallas import tpu as pltpu
from jax.sharding import Mesh, PartitionSpec as P

HD = 128
EPS = 1e-06
FLOOR = -(2.0**99)
SCALE = 1.0 / math.sqrt(HD)
F32 = jnp.float32
BF16 = jnp.bfloat16
REQ = ("z", "y", "c")
VLIM = pltpu.CompilerParams(vmem_limit_bytes=24 * 1024 * 1024)
VM = pl.BlockSpec(memory_space=pltpu.VMEM)


class Pending:
    def __init__(self, buf, copy):
        self.buf, self.copy, self.done = buf, copy, False

    def get(self):
        if not self.done:
            self.copy.wait()
            self.done = True
        return self.buf


def pin(xs):
    return [pltpu.with_memory_space_constraint(x, pltpu.HBM) for x in xs]


PIECES = 4


class Leaving:
    def __init__(self, buf, out, sems, base):
        rows = buf.shape[0] // PIECES
        parts = [pl.ds(j * rows, rows) for j in range(PIECES)]
        self.buf, self.sent = buf, 0
        self.copies = [pltpu.make_async_copy(buf.at[p], out.at[p], sems.at[base + j]) for j, p in enumerate(parts)]

    def send(self):
        self.copies[self.sent].start()
        self.sent += 1

    def finish(self):
        while self.sent < PIECES:
            self.send()
        for copy in self.copies:
            copy.wait()


class Moved:
    def __init__(self, buf, copies):
        self.buf, self.copies, self.done = buf, copies, False

    def get(self):
        if not self.done:
            for copy in self.copies:
                copy.wait()
            self.done = True
        return self.buf


def part_of(x):
    return x if isinstance(x, tuple) else (x, 0, x.shape[0])


def run(body, name, outs, near, far, scratch=(), after=(), moves=(), leaving=(), after_hbm=()):
    after = [*after, *pin(after_hbm)]
    far, moves = [part_of(x) for x in far], [part_of(x) for x in moves]
    na, nh, nn, nf, nm = len(after), len(after_hbm), len(near), len(far), len(moves)
    no, nl = len(outs), len(leaving)

    def kernel(*refs):
        ins, refs = refs[: nn + nf + na + nm], refs[nn + nf + na + nm :]
        outputs, out_hbm, moved = refs[:no], refs[no : no + nl], refs[no + nl : no + nl + nm]
        rest = refs[no + nl + nm :]
        bufs, out_bufs, rest = rest[:nf], rest[nf : nf + nl], rest[nf + nl :]
        sems, move_sems, out_sems, own = rest[0], rest[1], rest[2], rest[3:]
        pending = []
        for i, (x, first, rows) in enumerate(far):
            src = ins[nn + i] if rows == x.shape[0] else ins[nn + i].at[pl.ds(first, rows)]
            copy = pltpu.make_async_copy(src, bufs[i], sems.at[i])
            copy.start()
            pending.append(Pending(bufs[i], copy))
        moving = []
        for i, (x, first, rows) in enumerate(moves):
            rows, copies = rows // PIECES, []
            for j in range(PIECES):
                src = ins[nn + nf + na + i].at[pl.ds(first + j * rows, rows)]
                dst = moved[i].at[pl.ds(j * rows, rows)]
                copies.append(pltpu.make_async_copy(src, dst, move_sems.at[PIECES * i + j]))
                copies[-1].start()
            moving.append(Moved(moved[i], copies))
        going = [Leaving(out_bufs[i], out_hbm[i], out_sems, PIECES * i) for i in range(nl)]
        body(ins[:nn], pending, (*outputs, *going, *moving), own)
        for p in pending:
            p.get()
        for g in going:
            g.finish()
        for m in moving:
            m.get()

    hbm, any_space = pl.BlockSpec(memory_space=pltpu.HBM), pl.BlockSpec(memory_space=pl.ANY)
    far_shapes = [((r,) + x.shape[1:], x.dtype) for x, _, r in far]
    return pl.pallas_call(
        kernel,
        name=name,
        out_shape=list(outs)
        + [pltpu.HBM(x.shape, x.dtype) for x in leaving]
        + [sds((r,) + x.shape[1:], x.dtype) for x, _, r in moves],
        in_specs=[VM] * nn + [hbm] * nf + [any_space] * (na - nh) + [hbm] * (nh + nm),
        out_specs=[VM] * no + [hbm] * nl + [VM] * nm,
        scratch_shapes=[pltpu.VMEM(*f) for f in far_shapes]
        + [pltpu.VMEM(x.shape, x.dtype) for x in leaving]
        + [pltpu.SemaphoreType.DMA((max(n, 1),)) for n in (nf, nm * PIECES, nl * PIECES)]
        + list(scratch),
        compiler_params=VLIM,
    )(*near, *pin([x for x, _, _ in far]), *after, *pin([x for x, _, _ in moves]))


def sds(shape, dtype):
    return jax.ShapeDtypeStruct(shape, dtype)


def iota(shape, dim):
    return lax.broadcasted_iota(jnp.int32, shape, dim)


def core_id():
    return lax.axis_index("c")


def head_id():
    return lax.axis_index("head")


def dot(a, b):
    return jnp.dot(a, b, preferred_element_type=F32)


def hi_lo(x):
    hi = x.astype(BF16)
    return hi, (x - hi.astype(F32)).astype(BF16)


def hits(routes, expert):
    hit = jnp.zeros(expert.shape, F32)
    for k in range(routes.shape[1]):
        hit = hit + jnp.where(routes[:, k : k + 1] == expert, 1.0, 0.0)
    return hit


def cell_map(routes, expert, lane):
    hit = hits(routes, expert)
    hit = jnp.where(rank_of(hit) == (lane % 4).astype(F32), hit, 0.0)
    left = lane % 8 < 4
    return jnp.concatenate([jnp.where(left, hit, 0.0), jnp.where(left, 0.0, hit)], axis=0).astype(BF16)


def outset_body(near, far, outs, own):
    chips, _, width = outs[0].shape
    rows = far[0].buf.shape[0]
    routes = flip(far[2].get()[...], 1)
    lane = iota((rows, chips * 16), 1)
    expert = (lane // 16) * 2 + (core_id() + (lane // 8) % 2) % 2
    pick = cell_map(routes, expert.astype(F32), lane)
    first = pl.multiple_of(head_id() * 2 * width, 2 * width)
    res = far[1].get()
    both = jnp.concatenate([res[:, pl.ds(first, width)], res[:, pl.ds(first + width, width)]], axis=0)
    out = lax.dot_general(pick, both, (((0,), (0,)), ((), ())), preferred_element_type=F32)
    outs[0][:, 16:32, :] = out.astype(BF16).reshape(chips, 16, width)
    q = far[0].get()[...]
    outs[0][:, 0:16, :] = jnp.broadcast_to(q[None], (chips,) + q.shape)


def outset(queries, residual, routes, chips):
    out = sds((chips, 32, queries.shape[1]), BF16)
    return run(outset_body, "outset", [out], [], [queries, residual, routes.T])[0]


def tables_body(near, far, outs, own, page):
    pick_ref, count_ref, same_ref, mine_ref, spread_ref, spread8_ref = outs[:6]
    req = far[0].get()[...]
    slots, total = pick_ref.shape
    half = total // 2
    place = jnp.where((req // 16) % 2 == core_id(), 0, half) + (req // 32) * 16 + req % 16
    spread_ref[...] = jnp.where(iota((total, slots), 0) == place, 1.0, 0.0).astype(BF16)
    owners = jnp.where(iota((half, slots), 0) // 8 == place // 16, 1.0, 0.0)
    spread8_ref[...] = owners.astype(BF16)
    eye = iota((slots, slots), 0) == iota((slots, slots), 1)

    def to_col(row):
        return jnp.sum(jnp.where(eye, row.astype(F32), 0.0), axis=1, keepdims=True)

    req_col = to_col(req)
    same = req_col == req.astype(F32)
    same_ref[...] = jnp.where(same, 1.0, 0.0)
    slot_row = iota((slots, slots), 1).astype(F32)
    first = jnp.min(jnp.where(same, slot_row, 9999.0), axis=1, keepdims=True)
    leader = first == iota((slots, 1), 0).astype(F32)
    mine = (iota((slots, HD), 1) % 16).astype(F32) == to_col(req % 16)
    mine_ref[...] = jnp.where(mine & leader, 1.0, 0.0)
    lane_total = iota((slots, total), 1).astype(F32)
    pick_ref[...] = jnp.where(to_col(place) == lane_total, 1.0, 0.0).astype(BF16)
    lengths = far[3].get()[...].astype(F32)
    len_col = jnp.sum(jnp.where(req_col == lane_total, lengths, 0.0), axis=1, keepdims=True)
    count = jnp.clip(len_col - to_col(far[1].get()[...]) * page, 0.0, float(page))
    count = jnp.where(to_col(far[2].get()[...]) == 1.0, count, 0.0)
    count_ref[...] = jnp.broadcast_to(count, (slots, HD))


def slot_tables(slot_request, slot_page, slot_used, lengths, kv_cache, after):
    slots = kv_cache.shape[0]
    total = lengths.shape[0]
    return run(
        functools.partial(tables_body, page=kv_cache.shape[2]),
        "slot_tables",
        [
            sds((slots, total), BF16),
            sds((slots, HD), F32),
            sds((slots, slots), F32),
            sds((slots, HD), F32),
            sds((total, slots), BF16),
            sds((total // 2, slots), BF16),
        ],
        [],
        [slot_request.reshape(1, slots), slot_page.reshape(1, slots), slot_used.reshape(1, slots), lengths.reshape(1, total)],
        after=after,
        moves=[kv_cache],
    )


def attn_body(near, far, outs, own):
    pick_ref, count_ref, same_ref, mine_ref, spread_ref, spread8_ref, kv_ref, qa_ref, qb_ref = near
    keep_ref, send_ref = outs
    n_scr, m_scr, l_scr = own
    slots = kv_ref.shape[0]
    page = kv_ref.shape[2]
    half = qa_ref.shape[0] * 16
    qa, qb = (r[:, 0:16, :].reshape(half, 2 * HD) for r in (qa_ref, qb_ref))
    chosen = dot(pick_ref[:, :half], qa) + dot(pick_ref[:, half:], qb)
    low_lanes = iota((8, 2 * HD), 1) < HD
    rel = iota((16, 8 * page), 1) - (iota((16, 8 * page), 0) % 8) * page
    rel = rel.astype(F32)
    for b in range(slots // 8):
        q8 = chosen[b * 8 : b * 8 + 8]
        q16 = jnp.concatenate([jnp.where(low_lanes, q8, 0.0), jnp.where(low_lanes, 0.0, q8)], axis=0).astype(BF16)
        keys = kv_ref[b * 8 : b * 8 + 8, 0].reshape(8 * page, 2 * HD)
        vals = kv_ref[b * 8 : b * 8 + 8, 1].reshape(8 * page, 2 * HD)
        s = lax.dot_general(q16, keys, (((1,), (1,)), ((), ())), preferred_element_type=F32) * SCALE
        c8 = count_ref[b * 8 : b * 8 + 8, :1]
        ok = (rel >= 0.0) & (rel < jnp.concatenate([c8, c8], axis=0))
        s = jnp.where(ok, s, FLOOR)
        m = jnp.max(s, axis=1, keepdims=True)
        w = jnp.where(ok, jnp.exp(s - m), 0.0).astype(BF16)
        l = jnp.sum(w.astype(F32), axis=1, keepdims=True)
        n = dot(w, vals)
        for h in range(2):
            n_scr[h, b * 8 : b * 8 + 8, :] = n[8 * h : 8 * h + 8, HD * h : HD * h + HD]
            m_scr[h, b * 8 : b * 8 + 8, :] = jnp.broadcast_to(m[8 * h : 8 * h + 8], (8, slots))
            l_scr[h, b * 8 : b * 8 + 8, :] = jnp.broadcast_to(l[8 * h : 8 * h + 8], (8, slots))

    eye = iota((slots, slots), 0) == iota((slots, slots), 1)
    same = same_ref[...] > 0.0

    def to_row(wide):
        return jnp.sum(jnp.where(eye, wide, 0.0), axis=0, keepdims=True)

    group = iota((slots, HD), 1) // 16
    board = jnp.zeros((slots, HD), F32)
    for h in range(2):
        m_wide = m_scr[h]
        m_ref = jnp.max(jnp.where(same, to_row(m_wide), FLOOR), axis=1, keepdims=True)
        m_ref = m_ref.astype(BF16).astype(F32)
        lift = jnp.exp(m_wide - m_ref)
        n_hi, n_lo = hi_lo(n_scr[h] * lift)
        l_sum = jnp.sum(jnp.where(same, to_row(l_scr[h] * lift), 0.0), axis=1, keepdims=True)
        out = (dot(spread_ref[...], n_hi) + dot(spread_ref[...], n_lo)).astype(BF16)
        keep_ref[:, 16 * h : 16 * h + 16, :] = out[:half].reshape(half // 16, 16, HD)
        send_ref[:, 16 * h : 16 * h + 16, :] = out[half:].reshape(half // 16, 16, HD)
        l_hi = l_sum.astype(BF16).astype(F32)
        for i, stat in enumerate((m_ref, l_hi, l_sum - l_hi)):
            board = jnp.where(group == 2 * i + h, stat, board)
    board = jnp.where(mine_ref[...] > 0.0, board, 0.0).astype(BF16)
    out = dot(spread8_ref[...], board).astype(BF16)
    keep_ref[:, 32:40, :] = out[: half // 2].reshape(half // 16, 8, HD)
    send_ref[:, 32:40, :] = out[half // 2 :].reshape(half // 16, 8, HD)


def attend_pages(tables, qa, qb):
    slots, total = tables[0].shape
    scratch = [pltpu.VMEM((2, slots, n), F32) for n in (HD, slots, slots)]
    outs = [sds((total // 32, 40, HD), BF16)] * 2
    return run(attn_body, "attend_pages", outs, [*tables, qa, qb], [], scratch)


def merge_body(near, far, outs, own):
    chips = near[0].shape[0] // PIECES
    for piece in range(PIECES):
        part = slice(piece * chips, piece * chips + chips)
        a_ref, b_ref, out_ref = near[0].at[part], near[1].at[part], outs[0].buf.at[part]
        a, b = a_ref[:, 32:40, :].astype(F32), b_ref[:, 32:40, :].astype(F32)
        lane, row = iota(a.shape, 2), iota(a.shape, 1)
        board = jnp.zeros(a.shape, F32)
        for h in range(2):
            (ma, la), (mb, lb) = read_stats(a, h), read_stats(b, h)
            m = jnp.maximum(ma, mb)
            fa, fb = jnp.exp(ma - m), jnp.exp(mb - m)
            rows = slice(16 * h, 16 * h + 16)
            out_ref[:, rows, :] = (a_ref[:, rows, :].astype(F32) * fa + b_ref[:, rows, :].astype(F32) * fb).astype(BF16)
            l = la * fa + lb * fb
            l_hi = l.astype(BF16).astype(F32)
            for i, stat in enumerate((m, l_hi, l - l_hi)):
                for u in range(2):
                    at = row + 8 * u + 32 * i + 16 * h
                    board = jnp.where(lane == at, stat[:, 8 * u : 8 * u + 8], board)
        out_ref[:, 32:40, :] = board.astype(BF16)
        outs[0].send()


def merge(a, b):
    return run(merge_body, "merge", [], [a, b], [], leaving=[sds(a.shape, BF16)])[0]


def fetch(after, *arrays):
    return run(lambda *_: None, "fetch", [], [], [], after=[after], moves=arrays)


def pack_kernel(w_ref, qa_ref, qb_ref, after_ref, *refs):
    outs, far_block, refs = refs[:4], refs[4], refs[5:]
    res_buf, in_a, in_b, bufs, sems = refs[0], refs[1], refs[2], refs[3:7], refs[7]
    rows, width = bufs[0].shape[0] // 2, bufs[0].shape[1]
    held = res_buf.shape[0]
    reads = [
        pltpu.make_async_copy(qa_ref.at[:, pl.ds(16, 8), :], in_a, sems.at[16]),
        pltpu.make_async_copy(qb_ref.at[:, pl.ds(24, 8), :], in_b, sems.at[17]),
    ]
    for read in reads:
        read.start()
    cuts, writes = [], []
    for k in range(4):
        first = pl.multiple_of(((head_id() + k) % 4) * 2 * width, 2 * width)
        for f in range(2):
            src = w_ref.at[:, pl.ds(first + f * width, width)]
            cuts.append(pltpu.make_async_copy(src, bufs[k].at[pl.ds(f * rows, rows)], sems.at[2 * k + f]))
        block = far_block if k == 2 else outs[k].at[pl.ds(held, 2 * rows)]
        writes.append(pltpu.make_async_copy(bufs[k], block, sems.at[8 + k]))
    for cut in cuts:
        cut.start()
    for read in reads:
        read.wait()
    mine, other = in_a[...].astype(F32), in_b[...].astype(F32)
    first = core_id() == 0
    both = [jnp.where(first, mine, other), jnp.where(first, other, mine)]
    res_buf[...] = jnp.stack(both, axis=1).reshape(res_buf.shape).astype(BF16)
    for k in range(4):
        writes.append(pltpu.make_async_copy(res_buf, outs[k].at[pl.ds(0, held)], sems.at[12 + k]))
        writes[-1].start()
    for k in range(4):
        cuts[2 * k].wait()
        cuts[2 * k + 1].wait()
        writes[k].start()
    for write in writes:
        write.wait()


def pack(w_down, qa, qb, after):
    hbm = pl.BlockSpec(memory_space=pltpu.HBM)
    rows, width = w_down.shape[0], w_down.shape[1] // 8
    chips = qa.shape[0]
    held = chips * 16
    return pl.pallas_call(
        pack_kernel,
        name="pack",
        out_shape=[pltpu.HBM((held + (0 if k == 2 else 2 * rows), width), BF16) for k in range(4)]
        + [pltpu.HBM((2 * rows, width), BF16)],
        in_specs=[hbm] * 4,
        out_specs=[hbm] * 5,
        scratch_shapes=[pltpu.VMEM((held, width), BF16)]
        + [pltpu.VMEM((chips, 8, width), BF16)] * 2
        + [pltpu.VMEM((2 * rows, width), BF16)] * 4
        + [pltpu.SemaphoreType.DMA((18,))],
        compiler_params=VLIM,
    )(*pin([w_down, qa, qb, after]))


def cells_body(near, far, outs, own):
    buf = outs[0].buf
    lane = iota((buf.shape[0] // 2, buf.shape[1]), 1)
    buf[...] = cell_map(flip(far[0].get()[...], 1), (lane // 8).astype(F32), lane)


def cells_table(routes, experts, after):
    out = sds((2 * routes.shape[0], experts * 8), BF16)
    return run(cells_body, "cells_table", [], [], [routes.T], after_hbm=[after], leaving=[out])[0]


def mix_body(near, far, outs, own):
    routes, share = flip(far[0].get()[...], 1), flip(far[1].get()[...], 3)
    rows, cells = outs[0].shape
    lane = iota((rows, cells), 1)
    expert = (lane // 4).astype(F32)
    mix = jnp.zeros((rows, cells), F32)
    for k in range(routes.shape[1]):
        mix = mix + jnp.where(routes[:, k : k + 1] == expert, share[:, k : k + 1], 0.0)
    mix = jnp.where(rank_of(hits(routes, expert)) == (lane % 4).astype(F32), mix, 0.0)
    outs[0][...], outs[1][...] = hi_lo(mix)


def mix_table(routes, route_weights, experts, after):
    out = sds((routes.shape[0], experts * 4), BF16)
    return run(mix_body, "mix_table", [out, out], [], [routes.T, route_weights.T], after=[after])


def read_stats(board, h):
    lane, row = iota(board.shape, 2), iota(board.shape, 1)
    ms, ls = [], []
    for u in range(2):
        at = row + 8 * u + 16 * h
        ms.append(jnp.sum(jnp.where(lane == at, board, 0.0), axis=2, keepdims=True))
        ls.append(jnp.sum(jnp.where((lane == at + 32) | (lane == at + 64), board, 0.0), axis=2, keepdims=True))
    m, l = jnp.concatenate(ms, axis=1), jnp.concatenate(ls, axis=1)
    return jnp.where(l > 0.0, m, FLOOR), l


def owner_body(near, far, outs, own_scratch):
    part_ref = near[0]
    att_ref, disp = outs
    board = part_ref[:, 32:40, :].astype(F32)
    stats = [read_stats(board, h) for h in range(2)]
    tops = [jnp.max(m, axis=0) for m, _ in stats]
    q = far[0].get()[...].astype(F32)
    nkv = far[1].get()[...].astype(F32)
    nkv = jnp.concatenate([nkv[:, 0, :], nkv[:, 1, :]], axis=1)
    att = []
    for h, (m, l) in enumerate(stats):
        own = jnp.sum(q[:, HD * h : HD * h + HD] * nkv[:, HD * h : HD * h + HD], axis=1, keepdims=True) * SCALE
        top = jnp.maximum(tops[h], own)
        lift = jnp.exp(m - top[None])
        n = jnp.sum(part_ref[:, 16 * h : 16 * h + 16, :].astype(F32) * lift, axis=0)
        den = jnp.sum(l * lift, axis=0)
        new = jnp.exp(own - top)
        v = nkv[:, 2 * HD + HD * h : 2 * HD + HD * h + HD]
        att.append((n + new * v) / (den + new))
    both = jnp.concatenate(att, axis=0).astype(BF16)
    pick = far[2].get()
    cells = pick.shape[1] // PIECES
    for j in range(PIECES):
        part = pick[:, j * cells : j * cells + cells]
        out = lax.dot_general(part, both, (((0,), (0,)), ((), ())), preferred_element_type=F32)
        disp.buf[j * cells // 8 : (j + 1) * cells // 8] = out.astype(BF16).reshape(cells // 8, 8, HD)
        disp.send()
    att_ref[...] = jnp.concatenate(att, axis=1).astype(BF16)


def owner_part(parts, queries, new_kv, cells, experts):
    outs, leaving = [sds(queries.shape, BF16)], [sds((experts, 8, HD), BF16)]
    return run(owner_body, "owner_part", outs, [parts], [queries, new_kv, cells], leaving=leaving)


def flip(x, terms):
    n = x.shape[1]
    eye = jnp.where(iota((n, n), 0) == iota((n, n), 1), 1.0, 0.0).astype(BF16)
    x = x.astype(F32)
    out = jnp.zeros((n, x.shape[0]), F32)
    for _ in range(terms):
        part = x.astype(BF16)
        out = out + lax.dot_general(eye, part, (((1,), (1,)), ((), ())), preferred_element_type=F32)
        x = x - part.astype(F32)
    return out


def rank_of(hit):
    rows = hit.shape[0]
    before = jnp.where(iota((rows, rows), 0) > iota((rows, rows), 1), 1.0, 0.0).astype(BF16)
    return dot(before, hit.astype(BF16))


def unfold(x):
    n, _, w = x.shape
    x = x.reshape(n // 2, 2, 8, w)
    a, b = x[:, 0], x[:, 1]
    top = iota(a.shape, 1) < 4
    left = jnp.where(top, a, pltpu.roll(b, 4, 1))
    right = jnp.where(top, pltpu.roll(a, 4, 1), b)
    return left.reshape(n * 4, w), right.reshape(n * 4, w)


def fold(left, right):
    rows, w = left.shape
    left, right = left.reshape(rows // 8, 8, w), right.reshape(rows // 8, 8, w)
    top = iota(left.shape, 1) < 4
    a = jnp.where(top, left, pltpu.roll(right, 4, 1))
    b = jnp.where(top, pltpu.roll(left, 4, 1), right)
    return a, b


def head_blocks(size):
    return [pl.multiple_of(((head_id() + 4 - k) % 4) * size, size) for k in range(4)]


def early_body(near, far, outs, own):
    tok_ref = near[0]
    xs, wo = outs
    eff, w = 2 * HD, xs.shape[2]
    att = jnp.concatenate(unfold(tok_ref[...].astype(F32)), axis=1).astype(BF16)
    for k in range(4):
        res = far[k].get()[...].astype(F32)
        xs[2 * k], xs[2 * k + 1] = unfold(res.reshape(res.shape[0] // 8, 8, w))
    wo_ref = wo.get()
    rows = pl.ds(head_blocks(eff)[0], eff)
    for k, first in enumerate(head_blocks(2 * w)):
        for f in range(2):
            xs[2 * k + f] = xs[2 * k + f] + dot(att, wo_ref[rows, pl.ds(first + f * w, w)])


def early_rows(tokens, out_weight, res):
    n = tokens.shape[0]
    w = res[0][0].shape[1]
    return run(early_body, "early_rows", [sds((8, n * 4, w), F32)], [tokens], res, moves=[out_weight])


def expert_body(near, far, outs, own):
    inner_ref, hid = outs
    hs = own[0]
    att, (xs, wo_ref) = near[:3], near[3:]
    gain, mine, own_res, w_gate, w_up = far[0], far[1:5], *far[5:]
    n = inner_ref.shape[0]
    eff = 2 * HD
    w = xs.shape[2]
    att = [jnp.concatenate(unfold(a[...].astype(F32)), axis=1).astype(BF16) for a in att]
    block = head_blocks(eff)
    firsts = [first + f * w for first in head_blocks(2 * w) for f in range(2)]
    cols = pl.ds(head_blocks(2 * w)[0], 2 * w)
    acc = own_res.get()[:, cols].astype(F32)
    acc = acc + sum(dot(mine[i].get()[...], wo_ref[pl.ds(block[i], eff), cols]) for i in range(4))
    hid.buf[...] = acc.astype(BF16)
    for _ in range(PIECES):
        hid.send()
    total = jnp.zeros((n, 1), F32)
    for j, first in enumerate(firsts):
        acc = xs[j]
        for i in range(3):
            acc = acc + dot(att[i], wo_ref[pl.ds(block[i + 1], eff), pl.ds(first, w)])
        part = acc.astype(BF16)
        hs[j] = part
        part = part.astype(F32)
        total = total + jnp.sum(part * part, axis=1, keepdims=True)
    scale = lax.rsqrt(total / (8 * w) + EPS)
    gain_ref = gain.get()
    wg_ref, wu_ref = w_gate.get(), w_up.get()
    gate = jnp.zeros((n, wg_ref.shape[1]), F32)
    up = jnp.zeros((n, wg_ref.shape[1]), F32)
    for j, first in enumerate(firsts):
        normed = (hs[j].astype(F32) * scale * gain_ref[:, pl.ds(first, w)]).astype(BF16)
        gate = gate + dot(normed, wg_ref[pl.ds(first, w), :])
        up = up + dot(normed, wu_ref[pl.ds(first, w), :])
    inner_ref[...] = (gate / (1.0 + jnp.exp(-gate)) * up).astype(BF16)


def expert_rows(tokens, early, out_weight, w_gate, w_up, gain, mine, residual):
    _, n, w = early.shape
    outs, leaving = [sds((n, w_gate.shape[1]), BF16)], [sds((residual.shape[0], 2 * w), BF16)]
    near = [*tokens, early, out_weight]
    scratch = [pltpu.VMEM((8, n, w), BF16)]
    far = [gain.reshape(1, -1), *mine, residual, w_gate, w_up]
    return run(expert_body, "expert_rows", outs, near, far, scratch, leaving=leaving)


def down_body(near, far, outs, own):
    out_ref = outs[0]
    k_rows = near[0].shape[1]
    left = sum(dot(near[k][...], near[4 + k][0:k_rows]) for k in range(4))
    right = sum(dot(near[k][...], near[4 + k][k_rows : 2 * k_rows]) for k in range(4))
    a, b = fold(left, right)
    out_ref[:, 0] = a.astype(BF16)
    out_ref[:, 1] = b.astype(BF16)


def down(inners, w_cols, after):
    rows = inners[0].shape[0]
    width = w_cols[0].shape[1]
    out = run(down_body, "down", [sds((rows // 8, 2, 8, width), BF16)], [*inners, *w_cols], [], after=[after])[0]
    return out.reshape(rows // 4, 8, width)


def blend_body(near, far, outs, own):
    y_ref, hi_ref, low_ref = near
    w = y_ref.shape[2]
    moe = []
    for part in unfold(y_ref[...].astype(F32)):
        part = part.astype(BF16)
        moe.append(dot(hi_ref[...], part) + dot(low_ref[...], part))
    hid_ref = far[0].get()
    for f in range(2):
        cols = slice(f * w, f * w + w)
        outs[0][:, cols] = (hid_ref[:, cols].astype(F32) + moe[f]).astype(BF16)


def blend(returned, mix, hidden):
    return run(blend_body, "blend", [sds(hidden.shape, BF16)], [returned, *mix], [hidden])[0]


def proj_share(x, k, gain_ref, w_ref):
    w = x.shape[1]
    cols = pl.ds(head_blocks(w)[k], w)
    part = (x * gain_ref[:, cols]).astype(BF16)
    return [dot(part, w_ref[i, cols, :]) for i in range(w_ref.shape[0])], jnp.sum(x * x, axis=1, keepdims=True)


def own_proj_body(near, far, outs, own):
    shares, total = proj_share(far[1].get()[...].astype(F32), 0, far[0].get(), near[0])
    for i, share in enumerate(shares):
        outs[0][i] = share
    outs[1][...] = jnp.broadcast_to(total, outs[1].shape)
    outs[2][...] = far[0].get()[...]


def proj_body(near, far, outs, own):
    others, (w_ref, first_ref, total_ref, gain_ref) = near[:3], near[3:]
    total = total_ref[:, 0:1]
    accs = [first_ref[i] for i in range(w_ref.shape[0])]
    for k, s in enumerate(others):
        shares, add = proj_share(s[...].astype(F32), k + 1, gain_ref, w_ref)
        accs, total = [a + b for a, b in zip(accs, shares)], total + add
    scale = lax.rsqrt(total / w_ref.shape[1] + EPS)
    for i, acc in enumerate(accs):
        outs[0][i] = (acc * scale).astype(BF16)


def next_proj(parts, gain, weight):
    kinds, _, width = weight.shape
    rows = parts[0].shape[0]
    shape = (kinds, rows, width)
    gain = gain.reshape(1, -1)
    outs = [sds(shape, F32), sds((rows, HD), F32), sds(gain.shape, F32)]
    first = run(own_proj_body, "own_proj", outs, [weight], [gain, parts[0]])
    return run(proj_body, "next_proj", [sds(shape, BF16)], [*parts[1:], weight, *first], [])[0]


def from_heads(x):
    n = lax.axis_size("head")
    return [x] + [lax.ppermute(x, "head", [(i, (i + k) % n) for i in range(n)]) for k in range(1, n)]


def to_heads(xs):
    n = lax.axis_size("head")
    return [xs[0]] + [lax.ppermute(xs[k], "head", [(i, (i + k) % n) for i in range(n)]) for k in range(1, n)]


def swap_core(x):
    return lax.ppermute(x, "c", [(0, 1), (1, 0)])


def local(
    residual, queries, new_kv, kv_cache, lengths, slot_request, slot_page, slot_used, out_weight,
    norm_gain, routes, route_weights, w_gate, w_up, w_down, next_gain, next_weight,
):
    rows = queries.shape[0]
    experts = lax.axis_size(REQ)
    chips = experts // 2
    out_weight = lax.all_gather(out_weight, "head", axis=0, tiled=True)
    qa = lax.all_to_all(outset(queries, residual, routes, chips), ("z", "y"), 0, 0, tiled=True)
    tables = slot_tables(slot_request, slot_page, slot_used, lengths, kv_cache, [qa])
    qb = swap_core(qa)
    keep, send = attend_pages(tables, qa, qb)
    merged = merge(keep, swap_core(send))
    *packs, block = pack(w_down[0], qa, qb, merged)
    packs = to_heads(packs)
    for _ in range(2):
        block = lax.ppermute(block, "head", [(i, (i + 3) % 4) for i in range(4)])
    cells = cells_table(routes, experts, merged)
    arrived = lax.all_to_all(merged, ("z", "y"), 0, 0, tiled=True)
    arrived, cells = lax.optimization_barrier((arrived, cells))
    attended, disp = owner_part(arrived, queries, new_kv, cells, experts)
    tokens = lax.all_to_all(disp, REQ, 0, 0, tiled=True)
    mine = from_heads(attended)
    tokens, mine, packs, block = lax.optimization_barrier((tokens, mine, packs, block))
    held = experts * 8
    res = [(p, 0, held) for p in packs]
    early, out_weight = early_rows(tokens, out_weight, res)
    others = from_heads(tokens)[1:]
    inner, hidden = expert_rows(others, early, out_weight, w_gate[0], w_up[0], norm_gain, mine, residual)
    blocks = [block if k == 2 else (p, held, p.shape[0] - held) for k, p in enumerate(packs)]
    w_cols = fetch(inner, *blocks)
    mix = mix_table(routes, route_weights, experts, inner)
    expert_out = down(from_heads(inner), w_cols, mix[0])
    returned = lax.all_to_all(expert_out, REQ, 0, 0, tiled=True)
    stream = blend(returned, mix, hidden)
    next_qkv = next_proj(from_heads(stream), next_gain, next_weight.transpose(1, 0, 2)).transpose(1, 0, 2)
    return stream, next_qkv


def solution(mesh):
    split = Mesh(mesh.devices.reshape(8, 4, 2, 4), ("z", "y", "c", "head"))
    placed = (
        P(REQ, None),
        P(REQ, "head"),
        P(REQ, None, "head"),
        P(REQ, None, None, "head"),
        P(),
        P(REQ),
        P(REQ),
        P(REQ),
        P("head", None),
        P(),
        P(REQ, None),
        P(REQ, None),
        P(REQ, None, "head"),
        P(REQ, None, "head"),
        P(REQ, "head", None),
        P(),
        P(None, None, "head"),
    )
    return jax.shard_map(
        local,
        mesh=split,
        in_specs=placed,
        out_specs=(P(REQ, "head"), P(REQ, None, "head")),
        check_vma=False,
    )
```

```python
import functools
import math

import jax
import jax.numpy as jnp
from jax import lax
from jax.experimental import pallas as pl
from jax.experimental.pallas import tpu as pltpu
from jax.sharding import Mesh, PartitionSpec as P

HD = 128
EPS = 1e-06
FLOOR = -(2.0**99)
SCALE = 1.0 / math.sqrt(HD)
F32 = jnp.float32
BF16 = jnp.bfloat16
REQ = ("z", "y", "c")
VLIM = pltpu.CompilerParams(vmem_limit_bytes=24 * 1024 * 1024)
VM = pl.BlockSpec(memory_space=pltpu.VMEM)


class Pending:
    def __init__(self, buf, copy):
        self.buf, self.copy, self.done = buf, copy, False

    def get(self):
        if not self.done:
            self.copy.wait()
            self.done = True
        return self.buf


def pin(xs):
    return [pltpu.with_memory_space_constraint(x, pltpu.HBM) for x in xs]


PIECES = 4


class Leaving:
    def __init__(self, buf, out, sems, base):
        rows = buf.shape[0] // PIECES
        parts = [pl.ds(j * rows, rows) for j in range(PIECES)]
        self.buf, self.sent = buf, 0
        self.copies = [pltpu.make_async_copy(buf.at[p], out.at[p], sems.at[base + j]) for j, p in enumerate(parts)]

    def send(self):
        self.copies[self.sent].start()
        self.sent += 1

    def finish(self):
        while self.sent < PIECES:
            self.send()
        for copy in self.copies:
            copy.wait()


class Moved:
    def __init__(self, buf, copies):
        self.buf, self.copies, self.done = buf, copies, False

    def get(self):
        if not self.done:
            for copy in self.copies:
                copy.wait()
            self.done = True
        return self.buf


def part_of(x):
    return x if isinstance(x, tuple) else (x, 0, x.shape[0])


def run(body, name, outs, near, far, scratch=(), after=(), moves=(), leaving=(), after_hbm=()):
    after = [*after, *pin(after_hbm)]
    far, moves = [part_of(x) for x in far], [part_of(x) for x in moves]
    na, nh, nn, nf, nm = len(after), len(after_hbm), len(near), len(far), len(moves)
    no, nl = len(outs), len(leaving)

    def kernel(*refs):
        ins, refs = refs[: nn + nf + na + nm], refs[nn + nf + na + nm :]
        outputs, out_hbm, moved = refs[:no], refs[no : no + nl], refs[no + nl : no + nl + nm]
        rest = refs[no + nl + nm :]
        bufs, out_bufs, rest = rest[:nf], rest[nf : nf + nl], rest[nf + nl :]
        sems, move_sems, out_sems, own = rest[0], rest[1], rest[2], rest[3:]
        pending = []
        for i, (x, first, rows) in enumerate(far):
            src = ins[nn + i] if rows == x.shape[0] else ins[nn + i].at[pl.ds(first, rows)]
            copy = pltpu.make_async_copy(src, bufs[i], sems.at[i])
            copy.start()
            pending.append(Pending(bufs[i], copy))
        moving = []
        for i, (x, first, rows) in enumerate(moves):
            rows, copies = rows // PIECES, []
            for j in range(PIECES):
                src = ins[nn + nf + na + i].at[pl.ds(first + j * rows, rows)]
                dst = moved[i].at[pl.ds(j * rows, rows)]
                copies.append(pltpu.make_async_copy(src, dst, move_sems.at[PIECES * i + j]))
                copies[-1].start()
            moving.append(Moved(moved[i], copies))
        going = [Leaving(out_bufs[i], out_hbm[i], out_sems, PIECES * i) for i in range(nl)]
        body(ins[:nn], pending, (*outputs, *going, *moving), own)
        for p in pending:
            p.get()
        for g in going:
            g.finish()
        for m in moving:
            m.get()

    hbm, any_space = pl.BlockSpec(memory_space=pltpu.HBM), pl.BlockSpec(memory_space=pl.ANY)
    far_shapes = [((r,) + x.shape[1:], x.dtype) for x, _, r in far]
    return pl.pallas_call(
        kernel,
        name=name,
        out_shape=list(outs)
        + [pltpu.HBM(x.shape, x.dtype) for x in leaving]
        + [sds((r,) + x.shape[1:], x.dtype) for x, _, r in moves],
        in_specs=[VM] * nn + [hbm] * nf + [any_space] * (na - nh) + [hbm] * (nh + nm),
        out_specs=[VM] * no + [hbm] * nl + [VM] * nm,
        scratch_shapes=[pltpu.VMEM(*f) for f in far_shapes]
        + [pltpu.VMEM(x.shape, x.dtype) for x in leaving]
        + [pltpu.SemaphoreType.DMA((max(n, 1),)) for n in (nf, nm * PIECES, nl * PIECES)]
        + list(scratch),
        compiler_params=VLIM,
    )(*near, *pin([x for x, _, _ in far]), *after, *pin([x for x, _, _ in moves]))


def sds(shape, dtype):
    return jax.ShapeDtypeStruct(shape, dtype)


def iota(shape, dim):
    return lax.broadcasted_iota(jnp.int32, shape, dim)


def core_id():
    return lax.axis_index("c")


def head_id():
    return lax.axis_index("head")


def dot(a, b):
    return jnp.dot(a, b, preferred_element_type=F32)


def hi_lo(x):
    hi = x.astype(BF16)
    return hi, (x - hi.astype(F32)).astype(BF16)


def hits(routes, expert):
    hit = jnp.zeros(expert.shape, F32)
    for k in range(routes.shape[1]):
        hit = hit + jnp.where(routes[:, k : k + 1] == expert, 1.0, 0.0)
    return hit


def cell_map(routes, expert, lane):
    hit = hits(routes, expert)
    hit = jnp.where(rank_of(hit) == (lane % 4).astype(F32), hit, 0.0)
    left = lane % 8 < 4
    return jnp.concatenate([jnp.where(left, hit, 0.0), jnp.where(left, 0.0, hit)], axis=0).astype(BF16)


def outset_body(near, far, outs, own):
    chips, _, width = outs[0].shape
    rows = far[0].buf.shape[0]
    routes = flip(far[2].get()[...], 1)
    lane = iota((rows, chips * 16), 1)
    expert = (lane // 16) * 2 + (core_id() + (lane // 8) % 2) % 2
    pick = cell_map(routes, expert.astype(F32), lane)
    first = pl.multiple_of(head_id() * 2 * width, 2 * width)
    res = far[1].get()
    both = jnp.concatenate([res[:, pl.ds(first, width)], res[:, pl.ds(first + width, width)]], axis=0)
    out = lax.dot_general(pick, both, (((0,), (0,)), ((), ())), preferred_element_type=F32)
    outs[0][:, 16:32, :] = out.astype(BF16).reshape(chips, 16, width)
    q = far[0].get()[...]
    outs[0][:, 0:16, :] = jnp.broadcast_to(q[None], (chips,) + q.shape)


def outset(queries, residual, routes, chips):
    out = sds((chips, 32, queries.shape[1]), BF16)
    return run(outset_body, "outset", [out], [], [queries, residual, routes.T])[0]


def tables_body(near, far, outs, own, page):
    pick_ref, count_ref, same_ref, mine_ref, spread_ref, spread8_ref = outs[:6]
    req = far[0].get()[...]
    slots, total = pick_ref.shape
    half = total // 2
    place = jnp.where((req // 16) % 2 == core_id(), 0, half) + (req // 32) * 16 + req % 16
    spread_ref[...] = jnp.where(iota((total, slots), 0) == place, 1.0, 0.0).astype(BF16)
    owners = jnp.where(iota((half, slots), 0) // 8 == place // 16, 1.0, 0.0)
    spread8_ref[...] = owners.astype(BF16)
    eye = iota((slots, slots), 0) == iota((slots, slots), 1)

    def to_col(row):
        return jnp.sum(jnp.where(eye, row.astype(F32), 0.0), axis=1, keepdims=True)

    req_col = to_col(req)
    same = req_col == req.astype(F32)
    same_ref[...] = jnp.where(same, 1.0, 0.0)
    slot_row = iota((slots, slots), 1).astype(F32)
    first = jnp.min(jnp.where(same, slot_row, 9999.0), axis=1, keepdims=True)
    leader = first == iota((slots, 1), 0).astype(F32)
    mine = (iota((slots, HD), 1) % 16).astype(F32) == to_col(req % 16)
    mine_ref[...] = jnp.where(mine & leader, 1.0, 0.0)
    lane_total = iota((slots, total), 1).astype(F32)
    pick_ref[...] = jnp.where(to_col(place) == lane_total, 1.0, 0.0).astype(BF16)
    lengths = far[3].get()[...].astype(F32)
    len_col = jnp.sum(jnp.where(req_col == lane_total, lengths, 0.0), axis=1, keepdims=True)
    count = jnp.clip(len_col - to_col(far[1].get()[...]) * page, 0.0, float(page))
    count = jnp.where(to_col(far[2].get()[...]) == 1.0, count, 0.0)
    count_ref[...] = jnp.broadcast_to(count, (slots, HD))


def slot_tables(slot_request, slot_page, slot_used, lengths, kv_cache, after):
    slots = kv_cache.shape[0]
    total = lengths.shape[0]
    return run(
        functools.partial(tables_body, page=kv_cache.shape[2]),
        "slot_tables",
        [
            sds((slots, total), BF16),
            sds((slots, HD), F32),
            sds((slots, slots), F32),
            sds((slots, HD), F32),
            sds((total, slots), BF16),
            sds((total // 2, slots), BF16),
        ],
        [],
        [slot_request.reshape(1, slots), slot_page.reshape(1, slots), slot_used.reshape(1, slots), lengths.reshape(1, total)],
        after=after,
        moves=[kv_cache],
    )


def attn_body(near, far, outs, own):
    pick_ref, count_ref, same_ref, mine_ref, spread_ref, spread8_ref, kv_ref, qa_ref, qb_ref = near
    keep_ref, send_ref = outs
    n_scr, m_scr, l_scr = own
    slots = kv_ref.shape[0]
    page = kv_ref.shape[2]
    half = qa_ref.shape[0] * 16
    qa, qb = (r[:, 0:16, :].reshape(half, 2 * HD) for r in (qa_ref, qb_ref))
    chosen = dot(pick_ref[:, :half], qa) + dot(pick_ref[:, half:], qb)
    low_lanes = iota((8, 2 * HD), 1) < HD
    rel = iota((16, 8 * page), 1) - (iota((16, 8 * page), 0) % 8) * page
    rel = rel.astype(F32)
    for b in range(slots // 8):
        q8 = chosen[b * 8 : b * 8 + 8]
        q16 = jnp.concatenate([jnp.where(low_lanes, q8, 0.0), jnp.where(low_lanes, 0.0, q8)], axis=0).astype(BF16)
        keys = kv_ref[b * 8 : b * 8 + 8, 0].reshape(8 * page, 2 * HD)
        vals = kv_ref[b * 8 : b * 8 + 8, 1].reshape(8 * page, 2 * HD)
        s = lax.dot_general(q16, keys, (((1,), (1,)), ((), ())), preferred_element_type=F32) * SCALE
        c8 = count_ref[b * 8 : b * 8 + 8, :1]
        ok = (rel >= 0.0) & (rel < jnp.concatenate([c8, c8], axis=0))
        s = jnp.where(ok, s, FLOOR)
        m = jnp.max(s, axis=1, keepdims=True)
        w = jnp.where(ok, jnp.exp(s - m), 0.0).astype(BF16)
        l = jnp.sum(w.astype(F32), axis=1, keepdims=True)
        n = dot(w, vals)
        for h in range(2):
            n_scr[h, b * 8 : b * 8 + 8, :] = n[8 * h : 8 * h + 8, HD * h : HD * h + HD]
            m_scr[h, b * 8 : b * 8 + 8, :] = jnp.broadcast_to(m[8 * h : 8 * h + 8], (8, slots))
            l_scr[h, b * 8 : b * 8 + 8, :] = jnp.broadcast_to(l[8 * h : 8 * h + 8], (8, slots))

    eye = iota((slots, slots), 0) == iota((slots, slots), 1)
    same = same_ref[...] > 0.0

    def to_row(wide):
        return jnp.sum(jnp.where(eye, wide, 0.0), axis=0, keepdims=True)

    group = iota((slots, HD), 1) // 16
    board = jnp.zeros((slots, HD), F32)
    for h in range(2):
        m_wide = m_scr[h]
        m_ref = jnp.max(jnp.where(same, to_row(m_wide), FLOOR), axis=1, keepdims=True)
        m_ref = m_ref.astype(BF16).astype(F32)
        lift = jnp.exp(m_wide - m_ref)
        n_hi, n_lo = hi_lo(n_scr[h] * lift)
        l_sum = jnp.sum(jnp.where(same, to_row(l_scr[h] * lift), 0.0), axis=1, keepdims=True)
        out = (dot(spread_ref[...], n_hi) + dot(spread_ref[...], n_lo)).astype(BF16)
        keep_ref[:, 16 * h : 16 * h + 16, :] = out[:half].reshape(half // 16, 16, HD)
        send_ref[:, 16 * h : 16 * h + 16, :] = out[half:].reshape(half // 16, 16, HD)
        l_hi = l_sum.astype(BF16).astype(F32)
        for i, stat in enumerate((m_ref, l_hi, l_sum - l_hi)):
            board = jnp.where(group == 2 * i + h, stat, board)
    board = jnp.where(mine_ref[...] > 0.0, board, 0.0).astype(BF16)
    out = dot(spread8_ref[...], board).astype(BF16)
    keep_ref[:, 32:40, :] = out[: half // 2].reshape(half // 16, 8, HD)
    send_ref[:, 32:40, :] = out[half // 2 :].reshape(half // 16, 8, HD)


def attend_pages(tables, qa, qb):
    slots, total = tables[0].shape
    scratch = [pltpu.VMEM((2, slots, n), F32) for n in (HD, slots, slots)]
    outs = [sds((total // 32, 40, HD), BF16)] * 2
    return run(attn_body, "attend_pages", outs, [*tables, qa, qb], [], scratch)


def merge_body(near, far, outs, own):
    chips = near[0].shape[0] // PIECES
    for piece in range(PIECES):
        part = slice(piece * chips, piece * chips + chips)
        a_ref, b_ref, out_ref = near[0].at[part], near[1].at[part], outs[0].buf.at[part]
        a, b = a_ref[:, 32:40, :].astype(F32), b_ref[:, 32:40, :].astype(F32)
        lane, row = iota(a.shape, 2), iota(a.shape, 1)
        board = jnp.zeros(a.shape, F32)
        for h in range(2):
            (ma, la), (mb, lb) = read_stats(a, h), read_stats(b, h)
            m = jnp.maximum(ma, mb)
            fa, fb = jnp.exp(ma - m), jnp.exp(mb - m)
            rows = slice(16 * h, 16 * h + 16)
            out_ref[:, rows, :] = (a_ref[:, rows, :].astype(F32) * fa + b_ref[:, rows, :].astype(F32) * fb).astype(BF16)
            l = la * fa + lb * fb
            l_hi = l.astype(BF16).astype(F32)
            for i, stat in enumerate((m, l_hi, l - l_hi)):
                for u in range(2):
                    at = row + 8 * u + 32 * i + 16 * h
                    board = jnp.where(lane == at, stat[:, 8 * u : 8 * u + 8], board)
        out_ref[:, 32:40, :] = board.astype(BF16)
        outs[0].send()


def merge(a, b):
    return run(merge_body, "merge", [], [a, b], [], leaving=[sds(a.shape, BF16)])[0]


def fetch(after, *arrays):
    return run(lambda *_: None, "fetch", [], [], [], after=[after], moves=arrays)


def pack_kernel(w_ref, qa_ref, qb_ref, after_ref, *refs):
    outs, res_buf, in_a, in_b, bufs, sems = refs[:4], refs[4], refs[5], refs[6], refs[7:11], refs[11]
    rows, width = bufs[0].shape[0] // 2, bufs[0].shape[1]
    held = res_buf.shape[0]
    reads = [
        pltpu.make_async_copy(qa_ref.at[:, pl.ds(16, 8), :], in_a, sems.at[16]),
        pltpu.make_async_copy(qb_ref.at[:, pl.ds(24, 8), :], in_b, sems.at[17]),
    ]
    for read in reads:
        read.start()
    cuts, writes = [], []
    for k in range(4):
        first = pl.multiple_of(((head_id() + k) % 4) * 2 * width, 2 * width)
        for f in range(2):
            src = w_ref.at[:, pl.ds(first + f * width, width)]
            cuts.append(pltpu.make_async_copy(src, bufs[k].at[pl.ds(f * rows, rows)], sems.at[2 * k + f]))
        writes.append(pltpu.make_async_copy(bufs[k], outs[k].at[pl.ds(held, 2 * rows)], sems.at[8 + k]))
    for cut in cuts:
        cut.start()
    for read in reads:
        read.wait()
    mine, other = in_a[...].astype(F32), in_b[...].astype(F32)
    first = core_id() == 0
    both = [jnp.where(first, mine, other), jnp.where(first, other, mine)]
    res_buf[...] = jnp.stack(both, axis=1).reshape(res_buf.shape).astype(BF16)
    for k in range(4):
        writes.append(pltpu.make_async_copy(res_buf, outs[k].at[pl.ds(0, held)], sems.at[12 + k]))
        writes[-1].start()
    for k in range(4):
        cuts[2 * k].wait()
        cuts[2 * k + 1].wait()
        writes[k].start()
    for write in writes:
        write.wait()


def pack(w_down, qa, qb, after):
    hbm = pl.BlockSpec(memory_space=pltpu.HBM)
    rows, width = w_down.shape[0], w_down.shape[1] // 8
    chips = qa.shape[0]
    held = chips * 16
    return pl.pallas_call(
        pack_kernel,
        name="pack",
        out_shape=[pltpu.HBM((held + 2 * rows, width), BF16)] * 4,
        in_specs=[hbm] * 4,
        out_specs=[hbm] * 4,
        scratch_shapes=[pltpu.VMEM((held, width), BF16)]
        + [pltpu.VMEM((chips, 8, width), BF16)] * 2
        + [pltpu.VMEM((2 * rows, width), BF16)] * 4
        + [pltpu.SemaphoreType.DMA((18,))],
        compiler_params=VLIM,
    )(*pin([w_down, qa, qb, after]))


def cells_body(near, far, outs, own):
    buf = outs[0].buf
    lane = iota((buf.shape[0] // 2, buf.shape[1]), 1)
    buf[...] = cell_map(flip(far[0].get()[...], 1), (lane // 8).astype(F32), lane)


def cells_table(routes, experts, after):
    out = sds((2 * routes.shape[0], experts * 8), BF16)
    return run(cells_body, "cells_table", [], [], [routes.T], after_hbm=[after], leaving=[out])[0]


def mix_body(near, far, outs, own):
    routes, share = flip(far[0].get()[...], 1), flip(far[1].get()[...], 3)
    rows, cells = outs[0].shape
    lane = iota((rows, cells), 1)
    expert = (lane // 4).astype(F32)
    mix = jnp.zeros((rows, cells), F32)
    for k in range(routes.shape[1]):
        mix = mix + jnp.where(routes[:, k : k + 1] == expert, share[:, k : k + 1], 0.0)
    mix = jnp.where(rank_of(hits(routes, expert)) == (lane % 4).astype(F32), mix, 0.0)
    outs[0][...], outs[1][...] = hi_lo(mix)


def mix_table(routes, route_weights, experts, after):
    out = sds((routes.shape[0], experts * 4), BF16)
    return run(mix_body, "mix_table", [out, out], [], [routes.T, route_weights.T], after=[after])


def read_stats(board, h):
    lane, row = iota(board.shape, 2), iota(board.shape, 1)
    ms, ls = [], []
    for u in range(2):
        at = row + 8 * u + 16 * h
        ms.append(jnp.sum(jnp.where(lane == at, board, 0.0), axis=2, keepdims=True))
        ls.append(jnp.sum(jnp.where((lane == at + 32) | (lane == at + 64), board, 0.0), axis=2, keepdims=True))
    m, l = jnp.concatenate(ms, axis=1), jnp.concatenate(ls, axis=1)
    return jnp.where(l > 0.0, m, FLOOR), l


def owner_body(near, far, outs, own_scratch):
    part_ref = near[0]
    att_ref, disp = outs
    board = part_ref[:, 32:40, :].astype(F32)
    stats = [read_stats(board, h) for h in range(2)]
    tops = [jnp.max(m, axis=0) for m, _ in stats]
    q = far[0].get()[...].astype(F32)
    nkv = far[1].get()[...].astype(F32)
    nkv = jnp.concatenate([nkv[:, 0, :], nkv[:, 1, :]], axis=1)
    att = []
    for h, (m, l) in enumerate(stats):
        own = jnp.sum(q[:, HD * h : HD * h + HD] * nkv[:, HD * h : HD * h + HD], axis=1, keepdims=True) * SCALE
        top = jnp.maximum(tops[h], own)
        lift = jnp.exp(m - top[None])
        n = jnp.sum(part_ref[:, 16 * h : 16 * h + 16, :].astype(F32) * lift, axis=0)
        den = jnp.sum(l * lift, axis=0)
        new = jnp.exp(own - top)
        v = nkv[:, 2 * HD + HD * h : 2 * HD + HD * h + HD]
        att.append((n + new * v) / (den + new))
    both = jnp.concatenate(att, axis=0).astype(BF16)
    pick = far[2].get()
    cells = pick.shape[1] // PIECES
    for j in range(PIECES):
        part = pick[:, j * cells : j * cells + cells]
        out = lax.dot_general(part, both, (((0,), (0,)), ((), ())), preferred_element_type=F32)
        disp.buf[j * cells // 8 : (j + 1) * cells // 8] = out.astype(BF16).reshape(cells // 8, 8, HD)
        disp.send()
    att_ref[...] = jnp.concatenate(att, axis=1).astype(BF16)


def owner_part(parts, queries, new_kv, cells, experts):
    outs, leaving = [sds(queries.shape, BF16)], [sds((experts, 8, HD), BF16)]
    return run(owner_body, "owner_part", outs, [parts], [queries, new_kv, cells], leaving=leaving)


def flip(x, terms):
    n = x.shape[1]
    eye = jnp.where(iota((n, n), 0) == iota((n, n), 1), 1.0, 0.0).astype(BF16)
    x = x.astype(F32)
    out = jnp.zeros((n, x.shape[0]), F32)
    for _ in range(terms):
        part = x.astype(BF16)
        out = out + lax.dot_general(eye, part, (((1,), (1,)), ((), ())), preferred_element_type=F32)
        x = x - part.astype(F32)
    return out


def rank_of(hit):
    rows = hit.shape[0]
    before = jnp.where(iota((rows, rows), 0) > iota((rows, rows), 1), 1.0, 0.0).astype(BF16)
    return dot(before, hit.astype(BF16))


def unfold(x):
    n, _, w = x.shape
    x = x.reshape(n // 2, 2, 8, w)
    a, b = x[:, 0], x[:, 1]
    top = iota(a.shape, 1) < 4
    left = jnp.where(top, a, pltpu.roll(b, 4, 1))
    right = jnp.where(top, pltpu.roll(a, 4, 1), b)
    return left.reshape(n * 4, w), right.reshape(n * 4, w)


def fold(left, right):
    rows, w = left.shape
    left, right = left.reshape(rows // 8, 8, w), right.reshape(rows // 8, 8, w)
    top = iota(left.shape, 1) < 4
    a = jnp.where(top, left, pltpu.roll(right, 4, 1))
    b = jnp.where(top, pltpu.roll(left, 4, 1), right)
    return a, b


def head_blocks(size):
    return [pl.multiple_of(((head_id() + 4 - k) % 4) * size, size) for k in range(4)]


def early_body(near, far, outs, own):
    tok_ref = near[0]
    xs, wo = outs
    eff, w = 2 * HD, xs.shape[2]
    att = jnp.concatenate(unfold(tok_ref[...].astype(F32)), axis=1).astype(BF16)
    for k in range(4):
        res = far[k].get()[...].astype(F32)
        xs[2 * k], xs[2 * k + 1] = unfold(res.reshape(res.shape[0] // 8, 8, w))
    wo_ref = wo.get()
    rows = pl.ds(head_blocks(eff)[0], eff)
    for k, first in enumerate(head_blocks(2 * w)):
        for f in range(2):
            xs[2 * k + f] = xs[2 * k + f] + dot(att, wo_ref[rows, pl.ds(first + f * w, w)])


def early_rows(tokens, out_weight, res):
    n = tokens.shape[0]
    w = res[0][0].shape[1]
    return run(early_body, "early_rows", [sds((8, n * 4, w), F32)], [tokens], res, moves=[out_weight])


def expert_body(near, far, outs, own):
    inner_ref, hid = outs
    hs = own[0]
    att, (xs, wo_ref) = near[:3], near[3:]
    gain, mine, own_res, w_gate, w_up = far[0], far[1:5], *far[5:]
    n = inner_ref.shape[0]
    eff = 2 * HD
    w = xs.shape[2]
    att = [jnp.concatenate(unfold(a[...].astype(F32)), axis=1).astype(BF16) for a in att]
    block = head_blocks(eff)
    firsts = [first + f * w for first in head_blocks(2 * w) for f in range(2)]
    cols = pl.ds(head_blocks(2 * w)[0], 2 * w)
    acc = own_res.get()[:, cols].astype(F32)
    acc = acc + sum(dot(mine[i].get()[...], wo_ref[pl.ds(block[i], eff), cols]) for i in range(4))
    hid.buf[...] = acc.astype(BF16)
    for _ in range(PIECES):
        hid.send()
    total = jnp.zeros((n, 1), F32)
    for j, first in enumerate(firsts):
        acc = xs[j]
        for i in range(3):
            acc = acc + dot(att[i], wo_ref[pl.ds(block[i + 1], eff), pl.ds(first, w)])
        part = acc.astype(BF16)
        hs[j] = part
        part = part.astype(F32)
        total = total + jnp.sum(part * part, axis=1, keepdims=True)
    scale = lax.rsqrt(total / (8 * w) + EPS)
    gain_ref = gain.get()
    wg_ref, wu_ref = w_gate.get(), w_up.get()
    gate = jnp.zeros((n, wg_ref.shape[1]), F32)
    up = jnp.zeros((n, wg_ref.shape[1]), F32)
    for j, first in enumerate(firsts):
        normed = (hs[j].astype(F32) * scale * gain_ref[:, pl.ds(first, w)]).astype(BF16)
        gate = gate + dot(normed, wg_ref[pl.ds(first, w), :])
        up = up + dot(normed, wu_ref[pl.ds(first, w), :])
    inner_ref[...] = (gate / (1.0 + jnp.exp(-gate)) * up).astype(BF16)


def expert_rows(tokens, early, out_weight, w_gate, w_up, gain, mine, residual):
    _, n, w = early.shape
    outs, leaving = [sds((n, w_gate.shape[1]), BF16)], [sds((residual.shape[0], 2 * w), BF16)]
    near = [*tokens, early, out_weight]
    scratch = [pltpu.VMEM((8, n, w), BF16)]
    far = [gain.reshape(1, -1), *mine, residual, w_gate, w_up]
    return run(expert_body, "expert_rows", outs, near, far, scratch, leaving=leaving)


def down_body(near, far, outs, own):
    out_ref = outs[0]
    k_rows = near[0].shape[1]
    left = sum(dot(near[k][...], near[4 + k][0:k_rows]) for k in range(4))
    right = sum(dot(near[k][...], near[4 + k][k_rows : 2 * k_rows]) for k in range(4))
    a, b = fold(left, right)
    out_ref[:, 0] = a.astype(BF16)
    out_ref[:, 1] = b.astype(BF16)


def down(inners, w_cols, after):
    rows = inners[0].shape[0]
    width = w_cols[0].shape[1]
    out = run(down_body, "down", [sds((rows // 8, 2, 8, width), BF16)], [*inners, *w_cols], [], after=[after])[0]
    return out.reshape(rows // 4, 8, width)


def blend_body(near, far, outs, own):
    y_ref, hi_ref, low_ref = near
    w = y_ref.shape[2]
    moe = []
    for part in unfold(y_ref[...].astype(F32)):
        part = part.astype(BF16)
        moe.append(dot(hi_ref[...], part) + dot(low_ref[...], part))
    hid_ref = far[0].get()
    for f in range(2):
        cols = slice(f * w, f * w + w)
        outs[0][:, cols] = (hid_ref[:, cols].astype(F32) + moe[f]).astype(BF16)


def blend(returned, mix, hidden):
    return run(blend_body, "blend", [sds(hidden.shape, BF16)], [returned, *mix], [hidden])[0]


def proj_share(x, k, gain_ref, w_ref):
    w = x.shape[1]
    cols = pl.ds(head_blocks(w)[k], w)
    part = (x * gain_ref[:, cols]).astype(BF16)
    return [dot(part, w_ref[i, cols, :]) for i in range(w_ref.shape[0])], jnp.sum(x * x, axis=1, keepdims=True)


def own_proj_body(near, far, outs, own):
    shares, total = proj_share(far[1].get()[...].astype(F32), 0, far[0].get(), near[0])
    for i, share in enumerate(shares):
        outs[0][i] = share
    outs[1][...] = jnp.broadcast_to(total, outs[1].shape)
    outs[2][...] = far[0].get()[...]


def proj_body(near, far, outs, own):
    others, (w_ref, first_ref, total_ref, gain_ref) = near[:3], near[3:]
    total = total_ref[:, 0:1]
    accs = [first_ref[i] for i in range(w_ref.shape[0])]
    for k, s in enumerate(others):
        shares, add = proj_share(s[...].astype(F32), k + 1, gain_ref, w_ref)
        accs, total = [a + b for a, b in zip(accs, shares)], total + add
    scale = lax.rsqrt(total / w_ref.shape[1] + EPS)
    for i, acc in enumerate(accs):
        outs[0][i] = (acc * scale).astype(BF16)


def next_proj(parts, gain, weight):
    kinds, _, width = weight.shape
    rows = parts[0].shape[0]
    shape = (kinds, rows, width)
    gain = gain.reshape(1, -1)
    outs = [sds(shape, F32), sds((rows, HD), F32), sds(gain.shape, F32)]
    first = run(own_proj_body, "own_proj", outs, [weight], [gain, parts[0]])
    return run(proj_body, "next_proj", [sds(shape, BF16)], [*parts[1:], weight, *first], [])[0]


def from_heads(x):
    n = lax.axis_size("head")
    return [x] + [lax.ppermute(x, "head", [(i, (i + k) % n) for i in range(n)]) for k in range(1, n)]


def to_heads(xs):
    n = lax.axis_size("head")
    return [xs[0]] + [lax.ppermute(xs[k], "head", [(i, (i + k) % n) for i in range(n)]) for k in range(1, n)]


def swap_core(x):
    return lax.ppermute(x, "c", [(0, 1), (1, 0)])


def local(
    residual, queries, new_kv, kv_cache, lengths, slot_request, slot_page, slot_used, out_weight,
    norm_gain, routes, route_weights, w_gate, w_up, w_down, next_gain, next_weight,
):
    rows = queries.shape[0]
    experts = lax.axis_size(REQ)
    chips = experts // 2
    out_weight = lax.all_gather(out_weight, "head", axis=0, tiled=True)
    qa = lax.all_to_all(outset(queries, residual, routes, chips), ("z", "y"), 0, 0, tiled=True)
    tables = slot_tables(slot_request, slot_page, slot_used, lengths, kv_cache, [qa])
    qb = swap_core(qa)
    keep, send = attend_pages(tables, qa, qb)
    merged = merge(keep, swap_core(send))
    packs = to_heads(pack(w_down[0], qa, qb, merged))
    cells = cells_table(routes, experts, merged)
    arrived = lax.all_to_all(merged, ("z", "y"), 0, 0, tiled=True)
    arrived, cells = lax.optimization_barrier((arrived, cells))
    attended, disp = owner_part(arrived, queries, new_kv, cells, experts)
    tokens = lax.all_to_all(disp, REQ, 0, 0, tiled=True)
    mine = from_heads(attended)
    tokens, mine, packs = lax.optimization_barrier((tokens, mine, packs))
    held = experts * 8
    res = [(p, 0, held) for p in packs]
    early, out_weight = early_rows(tokens, out_weight, res)
    others = from_heads(tokens)[1:]
    inner, hidden = expert_rows(others, early, out_weight, w_gate[0], w_up[0], norm_gain, mine, residual)
    w_cols = fetch(inner, *[(p, held, p.shape[0] - held) for p in packs])
    mix = mix_table(routes, route_weights, experts, inner)
    expert_out = down(from_heads(inner), w_cols, mix[0])
    returned = lax.all_to_all(expert_out, REQ, 0, 0, tiled=True)
    stream = blend(returned, mix, hidden)
    next_qkv = next_proj(from_heads(stream), next_gain, next_weight.transpose(1, 0, 2)).transpose(1, 0, 2)
    return stream, next_qkv


def solution(mesh):
    split = Mesh(mesh.devices.reshape(8, 4, 2, 4), ("z", "y", "c", "head"))
    placed = (
        P(REQ, None),
        P(REQ, "head"),
        P(REQ, None, "head"),
        P(REQ, None, None, "head"),
        P(),
        P(REQ),
        P(REQ),
        P(REQ),
        P("head", None),
        P(),
        P(REQ, None),
        P(REQ, None),
        P(REQ, None, "head"),
        P(REQ, None, "head"),
        P(REQ, "head", None),
        P(),
        P(None, None, "head"),
    )
    return jax.shard_map(
        local,
        mesh=split,
        in_specs=placed,
        out_specs=(P(REQ, "head"), P(REQ, None, "head")),
        check_vma=False,
    )
```
